32 devices in a mesh: seq: 4 (over x, core), fsdp: 8 (over z, y).
Axes of the slice: x: 2, y: 2, z: 4, core: 2. Of those that a mesh axis runs over, the one named last changes fastest.
Arguments:
- tokens: bfloat16 [16, 1024, 768], P('fsdp', 'seq'), may hold values from -6 to 6
- pre_gain: bfloat16 [768], P('fsdp'), may hold values from 0.5 to 1.5
- pre_bias: bfloat16 [768], P('fsdp'), may hold values from -3 to 3
- query_key_value_weight: bfloat16 [768, 2304], P('fsdp'), may hold values from -0.21875 to 0.21875
- query_key_value_bias: bfloat16 [2304], P('fsdp'), may hold values from -3 to 3
- query_gain: bfloat16 [768], P('fsdp'), may hold values from 0.25 to 1.75
- key_gain: bfloat16 [768], P('fsdp'), may hold values from 0.25 to 1.75
- output_weight: bfloat16 [768, 768], P('fsdp'), may hold values from -0.875 to 0.875
- output_bias: bfloat16 [768], P('fsdp'), may hold values from -3 to 3
- mlp_gain: bfloat16 [768], P('fsdp'), may hold values from 0.5 to 1.5
- mlp_bias: bfloat16 [768], P('fsdp'), may hold values from -3 to 3
- up_matrix_weight: bfloat16 [768, 3072], P('fsdp'), may hold values from -0.21875 to 0.21875
- up_offset_bias: bfloat16 [3072], P('fsdp'), may hold values from -3 to 3
- down_matrix_weight: bfloat16 [3072, 768], P('fsdp'), may hold values from -0.109375 to 0.109375
- down_offset_bias: bfloat16 [768], P('fsdp'), may hold values from -3 to 3
- segments: int32 [16, 1024], P('fsdp'), may hold values from 0 to 3, never falling along the last dimension, each value on 1 to 512 neighbouring positions
- positions: int32 [2, 16, 1024], P(None, 'fsdp'), may hold values from 0 to 63
- cotangent: bfloat16 [16, 1024, 768], P('fsdp', 'seq'), may hold values from -6 to 6
Outputs:
- output: bfloat16 [16, 1024, 768], P('fsdp', 'seq')
- grad_tokens: bfloat16 [16, 1024, 768], P('fsdp', 'seq')
- grad_pre_gain: float32 [768], P('fsdp')
- grad_pre_bias: float32 [768], P('fsdp')
- grad_qkv_weight: float32 [768, 2304], P('fsdp')
- grad_query_key_bias: float32 [1536], P('fsdp')
- grad_value_bias: float32 [768], P('fsdp')
- grad_query_gain: float32 [768], P('fsdp')
- grad_key_gain: float32 [768], P('fsdp')
- grad_out_weight: float32 [768, 768], P('fsdp')
- grad_out_bias: float32 [768], P('fsdp')
- grad_mlp_gain: float32 [768], P('fsdp')
- grad_mlp_bias: float32 [768], P('fsdp')
- gradient_up_weight: float32 [768, 3072], P('fsdp')
- grad_up_bias: float32 [3072], P('fsdp')
- gradient_down_weight: float32 [3072, 768], P('fsdp')
- grad_down_bias: float32 [768], P('fsdp')
The draws below stay inside these ranges and needn't reach their ends.
Inputs may be any that keep to these rules, and one draw needn't show every extreme that they name: `segments`: within each packed sequence image numbers never fall; one image of a sequence holds at most 512 tokens, and one image of each sequence holds exactly that many.
All inputs are finite; a program needn't handle non-finite values.
Results may differ from the reference program's by a relative error of at most 0.015.
Values may be sent and summed in bfloat16 or wider, within the bound.
A program may use at most 192 MiB of HBM per device.

```python
import math
import jax
import jax.numpy as jnp
import numpy as np
from jax import lax

D = 768
H = 12
HD = 64
FF = 3072
LEN = 1024
SEQS = 16


def with_ends(drawn, key, low, largest):
    longest = drawn.shape.index(max(drawn.shape))
    spots = []
    for shift in (0, 1):
        where = [jax.random.randint(jax.random.fold_in(key, axis), (), 0, length) for axis, length in enumerate(drawn.shape)]
        where[longest] = (where[longest] + shift) % drawn.shape[longest]
        spots.append(tuple(where))
    return drawn.at[spots[0]].set(low).at[spots[1]].set(largest)


def block_scale(key, dims, split, least, top_value):
    gain = 1.0
    for axis_at, parts in split:
        draws = jax.random.uniform(jax.random.fold_in(jax.random.fold_in(key, 6), axis_at), (parts,), jnp.float32, least / len(split), top_value / len(split))
        gain = gain * jnp.repeat(jnp.exp(draws), dims[axis_at] // parts).reshape((-1,) + (1,) * (len(dims) - 1 - axis_at))
    return gain


def profile(amount, total, most, lean):
    weights = [(1 << 20) // math.isqrt(standing ** lean) + 1 for standing in range(2, amount + 1)]
    rest, counts = total - most - (amount - 1), [1] * (amount - 1)
    while rest > 0:
        candidates = [i for i in range(amount - 1) if counts[i] < most]
        mass, left = sum([weights[i] for i in candidates]), rest
        for i in candidates:
            addition = min(most - counts[i], max(1, left * weights[i] // mass), rest)
            counts[i] = counts[i] + addition
            rest = rest - addition
    return np.array([most] + counts)


def uneven(own_key, count, total, most, lean):
    if count == 2:
        one = jax.random.randint(own_key, (), max(1, total - most), min(most, total - 1) + 1)
        return jnp.stack([one, total - one])
    tallies = jnp.asarray(profile(count, total, most, lean), jnp.int32)
    pairs = (count - 1) // 2
    giver, sink = tallies[1:1 + 2 * pairs:2], tallies[2:2 + 2 * pairs:2]
    slack = jnp.minimum(giver - 1, most - sink)
    passed = jax.random.randint(jax.random.fold_in(own_key, 1), (pairs,), 0, 1 << 20) % (slack + 1)
    tallies = tallies.at[1:1 + 2 * pairs:2].set(giver - passed).at[2:2 + 2 * pairs:2].set(sink + passed)
    return tallies[jax.random.permutation(jax.random.fold_in(own_key, 2), count)]


def scatter_about(key, extent, scale, reach, split=(), kind=jnp.bfloat16):
    factor_of = block_scale(key, extent, split, -0.22, 0.18) if split else 1.0
    values = jax.random.normal(key, extent, jnp.float32) * scale * factor_of
    return jnp.minimum(jnp.maximum(values, -reach), reach).astype(kind)


def setup_inputs(seed: int = 0) -> dict:
    key_list = jax.random.split(jax.random.key(seed), 19)
    tokens = scatter_about(key_list[0], (SEQS, LEN, D), 1.0, 6.0, ((0, 8), (1, 4)))
    pre_gain = jnp.clip(1.0 + 0.1 * jax.random.normal(key_list[1], (D,), jnp.float32), 0.5, 1.5).astype(jnp.bfloat16)
    pre_bias = scatter_about(key_list[2], (D,), 0.5, 3.0, ((0, 8),))
    query_key_value_weight = scatter_about(key_list[3], (D, 3 * D), D ** -0.5, 0.21875, ((0, 8),))
    query_key_value_bias = scatter_about(key_list[4], (3 * D,), 0.5, 3.0, ((0, 8),))
    query_gain = jnp.clip(1.0 + 0.15 * jax.random.normal(key_list[5], (D,), jnp.float32), 0.25, 1.75).astype(jnp.bfloat16)
    key_gain = jnp.clip(1.0 + 0.15 * jax.random.normal(key_list[6], (D,), jnp.float32), 0.25, 1.75).astype(jnp.bfloat16)
    output_weight = scatter_about(key_list[7], (D, D), (D // 16) ** -0.5, 0.875, ((0, 8),))
    output_bias = scatter_about(key_list[8], (D,), 0.5, 3.0, ((0, 8),))
    mlp_gain = jnp.clip(1.0 + 0.1 * jax.random.normal(key_list[9], (D,), jnp.float32), 0.5, 1.5).astype(jnp.bfloat16)
    mlp_bias = scatter_about(key_list[10], (D,), 0.5, 3.0, ((0, 8),))
    up_matrix_weight = scatter_about(key_list[11], (D, FF), D ** -0.5, 0.21875, ((0, 8),))
    up_offset_bias = scatter_about(key_list[12], (FF,), 0.5, 3.0, ((0, 8),))
    down_matrix_weight = scatter_about(key_list[13], (FF, D), FF ** -0.5, 0.109375, ((0, 8),))
    down_offset_bias = scatter_about(key_list[14], (D,), 0.5, 3.0, ((0, 8),))
    segments = jax.vmap(lambda own: jnp.searchsorted(jnp.cumsum(uneven(own, 4, LEN, LEN // 2, 1)), jnp.arange(LEN), side="right"))(jax.random.split(key_list[15], SEQS)).reshape((SEQS, LEN)).astype(jnp.int32)
    positions = with_ends(jax.random.randint(key_list[16], (2, SEQS, LEN), 0, 64), jax.random.fold_in(key_list[16], 1), 0, 63).astype(jnp.int32)
    cotangent = scatter_about(key_list[17], (SEQS, LEN, D), 1.0, 6.0, ((0, 8), (1, 4)))
    return dict(tokens=tokens, pre_gain=pre_gain, pre_bias=pre_bias, query_key_value_weight=query_key_value_weight, query_key_value_bias=query_key_value_bias, query_gain=query_gain, key_gain=key_gain, output_weight=output_weight, output_bias=output_bias, mlp_gain=mlp_gain, mlp_bias=mlp_bias, up_matrix_weight=up_matrix_weight, up_offset_bias=up_offset_bias, down_matrix_weight=down_matrix_weight, down_offset_bias=down_offset_bias, segments=segments, positions=positions, cotangent=cotangent)


EPSILON = 1e-06
NEGATIVE = -1e+30
ROPE_BASE = 100.0
TOP_PRECISION = lax.Precision.HIGHEST

@jax.custom_vjp
def low(v):
    return lax.optimization_barrier(v.astype(jnp.bfloat16)).astype(jnp.float32)

@jax.custom_vjp
def low_back(v):
    return v

def low_keep(v):
    return (low(v), None)

def low_pass(kept, grad):
    return (grad,)

def back_keep(v):
    return (v, None)

def back_low(kept, grad):
    return (low(grad),)
low.defvjp(low_keep, low_pass)
low_back.defvjp(back_keep, back_low)

def layer_norm(values, scale_gain, shift_vec):
    row_mean = lax.optimization_barrier(jnp.mean(values, axis=-1, keepdims=True))
    centred = values - row_mean
    variance = lax.optimization_barrier(jnp.mean(centred * centred, axis=-1, keepdims=True))
    return centred * lax.rsqrt(variance + EPSILON) * scale_gain + shift_vec

def rotation(positions):
    quarter = HD // 4
    frequency = ROPE_BASE ** (-jnp.arange(quarter, dtype=jnp.float32) / quarter)
    places = jnp.moveaxis(positions, 0, -1).astype(jnp.float32)
    angles = places[..., None] * frequency
    return (jnp.cos(angles)[:, :, None], jnp.sin(angles)[:, :, None])

def turn_heads(vectors, scale_gain, cos_table, sine_table):
    row_mean = lax.optimization_barrier(jnp.mean(vectors, axis=-1, keepdims=True))
    centred = vectors - row_mean
    variance = lax.optimization_barrier(jnp.mean(centred * centred, axis=-1, keepdims=True))
    normalized_rows = centred * lax.rsqrt(variance + EPSILON) * scale_gain
    quarter = HD // 4
    pieces = normalized_rows.reshape(normalized_rows.shape[:-1] + (2, 2, quarter))
    first_half = pieces[..., 0, :]
    second = pieces[..., 1, :]
    turned = jnp.stack((first_half * cos_table - second * sine_table, second * cos_table + first_half * sine_table), axis=-2)
    return turned.reshape(normalized_rows.shape) * HD ** (-0.5)

def attend_one(bundle):
    queries, key_heads, value_heads, labels = bundle
    scores = jnp.einsum('qhd,khd->hqk', queries, key_heads, precision=TOP_PRECISION)
    scores = low_back(scores)
    same_image = labels[:, None] == labels[None, :]
    scores = jnp.where(same_image[None], scores, NEGATIVE)
    chances = jax.nn.softmax(scores, axis=-1)
    return jnp.einsum('hqk,khd->qhd', low(chances), value_heads, precision=TOP_PRECISION)

def forward(params, inputs, labels, positions):
    pre_gain, pre_bias, query_key_value_weight, query_key_value_bias, query_gain, key_gain, output_weight, output_bias, mlp_gain, mlp_bias, up_matrix_weight, up_offset_bias, down_matrix_weight, down_offset_bias = params
    per_round = inputs.shape[0]
    normalized_rows = low(layer_norm(inputs, pre_gain, pre_bias))
    projected_rows = jnp.einsum('wgz,zv->wgv', normalized_rows, query_key_value_weight, precision=TOP_PRECISION) + query_key_value_bias
    projected_rows = low(low_back(projected_rows))
    split_shape = (per_round, LEN, H, HD)
    queries = projected_rows[..., :D].reshape(split_shape)
    key_heads = projected_rows[..., D:2 * D].reshape(split_shape)
    value_heads = projected_rows[..., 2 * D:].reshape(split_shape)
    cos_table, sine_table = rotation(positions)
    queries = low(turn_heads(queries, query_gain.reshape(H, HD), cos_table, sine_table))
    key_heads = low(turn_heads(key_heads, key_gain.reshape(H, HD), cos_table, sine_table))
    attended_output = lax.map(jax.checkpoint(attend_one), (queries, key_heads, value_heads, labels))
    attended_output = low(low_back(attended_output.reshape(per_round, LEN, D)))
    attention_branch = low_back(jnp.einsum('wgz,zv->wgv', attended_output, output_weight, precision=TOP_PRECISION) + output_bias)
    middle = inputs + attention_branch
    hidden_state = low(layer_norm(middle, mlp_gain, mlp_bias))
    before_activation = low_back(jnp.einsum('anj,je->ane', hidden_state, up_matrix_weight, precision=TOP_PRECISION) + up_offset_bias)
    active_hidden = low(jax.nn.gelu(before_activation, approximate=False))
    feedforward_branch = low_back(jnp.einsum('pkq,qe->pke', active_hidden, down_matrix_weight, precision=TOP_PRECISION) + down_offset_bias)
    return middle + feedforward_branch

def reference(tokens, pre_gain, pre_bias, query_key_value_weight, query_key_value_bias, query_gain, key_gain, output_weight, output_bias, mlp_gain, mlp_bias, up_matrix_weight, up_offset_bias, down_matrix_weight, down_offset_bias, segments, positions, cotangent):
    params = tuple((member.astype(jnp.float32) for member in (pre_gain, pre_bias, query_key_value_weight, query_key_value_bias, query_gain, key_gain, output_weight, output_bias, mlp_gain, mlp_bias, up_matrix_weight, up_offset_bias, down_matrix_weight, down_offset_bias)))
    per_round = math.gcd(SEQS, 4)
    rounds = SEQS // per_round
    inputs = tokens.astype(jnp.float32).reshape(rounds, per_round, LEN, D)
    grads_in = cotangent.astype(jnp.float32).reshape(rounds, per_round, LEN, D)
    labels = segments.reshape(rounds, per_round, LEN)
    places = jnp.moveaxis(positions.reshape(2, rounds, per_round, LEN), 1, 0)

    def advance(totals, bundle):
        block_in, block_grad, block_labels, block_places = bundle

        def apply_layer(weights, values):
            return forward(weights, values, block_labels, block_places)
        result, pullback = jax.vjp(apply_layer, params, block_in)
        weight_grads, input_grads = pullback(block_grad)
        totals = jax.tree.map(jnp.add, totals, weight_grads)
        return (totals, (result.astype(jnp.bfloat16), input_grads.astype(jnp.bfloat16)))
    start_sums = jax.tree.map(jnp.zeros_like, params)
    totals, (results, input_grads) = lax.scan(advance, start_sums, (inputs, grads_in, labels, places))
    return (results.reshape(SEQS, LEN, D), input_grads.reshape(SEQS, LEN, D), totals[0], totals[1], totals[2], totals[3][:2 * D], totals[3][2 * D:], totals[4], totals[5], totals[6], totals[7], totals[8], totals[9], totals[10], totals[11], totals[12], totals[13])
```

```python
import functools

import jax
import jax.numpy as jnp
from jax import lax
from jax.experimental import pallas as pl
from jax.experimental.pallas import tpu as pltpu
from jax.sharding import PartitionSpec as P

H = 12
HD = 64
EPSILON = 1e-06
NEGATIVE = -1e30
ROPE_BASE = 100.0
F32 = jnp.float32
BF16 = jnp.bfloat16
TILE = 256


def dot_nn(a, b):
    return lax.dot_general(a, b, (((1,), (0,)), ((), ())), preferred_element_type=F32)


def dot_nt(a, b):
    return lax.dot_general(a, b, (((1,), (1,)), ((), ())), preferred_element_type=F32)


def dot_tn(a, b):
    return lax.dot_general(a, b, (((0,), (0,)), ((), ())), preferred_element_type=F32)


def tile_at(index, size=TILE):
    return pl.ds(pl.multiple_of(index * size, size), size)


def loop(count, body):
    def step(index, carry):
        body(index)
        return carry

    lax.fori_loop(0, count, step, 0)


def rows_sum(block):
    rows, width = block.shape
    return jnp.sum(block.reshape(rows // 8, 8, width), axis=0)


def column_sums_exact(ones, block):
    return dot_nn(ones, block)[0:1]


def place_tokens(r):
    bundle, length = r.place.shape
    labels = r.meta[0:1, :].astype(F32)
    start = jnp.zeros((1, 1), F32)
    found = jnp.zeros((1, 1), F32)
    for value in range(4):
        here = jnp.sum(jnp.where(labels == value, 1.0, 0.0), axis=1, keepdims=True)
        below = jnp.sum(jnp.where(labels < value, 1.0, 0.0), axis=1, keepdims=True)
        hit = jnp.where(here == bundle, 1.0, 0.0) * (1.0 - found)
        start = start + hit * below
        found = found + hit
    r.start[...] = jnp.broadcast_to(start, r.start.shape)
    core = lax.axis_index("seq") % 2

    def block(index):
        rows = tile_at(index, 128)
        shape = (128, length)
        mine = lax.broadcasted_iota(jnp.int32, shape, 0) + (index * 128 + core * bundle)
        target = mine.astype(F32) + start
        target = jnp.where(target >= length, target - length, target)
        source = lax.broadcasted_iota(jnp.int32, shape, 1).astype(F32)
        r.place[rows, :] = jnp.where(source == target, 1.0, 0.0).astype(BF16)

    loop(bundle // 128, block)
    r.marks_row[...] = dot_nt(r.meta[...], r.place[...])
    r.marks_col[...] = dot_nt(r.place[...], r.meta[...])


def rope_tables(r):
    quarter = HD // 4
    bundle = r.cosine.shape[-1]
    step = lax.broadcasted_iota(jnp.int32, (quarter, bundle), 0).astype(F32)
    frequency = jnp.exp(step * (-jnp.log(jnp.float32(ROPE_BASE)) / quarter))
    for axis in range(2):
        angle = r.marks_row[1 + axis : 2 + axis, :] * frequency
        r.cosine[axis] = jnp.cos(angle)
        r.sine[axis] = jnp.sin(angle)


def normalized(block):
    mean = jnp.mean(block, axis=-1, keepdims=True)
    centred = block - mean
    scale = lax.rsqrt(jnp.mean(centred * centred, axis=-1, keepdims=True) + EPSILON)
    return centred * scale, scale


def norm_rows(source, gain, bias, target, rows=32):
    def block(index):
        where = tile_at(index, rows)
        unit, _ = normalized(source[where, :].astype(F32))
        target[where, :] = (unit * gain + bias).astype(target.dtype)

    loop(source.shape[0] // rows, block)


def norm_rows_back(source, grads, base, gain, store, rows=32):
    width = source.shape[1]

    def block(index, carry):
        gain_sum, bias_sum = carry
        where = tile_at(index, rows)
        unit, scale = normalized(source[where, :].astype(F32))
        outer = grads[where, :]
        inner = outer * gain
        first = jnp.mean(inner, axis=-1, keepdims=True)
        second = jnp.mean(inner * unit, axis=-1, keepdims=True)
        store(where, base[where, :].astype(F32) + scale * (inner - first - unit * second))
        return gain_sum + rows_sum(outer * unit), bias_sum + rows_sum(outer)

    zero = jnp.zeros((8, width), F32)
    gain_sum, bias_sum = lax.fori_loop(0, source.shape[0] // rows, block, (zero, zero))
    return jnp.sum(gain_sum, axis=0, keepdims=True), jnp.sum(bias_sum, axis=0, keepdims=True)


def transpose_into(target, source):
    def block(index):
        where = tile_at(index, 128)
        target[where, :] = jnp.transpose(source[:, where])

    loop(source.shape[1] // 128, block)


def head_norm(vectors):
    mean = jnp.mean(vectors, axis=0, keepdims=True)
    centred = vectors - mean
    scale = lax.rsqrt(jnp.mean(centred * centred, axis=0, keepdims=True) + EPSILON)
    return centred * scale, scale


def turn(vectors, r):
    q = HD // 4
    out = []
    for axis in range(2):
        one, two = vectors[2 * axis * q : (2 * axis + 1) * q], vectors[(2 * axis + 1) * q : (2 * axis + 2) * q]
        cosine, sine = r.cosine[axis], r.sine[axis]
        out.append(one * cosine - two * sine)
        out.append(two * cosine + one * sine)
    return jnp.concatenate(out, axis=0) * HD ** (-0.5)


def turn_back(vectors, r):
    q = HD // 4
    out = []
    for axis in range(2):
        one, two = vectors[2 * axis * q : (2 * axis + 1) * q], vectors[(2 * axis + 1) * q : (2 * axis + 2) * q]
        cosine, sine = r.cosine[axis], r.sine[axis]
        out.append(one * cosine + two * sine)
        out.append(two * cosine - one * sine)
    return jnp.concatenate(out, axis=0) * HD ** (-0.5)


PRE_GAIN, PRE_BIAS, QUERY_GAIN, KEY_GAIN, OUT_BIAS, MLP_GAIN, MLP_BIAS, DOWN_BIAS = range(8)


def forward_attention(r):
    width = r.tokens.shape[1]
    norm_rows(r.tokens, r.small[PRE_GAIN : PRE_GAIN + 1, :], r.small[PRE_BIAS : PRE_BIAS + 1, :], r.hidden_pre)
    transpose_into(r.hidden_pre_t, r.hidden_pre)

    def project(index):
        cols = tile_at(index)
        part = dot_nn(r.hidden_pre[...], r.w_qkv[:, cols]) + r.qkv_bias[0:1, cols]
        r.projected_t[cols, :] = jnp.transpose(part.astype(BF16))

    loop(3 * width // TILE, project)

    def prepare(index):
        rows = tile_at(index, HD)
        unit, _ = head_norm(r.projected_t[rows, :].astype(F32))
        r.turned_t[rows, :] = turn(unit * r.head_gain[rows, 0:1], r).astype(BF16)

    loop(2 * H, prepare)

    def attend(index):
        rows = tile_at(index, HD)
        key_rows = tile_at(index + H, HD)
        value_rows = tile_at(index + 2 * H, HD)
        chance_rows = tile_at(index, r.tokens.shape[0])
        scores = dot_tn(r.turned_t[key_rows, :], r.turned_t[rows, :])
        scores = jnp.where(r.marks_col[:, 0:1] == r.marks_row[0:1, :], scores, NEGATIVE)
        raised = jnp.exp(scores - jnp.max(scores, axis=0, keepdims=True))
        chances = (raised * (1.0 / jnp.sum(raised, axis=0, keepdims=True))).astype(BF16)
        r.chances[chance_rows, :] = chances
        r.attended_t[rows, :] = dot_nn(r.projected_t[value_rows, :], chances).astype(BF16)

    loop(H, attend)
    transpose_into_rows(r.attended, r.attended_t)


def transpose_into_rows(target, source):
    def block(index):
        where = tile_at(index, 128)
        target[:, where] = jnp.transpose(source[where, :])

    loop(source.shape[0] // 128, block)


def forward_middle(r):
    width = r.tokens.shape[1]

    def branch(index):
        cols = tile_at(index)
        part = dot_nn(r.attended[...], r.w_out[:, cols]) + r.small[OUT_BIAS : OUT_BIAS + 1, cols]
        r.middle[:, cols] = r.tokens[:, cols].astype(F32) + part

    loop(width // TILE, branch)
    norm_rows(r.middle, r.small[MLP_GAIN : MLP_GAIN + 1, :], r.small[MLP_BIAS : MLP_BIAS + 1, :], r.hidden_mlp)
    transpose_into(r.hidden_mlp_t, r.hidden_mlp)


def forward_up(r):
    hidden = r.w_up.shape[1]

    def up(index):
        cols = tile_at(index)
        r.before[...] = dot_nn(r.hidden_mlp[...], r.w_up[:, cols]) + r.up_bias[0:1, cols]

        def activate(part):
            rows = tile_at(part, 64)
            v = r.before[rows, :]
            half = 0.5 + 0.5 * lax.erf(v * 0.7071067811865476)
            r.active[rows, cols] = (v * half).astype(BF16)
            r.slope[rows, cols] = (half + v * (jnp.exp(-0.5 * v * v) * 0.3989422804014327)).astype(BF16)

        loop(r.before.shape[0] // 64, activate)
        r.active_t[cols, :] = jnp.transpose(r.active[:, cols])

    loop(hidden // TILE, up)


def forward_down(r):
    def down(index):
        cols = tile_at(index)
        part = dot_nn(r.active[...], r.w_down[:, cols]) + r.small[DOWN_BIAS : DOWN_BIAS + 1, cols]
        r.result[:, cols] = (r.middle[:, cols] + part).astype(BF16)

    loop(r.w_down.shape[1] // TILE, down)


def backward_down(r):
    r.grad_small[DOWN_BIAS : DOWN_BIAS + 1, :] = column_sums_exact(r.ones[...], r.cotangent[...])

    def down(index):
        rows = tile_at(index)
        grads = dot_nt(r.cotangent[...], r.w_down[rows, :])
        before = (grads * r.slope[:, rows].astype(F32)).astype(BF16)
        r.slope[:, rows] = before
        r.grad_up_bias[0:1, rows] = column_sums_exact(r.ones[...], before)
        r.w_down[rows, :] = dot_nn(r.active_t[rows, :], r.cotangent[...]).astype(BF16)

    loop(r.w_down.shape[0] // TILE, down)


def backward_up(r):
    def hidden(index):
        cols = tile_at(index)
        r.grad_hidden[:, cols] = dot_nt(r.slope[...], r.w_up[cols, :])

    loop(r.w_up.shape[0] // TILE, hidden)

    def weight(index):
        cols = tile_at(index)
        r.w_up[:, cols] = dot_nn(r.hidden_mlp_t[...], r.slope[:, cols]).astype(BF16)

    loop(r.w_up.shape[1] // TILE, weight)


def backward_middle(r):
    def store(where, value):
        r.grad_middle[where, :] = value
        r.grad_branch[where, :] = value.astype(BF16)

    gain, bias = norm_rows_back(r.middle, r.grad_hidden, r.cotangent, r.small[MLP_GAIN : MLP_GAIN + 1, :], store)
    r.grad_small[MLP_GAIN : MLP_GAIN + 1, :] = gain
    r.grad_small[MLP_BIAS : MLP_BIAS + 1, :] = bias
    r.grad_small[OUT_BIAS : OUT_BIAS + 1, :] = column_sums_exact(r.ones[...], r.grad_branch[...])

    def attended(index):
        rows = tile_at(index)
        r.grad_attended_t[rows, :] = dot_nt(r.w_out[rows, :], r.grad_branch[...]).astype(BF16)
        r.w_out[rows, :] = dot_nn(r.attended_t[rows, :], r.grad_branch[...]).astype(BF16)

    loop(r.w_out.shape[0] // TILE, attended)


def backward_attention(r):
    def heads(index):
        rows = tile_at(index, HD)
        key_rows = tile_at(index + H, HD)
        value_rows = tile_at(index + 2 * H, HD)
        chance_rows = tile_at(index, r.tokens.shape[0])
        outer = r.grad_attended_t[rows, :]
        chances = r.chances[chance_rows, :]
        grads = dot_tn(r.projected_t[value_rows, :], outer)
        wide = chances.astype(F32)
        inner = jnp.sum(wide * grads, axis=0, keepdims=True)
        scores = (wide * (grads - inner)).astype(BF16)
        r.grad_projected_t[value_rows, :] = dot_nt(outer, chances).astype(BF16)
        for target, grad in (
            (rows, dot_nn(r.turned_t[key_rows, :], scores)),
            (key_rows, dot_nt(r.turned_t[rows, :], scores)),
        ):
            unit, scale = head_norm(r.projected_t[target, :].astype(F32))
            outer_turned = turn_back(grad, r)
            weighted = outer_turned * unit
            lanes = weighted.shape[1] // 128
            folded = weighted[:, 0:128]
            for lane in range(1, lanes):
                folded = folded + weighted[:, lane * 128 : (lane + 1) * 128]
            r.head_gain_sums[target, :] = folded
            inner_turned = outer_turned * r.head_gain[target, 0:1]
            first = jnp.mean(inner_turned, axis=0, keepdims=True)
            second = jnp.mean(inner_turned * unit, axis=0, keepdims=True)
            r.grad_projected_t[target, :] = (scale * (inner_turned - first - unit * second)).astype(BF16)

    loop(H, heads)


def split3(block):
    high = block.astype(BF16)
    rest = block - high.astype(F32)
    middle = rest.astype(BF16)
    return high, middle, (rest - middle.astype(F32)).astype(BF16)


def backward_inputs(r):
    width = r.tokens.shape[1]
    ones = r.ones[:, 0:128]
    sums = sum(dot_nt(ones, part)[0:1] for part in split3(r.head_gain_sums[...]))
    r.grad_small[QUERY_GAIN : QUERY_GAIN + 1, :] = sums[:, :width]
    r.grad_small[KEY_GAIN : KEY_GAIN + 1, :] = sums[:, width:]
    r.grad_qkv_bias[0:1, :] = dot_nt(r.ones[...], r.grad_projected_t[...])[0:1]

    def hidden(index):
        rows = tile_at(index)
        r.grad_hidden[:, rows] = jnp.transpose(dot_nn(r.w_qkv[rows, :], r.grad_projected_t[...]))

    loop(width // TILE, hidden)

    def weight(index):
        cols = tile_at(index)
        r.w_qkv[:, cols] = dot_nt(r.hidden_pre_t[...], r.grad_projected_t[cols, :]).astype(BF16)

    loop(3 * width // TILE, weight)

    def store(where, value):
        r.grad_result[where, :] = value.astype(BF16)

    gain, bias = norm_rows_back(r.tokens, r.grad_hidden, r.grad_middle, r.small[PRE_GAIN : PRE_GAIN + 1, :], store)
    r.grad_small[PRE_GAIN : PRE_GAIN + 1, :] = gain
    r.grad_small[PRE_BIAS : PRE_BIAS + 1, :] = bias


class Refs:
    pass


WEIGHTS = ("w_qkv", "w_out", "w_up", "w_down")


def layer_kernel(names, *refs):
    r = Refs()
    for name, ref in zip(names, refs, strict=True):
        setattr(r, name, ref)
    copies = [
        pltpu.make_async_copy(getattr(r, name + "_in"), getattr(r, name), r.sems.at[i]) for i, name in enumerate(WEIGHTS)
    ]
    for copy in copies:
        copy.start()
    r.ones[...] = jnp.ones(r.ones.shape, BF16)
    place_tokens(r)
    r.tokens[...] = dot_nn(r.place[...], r.seq_tokens[...]).astype(BF16)
    r.cotangent[...] = dot_nn(r.place[...], r.seq_cotangent[...]).astype(BF16)
    rope_tables(r)
    width = r.tokens.shape[1]
    columns = jnp.transpose(r.small[...])
    r.head_gain[0:width, :] = columns[:, QUERY_GAIN : QUERY_GAIN + 1]
    r.head_gain[width : 2 * width, :] = columns[:, KEY_GAIN : KEY_GAIN + 1]
    for copy in copies:
        copy.wait()
    forward_attention(r)
    forward_middle(r)
    forward_up(r)
    forward_down(r)
    backward_down(r)
    backward_up(r)
    backward_middle(r)
    backward_attention(r)
    backward_inputs(r)
    back = [
        pltpu.make_async_copy(getattr(r, name), getattr(r, name + "_grad"), r.sems.at[i]) for i, name in enumerate(WEIGHTS)
    ]
    for copy in back:
        copy.start()
    for copy in back:
        copy.wait()


def layer(seq_tokens, seq_cotangent, meta, small, qkv_bias, up_bias, w_qkv, w_out, w_up, w_down):
    length, width = seq_tokens.shape
    bundle = length // 2
    hidden = w_up.shape[1]
    shape = jax.ShapeDtypeStruct
    vmem = pl.BlockSpec(memory_space=pltpu.VMEM)
    hbm = pl.BlockSpec(memory_space=pl.ANY)
    inputs = dict(
        seq_tokens=(seq_tokens, vmem),
        seq_cotangent=(seq_cotangent, vmem),
        meta=(meta, vmem),
        small=(small, vmem),
        qkv_bias=(qkv_bias, vmem),
        up_bias=(up_bias, vmem),
        w_qkv_in=(w_qkv, hbm),
        w_out_in=(w_out, hbm),
        w_up_in=(w_up, hbm),
        w_down_in=(w_down, hbm),
    )
    outputs = dict(
        result=(shape((bundle, width), BF16), vmem),
        grad_result=(shape((bundle, width), BF16), vmem),
        grad_small=(shape((8, width), F32), vmem),
        grad_qkv_bias=(shape((8, 3 * width), F32), vmem),
        grad_up_bias=(shape((8, hidden), F32), vmem),
        w_qkv_grad=(shape(w_qkv.shape, BF16), hbm),
        w_out_grad=(shape(w_out.shape, BF16), hbm),
        w_up_grad=(shape(w_up.shape, BF16), hbm),
        w_down_grad=(shape(w_down.shape, BF16), hbm),
    )
    scratch = dict(
        w_qkv=pltpu.VMEM(w_qkv.shape, BF16),
        w_out=pltpu.VMEM(w_out.shape, BF16),
        w_up=pltpu.VMEM(w_up.shape, BF16),
        w_down=pltpu.VMEM(w_down.shape, BF16),
        sems=pltpu.SemaphoreType.DMA((4,)),
        ones=pltpu.VMEM((8, bundle), BF16),
        start=pltpu.VMEM((8, 128), F32),
        place=pltpu.VMEM((bundle, length), BF16),
        marks_row=pltpu.VMEM((8, bundle), F32),
        marks_col=pltpu.VMEM((bundle, 8), F32),
        cosine=pltpu.VMEM((2, HD // 4, bundle), F32),
        sine=pltpu.VMEM((2, HD // 4, bundle), F32),
        head_gain=pltpu.VMEM((2 * width, 1), F32),
        head_gain_sums=pltpu.VMEM((2 * width, 128), F32),
        tokens=pltpu.VMEM((bundle, width), BF16),
        cotangent=pltpu.VMEM((bundle, width), BF16),
        hidden_pre=pltpu.VMEM((bundle, width), BF16),
        hidden_pre_t=pltpu.VMEM((width, bundle), BF16),
        projected_t=pltpu.VMEM((3 * width, bundle), BF16),
        turned_t=pltpu.VMEM((2 * width, bundle), BF16),
        chances=pltpu.VMEM((H * bundle, bundle), BF16),
        attended_t=pltpu.VMEM((width, bundle), BF16),
        attended=pltpu.VMEM((bundle, width), BF16),
        middle=pltpu.VMEM((bundle, width), F32),
        hidden_mlp=pltpu.VMEM((bundle, width), BF16),
        hidden_mlp_t=pltpu.VMEM((width, bundle), BF16),
        before=pltpu.VMEM((bundle, TILE), F32),
        active=pltpu.VMEM((bundle, hidden), BF16),
        active_t=pltpu.VMEM((hidden, bundle), BF16),
        slope=pltpu.VMEM((bundle, hidden), BF16),
        grad_hidden=pltpu.VMEM((bundle, width), F32),
        grad_middle=pltpu.VMEM((bundle, width), F32),
        grad_branch=pltpu.VMEM((bundle, width), BF16),
        grad_attended_t=pltpu.VMEM((width, bundle), BF16),
        grad_projected_t=pltpu.VMEM((3 * width, bundle), BF16),
    )
    names = tuple(inputs) + tuple(outputs) + tuple(scratch)
    return pl.pallas_call(
        functools.partial(layer_kernel, names),
        out_shape=tuple(o[0] for o in outputs.values()),
        in_specs=[i[1] for i in inputs.values()],
        out_specs=tuple(o[1] for o in outputs.values()),
        scratch_shapes=list(scratch.values()),
        compiler_params=pltpu.CompilerParams(vmem_limit_bytes=62 << 20),
        name="layer",
    )(*(i[0] for i in inputs.values()))


def shards(
    tokens,
    pre_gain,
    pre_bias,
    query_key_value_weight,
    query_key_value_bias,
    query_gain,
    key_gain,
    output_weight,
    output_bias,
    mlp_gain,
    mlp_bias,
    up_matrix_weight,
    up_offset_bias,
    down_matrix_weight,
    down_offset_bias,
    segments,
    positions,
    cotangent,
):
    rank = lax.axis_index("seq")
    x = rank // 2
    width = tokens.shape[2]
    length = segments.shape[1]
    fsdp = lax.axis_size("fsdp")
    gather = functools.partial(lax.all_gather, axis_name="fsdp", axis=0, tiled=True)
    w_qkv, w_out, w_up, w_down = map(
        gather, (query_key_value_weight, output_weight, up_matrix_weight, down_matrix_weight)
    )
    vectors = (
        pre_gain, pre_bias, query_gain, key_gain, output_bias, mlp_gain, mlp_bias, down_offset_bias,
        query_key_value_bias, up_offset_bias,
    )
    packed = gather(jnp.concatenate(vectors)[None]).astype(F32)
    part = width // fsdp
    small = jnp.stack([packed[:, i * part : (i + 1) * part].reshape(width) for i in range(8)])
    qkv_bias = packed[:, 8 * part : 11 * part].reshape(1, 3 * width)
    up_bias = packed[:, 11 * part :].reshape(1, -1)
    seq_tokens = lax.dynamic_index_in_dim(lax.all_gather(tokens, "seq", axis=1, tiled=True), x, 0, False)
    seq_cotangent = lax.dynamic_index_in_dim(lax.all_gather(cotangent, "seq", axis=1, tiled=True), x, 0, False)
    labels = lax.dynamic_index_in_dim(segments, x, 0, True)
    places = lax.dynamic_index_in_dim(positions, x, 1, False)
    meta = jnp.concatenate([labels, places, jnp.zeros((5, length), jnp.int32)], axis=0).astype(BF16)
    result, grad_result, grad_small, grad_qkv_bias, grad_up_bias, *weight_grads = layer(
        seq_tokens, seq_cotangent, meta, small, qkv_bias, up_bias, w_qkv, w_out, w_up, w_down
    )
    counts = jnp.stack([jnp.sum(segments == v, axis=1) for v in range(4)])
    first = jnp.argmax(counts == length // 2, axis=0)
    starts = jnp.sum(segments < first[:, None], axis=1)

    def home(bundle):
        every = lax.all_gather(bundle, "seq").reshape(2, length, width)
        own = rank * (length // 4) + jnp.arange(length // 4)
        index = (own[None] - starts[:, None]) % length
        return jnp.take_along_axis(every, index[..., None], axis=1)

    scatter = functools.partial(lax.psum_scatter, axis_name="fsdp", scatter_dimension=0, tiled=True)

    def finish(grad):
        return lax.psum(scatter(grad).astype(BF16), "seq").astype(F32)

    weights = [finish(g) for g in weight_grads]
    pieces = [grad_small[i].reshape(fsdp, part) for i in range(8)]
    pieces += [grad_qkv_bias[0, : 2 * width].reshape(fsdp, -1), grad_qkv_bias[0, 2 * width :].reshape(fsdp, -1)]
    pieces += [grad_up_bias[0].reshape(fsdp, -1)]
    total = lax.psum(scatter(jnp.concatenate(pieces, axis=1)), "seq")[0]
    s = [total[i * part : (i + 1) * part] for i in range(8)]
    query_key_bias, value_bias, up_total = total[8 * part : 10 * part], total[10 * part : 11 * part], total[11 * part :]
    return (
        home(result), home(grad_result), s[PRE_GAIN], s[PRE_BIAS], weights[0], query_key_bias, value_bias,
        s[QUERY_GAIN], s[KEY_GAIN], weights[1], s[OUT_BIAS], s[MLP_GAIN], s[MLP_BIAS], weights[2], up_total,
        weights[3], s[DOWN_BIAS],
    )


def solution(mesh):
    rows, matrix, activations = P("fsdp"), P("fsdp", None), P("fsdp", "seq", None)
    placed = (
        activations, rows, rows, matrix, rows, rows, rows, matrix, rows, rows, rows, matrix, rows, matrix, rows,
        P("fsdp", None), P(None, "fsdp", None), activations,
    )
    given = (
        activations, activations, rows, rows, matrix, rows, rows, rows, rows, matrix, rows, rows, rows, matrix, rows,
        matrix, rows,
    )
    return jax.shard_map(shards, mesh=mesh, in_specs=placed, out_specs=given, check_vma=False)
```

```python
import functools

import jax
import jax.numpy as jnp
from jax import lax
from jax.experimental import pallas as pl
from jax.experimental.pallas import tpu as pltpu
from jax.sharding import PartitionSpec as P

H = 12
HD = 64
EPSILON = 1e-06
NEGATIVE = -1e30
ROPE_BASE = 100.0
F32 = jnp.float32
BF16 = jnp.bfloat16
TILE = 256


def dot_nn(a, b):
    return lax.dot_general(a, b, (((1,), (0,)), ((), ())), preferred_element_type=F32)


def dot_nt(a, b):
    return lax.dot_general(a, b, (((1,), (1,)), ((), ())), preferred_element_type=F32)


def dot_tn(a, b):
    return lax.dot_general(a, b, (((0,), (0,)), ((), ())), preferred_element_type=F32)


def tile_at(index, size=TILE):
    return pl.ds(pl.multiple_of(index * size, size), size)


def loop(count, body, first=0):
    def step(index, carry):
        body(index)
        return carry

    lax.fori_loop(first, first + count, step, 0)


def loop_beside(count, body, gather, parts, steps):
    for part in range(parts):
        loop(count // parts, body, part * (count // parts))
        gather.advance(steps)


def rows_sum(block):
    rows, width = block.shape
    return jnp.sum(block.reshape(rows // 8, 8, width), axis=0)


def column_sums_exact(ones, block):
    return dot_nn(ones, block)[0:1]


def place_tokens(r):
    bundle, length = r.place.shape
    labels = r.meta[0:1, :].astype(F32)
    start = jnp.zeros((1, 1), F32)
    found = jnp.zeros((1, 1), F32)
    for value in range(4):
        here = jnp.sum(jnp.where(labels == value, 1.0, 0.0), axis=1, keepdims=True)
        below = jnp.sum(jnp.where(labels < value, 1.0, 0.0), axis=1, keepdims=True)
        hit = jnp.where(here == bundle, 1.0, 0.0) * (1.0 - found)
        start = start + hit * below
        found = found + hit
    r.start[...] = jnp.broadcast_to(start, r.start.shape)
    core = lax.axis_index("seq") % 2

    def block(index):
        rows = tile_at(index, 128)
        shape = (128, length)
        mine = lax.broadcasted_iota(jnp.int32, shape, 0) + (index * 128 + core * bundle)
        target = mine.astype(F32) + start
        target = jnp.where(target >= length, target - length, target)
        source = lax.broadcasted_iota(jnp.int32, shape, 1).astype(F32)
        r.place[rows, :] = jnp.where(source == target, 1.0, 0.0).astype(BF16)

    loop(bundle // 128, block)
    r.marks_row[...] = dot_nt(r.meta[...], r.place[...])
    r.marks_col[...] = dot_nt(r.place[...], r.meta[...])


def rope_tables(r):
    quarter = HD // 4
    bundle = r.cosine.shape[-1]
    step = lax.broadcasted_iota(jnp.int32, (quarter, bundle), 0).astype(F32)
    frequency = jnp.exp(step * (-jnp.log(jnp.float32(ROPE_BASE)) / quarter))
    for axis in range(2):
        angle = r.marks_row[1 + axis : 2 + axis, :] * frequency
        r.cosine[axis] = jnp.cos(angle)
        r.sine[axis] = jnp.sin(angle)


def normalized(block):
    mean = jnp.mean(block, axis=-1, keepdims=True)
    centred = block - mean
    scale = lax.rsqrt(jnp.mean(centred * centred, axis=-1, keepdims=True) + EPSILON)
    return centred * scale, scale


def norm_rows(source, gain, bias, target, rows=32):
    def block(index):
        where = tile_at(index, rows)
        unit, _ = normalized(source[where, :].astype(F32))
        target[where, :] = (unit * gain + bias).astype(target.dtype)

    loop(source.shape[0] // rows, block)


def norm_rows_back(source, grads, base, gain, store, rows=32):
    width = source.shape[1]

    def block(index, carry):
        gain_sum, bias_sum = carry
        where = tile_at(index, rows)
        unit, scale = normalized(source[where, :].astype(F32))
        outer = grads[where, :]
        inner = outer * gain
        first = jnp.mean(inner, axis=-1, keepdims=True)
        second = jnp.mean(inner * unit, axis=-1, keepdims=True)
        store(where, base[where, :].astype(F32) + scale * (inner - first - unit * second))
        return gain_sum + rows_sum(outer * unit), bias_sum + rows_sum(outer)

    zero = jnp.zeros((8, width), F32)
    gain_sum, bias_sum = lax.fori_loop(0, source.shape[0] // rows, block, (zero, zero))
    return jnp.sum(gain_sum, axis=0, keepdims=True), jnp.sum(bias_sum, axis=0, keepdims=True)


def transpose_into(target, source):
    def block(index):
        where = tile_at(index, 128)
        target[where, :] = jnp.transpose(source[:, where])

    loop(source.shape[1] // 128, block)


def head_norm(vectors):
    mean = jnp.mean(vectors, axis=0, keepdims=True)
    centred = vectors - mean
    scale = lax.rsqrt(jnp.mean(centred * centred, axis=0, keepdims=True) + EPSILON)
    return centred * scale, scale


def turn(vectors, r):
    q = HD // 4
    out = []
    for axis in range(2):
        one, two = vectors[2 * axis * q : (2 * axis + 1) * q], vectors[(2 * axis + 1) * q : (2 * axis + 2) * q]
        cosine, sine = r.cosine[axis], r.sine[axis]
        out.append(one * cosine - two * sine)
        out.append(two * cosine + one * sine)
    return jnp.concatenate(out, axis=0) * HD ** (-0.5)


def turn_back(vectors, r):
    q = HD // 4
    out = []
    for axis in range(2):
        one, two = vectors[2 * axis * q : (2 * axis + 1) * q], vectors[(2 * axis + 1) * q : (2 * axis + 2) * q]
        cosine, sine = r.cosine[axis], r.sine[axis]
        out.append(one * cosine + two * sine)
        out.append(two * cosine - one * sine)
    return jnp.concatenate(out, axis=0) * HD ** (-0.5)


PRE_GAIN, PRE_BIAS, QUERY_GAIN, KEY_GAIN, OUT_BIAS, MLP_GAIN, MLP_BIAS, DOWN_BIAS = range(8)


def forward_attention(r, gather):
    width = r.tokens.shape[1]
    norm_rows(r.tokens, r.small[PRE_GAIN : PRE_GAIN + 1, :], r.small[PRE_BIAS : PRE_BIAS + 1, :], r.hidden_pre)
    transpose_into(r.hidden_pre_t, r.hidden_pre)
    gather.finish(0)

    def project(index):
        cols = tile_at(index)
        part = dot_nn(r.hidden_pre[...], r.w_qkv[:, cols]) + r.qkv_bias[0:1, cols]
        r.projected_t[cols, :] = jnp.transpose(part.astype(BF16))

    loop_beside(3 * width // TILE, project, gather, 3, 2)

    def prepare(index):
        rows = tile_at(index, HD)
        unit, _ = head_norm(r.projected_t[rows, :].astype(F32))
        r.turned_t[rows, :] = turn(unit * r.head_gain[rows, 0:1], r).astype(BF16)

    loop_beside(2 * H, prepare, gather, 2, 2)

    def attend(index):
        rows = tile_at(index, HD)
        key_rows = tile_at(index + H, HD)
        value_rows = tile_at(index + 2 * H, HD)
        chance_rows = tile_at(index, r.tokens.shape[0])
        scores = dot_tn(r.turned_t[key_rows, :], r.turned_t[rows, :])
        scores = jnp.where(r.marks_col[:, 0:1] == r.marks_row[0:1, :], scores, NEGATIVE)
        raised = jnp.exp(scores - jnp.max(scores, axis=0, keepdims=True))
        chances = (raised * (1.0 / jnp.sum(raised, axis=0, keepdims=True))).astype(BF16)
        r.chances[chance_rows, :] = chances
        r.attended_t[rows, :] = dot_nn(r.projected_t[value_rows, :], chances).astype(BF16)

    loop_beside(H, attend, gather, 6, 3)
    transpose_into_rows(r.attended, r.attended_t)


def transpose_into_rows(target, source):
    def block(index):
        where = tile_at(index, 128)
        target[:, where] = jnp.transpose(source[where, :])

    loop(source.shape[0] // 128, block)


def forward_middle(r):
    width = r.tokens.shape[1]

    def branch(index):
        cols = tile_at(index)
        part = dot_nn(r.attended[...], r.w_out[:, cols]) + r.small[OUT_BIAS : OUT_BIAS + 1, cols]
        r.middle[:, cols] = r.tokens[:, cols].astype(F32) + part

    loop(width // TILE, branch)
    norm_rows(r.middle, r.small[MLP_GAIN : MLP_GAIN + 1, :], r.small[MLP_BIAS : MLP_BIAS + 1, :], r.hidden_mlp)
    transpose_into(r.hidden_mlp_t, r.hidden_mlp)


def forward_up(r, gather):
    hidden = r.w_up.shape[1]

    def up(index):
        cols = tile_at(index)
        r.before[...] = dot_nn(r.hidden_mlp[...], r.w_up[:, cols]) + r.up_bias[0:1, cols]

        def activate(part):
            rows = tile_at(part, 64)
            v = r.before[rows, :]
            half = 0.5 + 0.5 * lax.erf(v * 0.7071067811865476)
            r.active[rows, cols] = (v * half).astype(BF16)
            r.slope[rows, cols] = (half + v * (jnp.exp(-0.5 * v * v) * 0.3989422804014327)).astype(BF16)

        loop(r.before.shape[0] // 64, activate)
        r.active_t[cols, :] = jnp.transpose(r.active[:, cols])

    loop_beside(hidden // TILE, up, gather, 4, 3)


def forward_down(r):
    def down(index):
        cols = tile_at(index)
        part = dot_nn(r.active[...], r.w_down[:, cols]) + r.small[DOWN_BIAS : DOWN_BIAS + 1, cols]
        r.result[:, cols] = (r.middle[:, cols] + part).astype(BF16)

    loop(r.w_down.shape[1] // TILE, down)


def backward_down(r):
    r.grad_small[DOWN_BIAS : DOWN_BIAS + 1, :] = column_sums_exact(r.ones[...], r.cotangent[...])

    def down(index):
        rows = tile_at(index)
        grads = dot_nt(r.cotangent[...], r.w_down[rows, :])
        before = (grads * r.slope[:, rows].astype(F32)).astype(BF16)
        r.slope[:, rows] = before
        r.grad_up_bias[0:1, rows] = column_sums_exact(r.ones[...], before)
        r.w_down[rows, :] = dot_nn(r.active_t[rows, :], r.cotangent[...]).astype(BF16)

    loop(r.w_down.shape[0] // TILE, down)


def backward_up(r):
    def hidden(index):
        cols = tile_at(index)
        r.grad_hidden[:, cols] = dot_nt(r.slope[...], r.w_up[cols, :])

    loop(r.w_up.shape[0] // TILE, hidden)

    def weight(index):
        cols = tile_at(index)
        r.w_up[:, cols] = dot_nn(r.hidden_mlp_t[...], r.slope[:, cols]).astype(BF16)

    loop(r.w_up.shape[1] // TILE, weight)


def backward_middle(r):
    def store(where, value):
        r.grad_middle[where, :] = value
        r.grad_branch[where, :] = value.astype(BF16)

    gain, bias = norm_rows_back(r.middle, r.grad_hidden, r.cotangent, r.small[MLP_GAIN : MLP_GAIN + 1, :], store)
    r.grad_small[MLP_GAIN : MLP_GAIN + 1, :] = gain
    r.grad_small[MLP_BIAS : MLP_BIAS + 1, :] = bias
    r.grad_small[OUT_BIAS : OUT_BIAS + 1, :] = column_sums_exact(r.ones[...], r.grad_branch[...])

    def attended(index):
        rows = tile_at(index)
        r.grad_attended_t[rows, :] = dot_nt(r.w_out[rows, :], r.grad_branch[...]).astype(BF16)
        r.w_out[rows, :] = dot_nn(r.attended_t[rows, :], r.grad_branch[...]).astype(BF16)

    loop(r.w_out.shape[0] // TILE, attended)


def backward_attention(r):
    def heads(index):
        rows = tile_at(index, HD)
        key_rows = tile_at(index + H, HD)
        value_rows = tile_at(index + 2 * H, HD)
        chance_rows = tile_at(index, r.tokens.shape[0])
        outer = r.grad_attended_t[rows, :]
        chances = r.chances[chance_rows, :]
        grads = dot_tn(r.projected_t[value_rows, :], outer)
        wide = chances.astype(F32)
        inner = jnp.sum(wide * grads, axis=0, keepdims=True)
        scores = (wide * (grads - inner)).astype(BF16)
        r.grad_projected_t[value_rows, :] = dot_nt(outer, chances).astype(BF16)
        for target, grad in (
            (rows, dot_nn(r.turned_t[key_rows, :], scores)),
            (key_rows, dot_nt(r.turned_t[rows, :], scores)),
        ):
            unit, scale = head_norm(r.projected_t[target, :].astype(F32))
            outer_turned = turn_back(grad, r)
            weighted = outer_turned * unit
            lanes = weighted.shape[1] // 128
            folded = weighted[:, 0:128]
            for lane in range(1, lanes):
                folded = folded + weighted[:, lane * 128 : (lane + 1) * 128]
            r.head_gain_sums[target, :] = folded
            inner_turned = outer_turned * r.head_gain[target, 0:1]
            first = jnp.mean(inner_turned, axis=0, keepdims=True)
            second = jnp.mean(inner_turned * unit, axis=0, keepdims=True)
            r.grad_projected_t[target, :] = (scale * (inner_turned - first - unit * second)).astype(BF16)

    loop(H, heads)


def split3(block):
    high = block.astype(BF16)
    rest = block - high.astype(F32)
    middle = rest.astype(BF16)
    return high, middle, (rest - middle.astype(F32)).astype(BF16)


def backward_inputs(r):
    width = r.tokens.shape[1]
    ones = r.ones[:, 0:128]
    sums = sum(dot_nt(ones, part)[0:1] for part in split3(r.head_gain_sums[...]))
    r.grad_small[QUERY_GAIN : QUERY_GAIN + 1, :] = sums[:, :width]
    r.grad_small[KEY_GAIN : KEY_GAIN + 1, :] = sums[:, width:]
    r.grad_qkv_bias[0:1, :] = dot_nt(r.ones[...], r.grad_projected_t[...])[0:1]

    def hidden(index):
        rows = tile_at(index)
        r.grad_hidden[:, rows] = jnp.transpose(dot_nn(r.w_qkv[rows, :], r.grad_projected_t[...]))

    loop(width // TILE, hidden)

    def weight(index):
        cols = tile_at(index)
        r.w_qkv[:, cols] = dot_nt(r.hidden_pre_t[...], r.grad_projected_t[cols, :]).astype(BF16)

    loop(3 * width // TILE, weight)

    def store(where, value):
        r.grad_result[where, :] = value.astype(BF16)

    gain, bias = norm_rows_back(r.tokens, r.grad_hidden, r.grad_middle, r.small[PRE_GAIN : PRE_GAIN + 1, :], store)
    r.grad_small[PRE_GAIN : PRE_GAIN + 1, :] = gain
    r.grad_small[PRE_BIAS : PRE_BIAS + 1, :] = bias


class Refs:
    pass

MESH = pl.DeviceIdType.MESH
GROUPS = ("w_qkv", "w_out", "w_up", "w_down")
LINE = 4


class Place:
    def __init__(self):
        seq, fsdp = lax.axis_index("seq"), lax.axis_index("fsdp")
        self.seq, self.fsdp = seq, fsdp
        self.x, self.c = seq // 2, seq % 2
        self.z, self.y = fsdp // 2, fsdp % 2
        x, c, z, y = self.x, self.c, self.z, self.y
        self.to = dict(
            core=(2 * x + 1 - c, fsdp),
            x=(2 * (1 - x) + c, fsdp),
            y=(seq, 2 * z + 1 - y),
            up=(seq, fsdp + 2),
            down=(seq, fsdp - 2),
        )
        high = z // 2
        low = z + high * (LINE - 1 - 2 * z)
        self.line = [z]
        for i in range(LINE - 1):
            other = (i + 1) - (low if i == 0 else 0)
            self.line.append(other + high * (LINE - 1 - 2 * other))


def push(source, target, to, send_sem, recv_sem):
    return pltpu.make_async_remote_copy(
        src_ref=source, dst_ref=target, send_sem=send_sem, recv_sem=recv_sem, device_id=to, device_id_type=MESH
    )


class Gather:
    def __init__(self, r, place, over_y):
        self.r, self.p, self.over_y = r, place, over_y
        self.sends = {g: [] for g in range(len(GROUPS))}
        self.queue = []
        self.rest = {}
        for g in range(len(GROUPS)):
            self.rest[g] = [functools.partial(self.from_core, g, kind, o) for kind, o in self.kinds()]
        n = LINE
        zs = lambda g, *i: [functools.partial(self.from_line, g, k) for k in i]
        xs = lambda g, *i: [functools.partial(self.from_x, g, k) for k in i]
        ys = lambda g, *i: [functools.partial(self.from_y, g, k) for k in i]
        ds = lambda g, *i: [functools.partial(self.from_corner, g, k) for k in i]
        own = lambda g: [functools.partial(self.own, g)]
        early = lambda g: zs(g, 1) + ys(g, 0) + zs(g, 2) + xs(g, 1) + ys(g, 1) + zs(g, 3)
        late = lambda g: xs(g, 2) + ys(g, 2) + ds(g, 0, 1) + xs(g, 3) + ys(g, 3) + ds(g, 2, 3)
        self.queue = own(0) + early(0) + own(1) + late(0) + [0]
        self.queue += early(1) + own(2) + late(1) + [1]
        self.queue += early(2) + own(3) + late(2) + [2]
        self.queue += early(3) + late(3) + [3]

    def kinds(self):
        return [("z", o) for o in (1, 2, 3)] + [(k, o) for k in ("y", "x", "d") for o in range(LINE) if (k, o) != ("x", 0)]

    def advance(self, count):
        while count and self.queue:
            item = self.queue.pop(0)
            if not isinstance(item, int):
                item()
                count -= 1

    def finish(self, g):
        while self.queue:
            item = self.queue.pop(0)
            if isinstance(item, int):
                if item == g:
                    break
            else:
                item()
        for item in self.rest[g]:
            item()

    def piece(self, g, z, y, h, c):
        ref = getattr(self.r, GROUPS[g])
        shard, cols = ref.shape[0] // (2 * LINE), ref.shape[1] // 2
        rows = shard // 2
        first = pl.multiple_of((z * 2 + y) * shard + h * rows, 16)
        return ref.at[pl.ds(first, rows), pl.ds(pl.multiple_of(c * cols, 128), cols)]

    def ident(self, z, y, h):
        return (z * 2 + y) * 2 + h

    def start(self, g, kind, o, when, to, z, y, h, recv):
        slot = dict(up=0, down=4, x1=8, y1=12, x2=16, y2=20, cz=24, cx=28, cy=32, cd=36)[kind] + o
        piece = self.piece(g, z, y, h, self.p.c)
        copy = push(piece, piece, self.p.to[to], self.r.gather_send.at[g, slot], recv.at[g, self.ident(z, y, h)])
        self.sends[g].append((when, copy))
        if when is None:
            copy.start()
        else:
            pl.when(when)(copy.start)

    def wait(self, g, z, y, h, c, recv):
        piece = self.piece(g, z, y, h, c)
        push(piece, piece, self.p.to["core"], self.r.gather_send.at[g, 0], recv.at[g, self.ident(z, y, h)]).wait_recv()

    def own(self, g):
        p, recv = self.p, self.r.gather_recv
        pltpu.make_async_copy(getattr(self.r, GROUPS[g] + "_in"), self.shard(g), self.r.local_sems.at[g]).wait()
        self.start(g, "up", 0, p.z < LINE - 1, "up", p.z, p.y, p.x, recv)
        self.start(g, "down", 0, p.z > 0, "down", p.z, p.y, p.x, recv)
        self.start(g, "y1", 0, None, "y", p.z, p.y, p.x, recv)
        if 0 in self.over_y[g]:
            self.start(g, "y2", 0, None, "y", p.z, p.y, 1 - p.x, recv)

    def shard(self, g):
        ref = getattr(self.r, GROUPS[g])
        rows = ref.shape[0] // (2 * LINE)
        return ref.at[pl.ds(pl.multiple_of(self.p.fsdp * rows, 16), rows), :]

    def from_line(self, g, o):
        p, recv = self.p, self.r.gather_recv
        z = p.line[o]
        self.wait(g, z, p.y, p.x, p.c, recv)
        self.start(g, "up", o, (z < p.z) & (p.z < LINE - 1), "up", z, p.y, p.x, recv)
        self.start(g, "down", o, (z > p.z) & (p.z > 0), "down", z, p.y, p.x, recv)
        self.start(g, "x1", o, None, "x", z, p.y, p.x, recv)
        self.start(g, "y1", o, None, "y", z, p.y, p.x, recv)
        self.start(g, "cz", o, None, "core", z, p.y, p.x, self.r.gather_core)

    def from_x(self, g, o):
        p, recv = self.p, self.r.gather_recv
        z = p.line[o]
        self.wait(g, z, p.y, 1 - p.x, p.c, recv)
        if o in self.over_y[g]:
            self.start(g, "y2", o, None, "y", z, p.y, 1 - p.x, recv)
        self.start(g, "cx", o, None, "core", z, p.y, 1 - p.x, self.r.gather_core)

    def from_y(self, g, o):
        p, recv = self.p, self.r.gather_recv
        z = p.line[o]
        self.wait(g, z, 1 - p.y, p.x, p.c, recv)
        if o not in self.over_y[g]:
            self.start(g, "x2", o, None, "x", z, 1 - p.y, p.x, recv)
        self.start(g, "cy", o, None, "core", z, 1 - p.y, p.x, self.r.gather_core)

    def from_corner(self, g, o):
        p = self.p
        z = p.line[o]
        self.wait(g, z, 1 - p.y, 1 - p.x, p.c, self.r.gather_recv)
        self.start(g, "cd", o, None, "core", z, 1 - p.y, 1 - p.x, self.r.gather_core)

    def from_core(self, g, kind, o):
        p = self.p
        y = p.y if kind in "zx" else 1 - p.y
        h = p.x if kind in "zy" else 1 - p.x
        self.wait(g, p.line[o], y, h, 1 - p.c, self.r.gather_core)

    def sent(self, g):
        for when, copy in self.sends[g]:
            if when is None:
                copy.wait_send()
            else:
                pl.when(when)(copy.wait_send)


def greet(place):
    barrier = pltpu.get_barrier_semaphore()
    seq, fsdp = place.seq, place.fsdp
    peers = 2 * LINE

    def others(k, carry):
        pl.semaphore_signal(barrier, inc=1, device_id=(seq, (fsdp + k) % peers), device_id_type=MESH)
        return carry

    lax.fori_loop(1, peers, others, 0)
    for to in ("x", "core"):
        pl.semaphore_signal(barrier, inc=1, device_id=place.to[to], device_id_type=MESH)
    pl.semaphore_wait(barrier, peers + 1)


def small_send(r, place, k):
    peers = 2 * LINE
    other = (place.fsdp + k) % peers
    return push(
        r.packed_in, r.packed.at[place.fsdp], (place.seq, other), r.small_send.at[k], r.small_recv.at[place.fsdp]
    )


def small_start(r, place):
    lax.fori_loop(1, 2 * LINE, lambda k, carry: (small_send(r, place, k).start(), carry)[1], 0)
    r.packed[place.fsdp] = r.packed_in[...]


def small_finish(r, place):
    def receive(k, carry):
        other = (place.fsdp + k) % (2 * LINE)
        push(
            r.packed_in, r.packed.at[other], (place.seq, other), r.small_send.at[k], r.small_recv.at[other]
        ).wait_recv()
        small_send(r, place, k).wait_send()
        return carry

    lax.fori_loop(1, 2 * LINE, receive, 0)
    part = r.tokens.shape[1] // (2 * LINE)
    for shard in range(2 * LINE):
        rows = r.packed[shard].astype(F32)
        for i in range(8):
            r.small[i : i + 1, shard * part : (shard + 1) * part] = rows[i : i + 1, 0:part]
        for i in range(3):
            first = (shard * 3 + i) * part
            r.qkv_bias[0:1, first : first + part] = rows[8 + i : 9 + i, 0:part]
        for i in range(4):
            first = (shard * 4 + i) * part
            r.up_bias[0:1, first : first + part] = rows[11 + i : 12 + i, 0:part]


class Exchange:
    def __init__(self, r, place, source, target, index):
        self.p, self.target = place, target
        rows = target.shape[0] // 4
        p = place

        def quarter(x, c):
            return target.at[pl.ds(pl.multiple_of((2 * x + c) * rows, 16), rows), :]

        self.keep = pltpu.make_async_copy(source.at[p.x], quarter(p.x, p.c), r.local_sems.at[4 + index])
        send, recv = r.rows_send, r.rows_recv
        self.along_x = push(source.at[1 - p.x], quarter(p.x, p.c), p.to["x"], send.at[index, 0], recv.at[index, 0])
        self.own = push(source.at[p.x], quarter(p.x, p.c), p.to["core"], send.at[index, 1], recv.at[index, 1])
        passed = quarter(1 - p.x, p.c)
        self.passed = push(passed, passed, p.to["core"], send.at[index, 2], recv.at[index, 2])
        there = quarter(1 - p.x, p.c)
        self.arrive_x = push(there, there, p.to["x"], send.at[index, 0], recv.at[index, 0])
        one, two = quarter(p.x, 1 - p.c), quarter(1 - p.x, 1 - p.c)
        self.arrive = [
            push(one, one, p.to["core"], send.at[index, 1], recv.at[index, 1]),
            push(two, two, p.to["core"], send.at[index, 2], recv.at[index, 2]),
        ]

    def start(self):
        self.keep.start()
        self.along_x.start()
        self.own.start()

    def forward(self):
        self.arrive_x.wait_recv()
        self.passed.start()

    def finish(self):
        self.keep.wait()
        for copy in self.arrive:
            copy.wait_recv()
        for copy in (self.along_x, self.own, self.passed):
            copy.wait_send()


def collect_meta(r, place):
    r.meta_rows[...] = jnp.zeros(r.meta_rows.shape, F32)
    r.meta_rows[0:1, :] = r.segments[pl.ds(place.x, 1), :].astype(F32)
    for axis in range(2):
        r.meta_rows[1 + axis : 2 + axis, :] = r.positions[axis, pl.ds(place.x, 1), :].astype(F32)
    r.meta[...] = r.meta_rows[...].astype(BF16)


WEIGHTS = ("w_qkv", "w_out", "w_up", "w_down")


class Whole:
    def __init__(self, r):
        self.copies = [
            pltpu.make_async_copy(getattr(r, name + "_in"), getattr(r, name), r.local_sems.at[i])
            for i, name in enumerate(WEIGHTS)
        ]
        for copy in self.copies:
            copy.start()

    def advance(self, count):
        pass

    def finish(self, g):
        self.copies[g].wait()

    def sent(self, g):
        pass


def spread_head_gains(r):
    width = r.tokens.shape[1]
    columns = jnp.transpose(r.small[...])
    r.head_gain[0:width, :] = columns[:, QUERY_GAIN : QUERY_GAIN + 1]
    r.head_gain[width : 2 * width, :] = columns[:, KEY_GAIN : KEY_GAIN + 1]


def run_layer(r, gather, arrive_cotangent):
    rope_tables(r)
    forward_attention(r, gather)
    gather.finish(1)
    forward_middle(r)
    gather.finish(2)
    arrive_cotangent()
    forward_up(r, gather)
    gather.finish(3)
    forward_down(r)
    gather.sent(3)
    backward_down(r)
    gather.sent(2)
    backward_up(r)
    gather.sent(1)
    backward_middle(r)
    backward_attention(r)
    gather.sent(0)
    backward_inputs(r)
    back = [
        pltpu.make_async_copy(getattr(r, name), getattr(r, name + "_grad"), r.local_sems.at[i])
        for i, name in enumerate(WEIGHTS)
    ]
    for copy in back:
        copy.start()
    for copy in back:
        copy.wait()


def place_rows(r, source, target):
    target[...] = dot_nn(r.place[...], source[...]).astype(BF16)


def whole_kernel(names, *refs):
    r = Refs()
    for name, ref in zip(names, refs, strict=True):
        setattr(r, name, ref)
    gather = Whole(r)
    r.ones[...] = jnp.ones(r.ones.shape, BF16)
    place_tokens(r)
    place_rows(r, r.seq_tokens, r.tokens)
    spread_head_gains(r)
    run_layer(r, gather, lambda: place_rows(r, r.seq_cotangent, r.cotangent))


def fused_kernel(names, *refs):
    r = Refs()
    for name, ref in zip(names, refs, strict=True):
        setattr(r, name, ref)
    place = Place()
    gather = Gather(r, place, {0: (0, 1), 1: (0,), 2: (0, 1), 3: (0,)})
    for g, name in enumerate(WEIGHTS):
        pltpu.make_async_copy(getattr(r, name + "_in"), gather.shard(g), r.local_sems.at[g]).start()
    tokens = Exchange(r, place, r.tokens_in, r.seq_tokens, 0)
    cotangent = Exchange(r, place, r.cotangent_in, r.seq_cotangent, 1)
    greet(place)
    gather.advance(1)
    tokens.start()
    small_start(r, place)
    r.ones[...] = jnp.ones(r.ones.shape, BF16)
    collect_meta(r, place)
    place_tokens(r)
    gather.advance(2)
    tokens.forward()
    gather.advance(2)
    small_finish(r, place)
    spread_head_gains(r)
    gather.advance(2)
    tokens.finish()
    place_rows(r, r.seq_tokens, r.tokens)
    gather.advance(4)
    cotangent.start()

    def arrive_cotangent():
        cotangent.forward()
        cotangent.finish()
        place_rows(r, r.seq_cotangent, r.cotangent)

    run_layer(r, gather, arrive_cotangent)


def layer(fused, tokens, cotangent, segments, positions, small, qkv_bias, up_bias, *weights):
    peers = 2 * LINE
    scale = peers if fused else 1
    width = tokens.shape[-1]
    length = segments.shape[1]
    bundle = length // 2
    hidden = weights[2].shape[1]
    shape = jax.ShapeDtypeStruct
    vmem = pl.BlockSpec(memory_space=pltpu.VMEM)
    hbm = pl.BlockSpec(memory_space=pl.ANY)
    inputs = {}
    if fused:
        inputs.update(
            tokens_in=(tokens, hbm),
            cotangent_in=(cotangent, hbm),
            segments=(segments, vmem),
            positions=(positions, vmem),
            packed_in=(small, vmem),
        )
    else:
        inputs.update(
            seq_tokens=(tokens, vmem),
            seq_cotangent=(cotangent, vmem),
            meta=(segments, vmem),
            small=(small, vmem),
            qkv_bias=(qkv_bias, vmem),
            up_bias=(up_bias, vmem),
        )
    full = [(w.shape[0] * scale, w.shape[1]) for w in weights]
    for name, w in zip(WEIGHTS, weights):
        inputs[name + "_in"] = (w, hbm)
    outputs = dict(
        result=(shape((bundle, width), BF16), vmem),
        grad_result=(shape((bundle, width), BF16), vmem),
        grad_small=(shape((8, width), F32), vmem),
        grad_qkv_bias=(shape((8, 3 * width), F32), vmem),
        grad_up_bias=(shape((8, hidden), F32), vmem),
    )
    scratch = {}
    for name, size in zip(WEIGHTS, full):
        outputs[name + "_grad"] = (shape(size, BF16), hbm)
        scratch[name] = pltpu.VMEM(size, BF16)
    if fused:
        groups, pieces = len(WEIGHTS), 2 * peers
        scratch.update(
            seq_tokens=pltpu.VMEM((length, width), BF16),
            seq_cotangent=pltpu.VMEM((length, width), BF16),
            meta_rows=pltpu.VMEM((8, length), F32),
            meta=pltpu.VMEM((8, length), BF16),
            packed=pltpu.VMEM((peers, 16, 128), BF16),
            small=pltpu.VMEM((8, width), F32),
            qkv_bias=pltpu.VMEM((1, 3 * width), F32),
            up_bias=pltpu.VMEM((1, hidden), F32),
            small_send=pltpu.SemaphoreType.DMA((peers,)),
            small_recv=pltpu.SemaphoreType.DMA((peers,)),
            rows_send=pltpu.SemaphoreType.DMA((2, 3)),
            rows_recv=pltpu.SemaphoreType.DMA((2, 3)),
            gather_send=pltpu.SemaphoreType.DMA((groups, 40)),
            gather_recv=pltpu.SemaphoreType.DMA((groups, pieces)),
            gather_core=pltpu.SemaphoreType.DMA((groups, pieces)),
        )
    scratch.update(
        local_sems=pltpu.SemaphoreType.DMA((8,)),
        ones=pltpu.VMEM((8, bundle), BF16),
        start=pltpu.VMEM((8, 128), F32),
        place=pltpu.VMEM((bundle, length), BF16),
        marks_row=pltpu.VMEM((8, bundle), F32),
        marks_col=pltpu.VMEM((bundle, 8), F32),
        cosine=pltpu.VMEM((2, HD // 4, bundle), F32),
        sine=pltpu.VMEM((2, HD // 4, bundle), F32),
        head_gain=pltpu.VMEM((2 * width, 1), F32),
        head_gain_sums=pltpu.VMEM((2 * width, 128), F32),
        tokens=pltpu.VMEM((bundle, width), BF16),
        cotangent=pltpu.VMEM((bundle, width), BF16),
        hidden_pre=pltpu.VMEM((bundle, width), BF16),
        hidden_pre_t=pltpu.VMEM((width, bundle), BF16),
        projected_t=pltpu.VMEM((3 * width, bundle), BF16),
        turned_t=pltpu.VMEM((2 * width, bundle), BF16),
        chances=pltpu.VMEM((H * bundle, bundle), BF16),
        attended_t=pltpu.VMEM((width, bundle), BF16),
        attended=pltpu.VMEM((bundle, width), BF16),
        middle=pltpu.VMEM((bundle, width), F32),
        hidden_mlp=pltpu.VMEM((bundle, width), BF16),
        hidden_mlp_t=pltpu.VMEM((width, bundle), BF16),
        before=pltpu.VMEM((bundle, TILE), F32),
        active=pltpu.VMEM((bundle, hidden), BF16),
        active_t=pltpu.VMEM((hidden, bundle), BF16),
        slope=pltpu.VMEM((bundle, hidden), BF16),
        grad_hidden=pltpu.VMEM((bundle, width), F32),
        grad_middle=pltpu.VMEM((bundle, width), F32),
        grad_branch=pltpu.VMEM((bundle, width), BF16),
        grad_attended_t=pltpu.VMEM((width, bundle), BF16),
        grad_projected_t=pltpu.VMEM((3 * width, bundle), BF16),
    )
    names = tuple(inputs) + tuple(outputs) + tuple(scratch)
    params = dict(vmem_limit_bytes=62 << 20)
    if fused:
        params.update(collective_id=0, has_side_effects=True)
    return pl.pallas_call(
        functools.partial(fused_kernel if fused else whole_kernel, names),
        out_shape=tuple(o[0] for o in outputs.values()),
        in_specs=[i[1] for i in inputs.values()],
        out_specs=tuple(o[1] for o in outputs.values()),
        scratch_shapes=list(scratch.values()),
        compiler_params=pltpu.CompilerParams(**params),
        name="layer",
    )(*(i[0] for i in inputs.values()))


def shards(
    tokens,
    pre_gain,
    pre_bias,
    query_key_value_weight,
    query_key_value_bias,
    query_gain,
    key_gain,
    output_weight,
    output_bias,
    mlp_gain,
    mlp_bias,
    up_matrix_weight,
    up_offset_bias,
    down_matrix_weight,
    down_offset_bias,
    segments,
    positions,
    cotangent,
):
    rank = lax.axis_index("seq")
    x = rank // 2
    width = tokens.shape[2]
    length = segments.shape[1]
    fsdp = lax.axis_size("fsdp")
    part = width // fsdp
    weights_in = (query_key_value_weight, output_weight, up_matrix_weight, down_matrix_weight)
    vectors = (
        pre_gain, pre_bias, query_gain, key_gain, output_bias, mlp_gain, mlp_bias, down_offset_bias,
        query_key_value_bias, up_offset_bias,
    )
    if fsdp == 2 * LINE:
        packed = jnp.concatenate(vectors).reshape(-1, part)
        packed = jnp.pad(packed, ((0, 16 - packed.shape[0]), (0, 128 - part)))
        results = layer(True, tokens, cotangent, segments, positions, packed, None, None, *weights_in)
    else:
        gather = functools.partial(lax.all_gather, axis_name="fsdp", axis=0, tiled=True)
        packed = gather(jnp.concatenate(vectors)[None]).astype(F32)
        small = jnp.stack([packed[:, i * part : (i + 1) * part].reshape(width) for i in range(8)])
        qkv_bias = packed[:, 8 * part : 11 * part].reshape(1, 3 * width)
        up_bias = packed[:, 11 * part :].reshape(1, -1)
        seq_tokens = lax.dynamic_index_in_dim(lax.all_gather(tokens, "seq", axis=1, tiled=True), x, 0, False)
        seq_cotangent = lax.dynamic_index_in_dim(lax.all_gather(cotangent, "seq", axis=1, tiled=True), x, 0, False)
        labels = lax.dynamic_index_in_dim(segments, x, 0, True)
        places = lax.dynamic_index_in_dim(positions, x, 1, False)
        meta = jnp.concatenate([labels, places, jnp.zeros((5, length), jnp.int32)], axis=0).astype(BF16)
        results = layer(False, seq_tokens, seq_cotangent, meta, None, small, qkv_bias, up_bias, *map(gather, weights_in))
    result, grad_result, grad_small, grad_qkv_bias, grad_up_bias, *weight_grads = results
    counts = jnp.stack([jnp.sum(segments == v, axis=1) for v in range(4)])
    first = jnp.argmax(counts == length // 2, axis=0)
    starts = jnp.sum(segments < first[:, None], axis=1)

    def home(bundle):
        every = lax.all_gather(bundle, "seq").reshape(2, length, width)
        own = rank * (length // 4) + jnp.arange(length // 4)
        index = (own[None] - starts[:, None]) % length
        return jnp.take_along_axis(every, index[..., None], axis=1)

    scatter = functools.partial(lax.psum_scatter, axis_name="fsdp", scatter_dimension=0, tiled=True)

    def finish(grad):
        return lax.psum(scatter(grad).astype(BF16), "seq").astype(F32)

    weights = [finish(g) for g in weight_grads]
    pieces = [grad_small[i].reshape(fsdp, part) for i in range(8)]
    pieces += [grad_qkv_bias[0, : 2 * width].reshape(fsdp, -1), grad_qkv_bias[0, 2 * width :].reshape(fsdp, -1)]
    pieces += [grad_up_bias[0].reshape(fsdp, -1)]
    total = lax.psum(scatter(jnp.concatenate(pieces, axis=1)), "seq")[0]
    s = [total[i * part : (i + 1) * part] for i in range(8)]
    query_key_bias, value_bias, up_total = total[8 * part : 10 * part], total[10 * part : 11 * part], total[11 * part :]
    return (
        home(result), home(grad_result), s[PRE_GAIN], s[PRE_BIAS], weights[0], query_key_bias, value_bias,
        s[QUERY_GAIN], s[KEY_GAIN], weights[1], s[OUT_BIAS], s[MLP_GAIN], s[MLP_BIAS], weights[2], up_total,
        weights[3], s[DOWN_BIAS],
    )


def solution(mesh):
    rows, matrix, activations = P("fsdp"), P("fsdp", None), P("fsdp", "seq", None)
    placed = (
        activations, rows, rows, matrix, rows, rows, rows, matrix, rows, rows, rows, matrix, rows, matrix, rows,
        P("fsdp", None), P(None, "fsdp", None), activations,
    )
    given = (
        activations, activations, rows, rows, matrix, rows, rows, rows, rows, matrix, rows, rows, rows, matrix, rows,
        matrix, rows,
    )
    return jax.shard_map(shards, mesh=mesh, in_specs=placed, out_specs=given, check_vma=False)
```

```python
import functools

import jax
import jax.numpy as jnp
from jax import lax
from jax.experimental import pallas as pl
from jax.experimental.pallas import tpu as pltpu
from jax.sharding import PartitionSpec as P

H = 12
HD = 64
EPSILON = 1e-06
NEGATIVE = -1e30
ROPE_BASE = 100.0
F32 = jnp.float32
BF16 = jnp.bfloat16
TILE = 256


def dot_nn(a, b):
    return lax.dot_general(a, b, (((1,), (0,)), ((), ())), preferred_element_type=F32)


def dot_nt(a, b):
    return lax.dot_general(a, b, (((1,), (1,)), ((), ())), preferred_element_type=F32)


def dot_tn(a, b):
    return lax.dot_general(a, b, (((0,), (0,)), ((), ())), preferred_element_type=F32)


def tile_at(index, size=TILE):
    return pl.ds(pl.multiple_of(index * size, size), size)


def loop(count, body, first=0):
    def step(index, carry):
        body(index)
        return carry

    lax.fori_loop(first, first + count, step, 0)


def loop_beside(count, body, gather, parts, steps):
    for part in range(parts):
        loop(count // parts, body, part * (count // parts))
        gather.advance(steps)


def rows_sum(block):
    rows, width = block.shape
    return jnp.sum(block.reshape(rows // 8, 8, width), axis=0)


def column_sums_exact(ones, block):
    return dot_nn(ones, block)[0:1]


def place_tokens(r):
    bundle, length = r.place.shape
    labels = r.meta[0:1, :].astype(F32)
    start = jnp.zeros((1, 1), F32)
    found = jnp.zeros((1, 1), F32)
    for value in range(4):
        here = jnp.sum(jnp.where(labels == value, 1.0, 0.0), axis=1, keepdims=True)
        below = jnp.sum(jnp.where(labels < value, 1.0, 0.0), axis=1, keepdims=True)
        hit = jnp.where(here == bundle, 1.0, 0.0) * (1.0 - found)
        start = start + hit * below
        found = found + hit
    r.start[...] = jnp.broadcast_to(start, r.start.shape)
    core = lax.axis_index("seq") % 2

    def block(index):
        rows = tile_at(index, 128)
        shape = (128, length)
        mine = lax.broadcasted_iota(jnp.int32, shape, 0) + (index * 128 + core * bundle)
        target = mine.astype(F32) + start
        target = jnp.where(target >= length, target - length, target)
        source = lax.broadcasted_iota(jnp.int32, shape, 1).astype(F32)
        r.place[rows, :] = jnp.where(source == target, 1.0, 0.0).astype(BF16)

    loop(bundle // 128, block)
    r.marks_row[...] = dot_nt(r.meta[...], r.place[...])
    r.marks_col[...] = dot_nt(r.place[...], r.meta[...])


def rope_tables(r):
    quarter = HD // 4
    bundle = r.cosine.shape[-1]
    step = lax.broadcasted_iota(jnp.int32, (quarter, bundle), 0).astype(F32)
    frequency = jnp.exp(step * (-jnp.log(jnp.float32(ROPE_BASE)) / quarter))
    for axis in range(2):
        angle = r.marks_row[1 + axis : 2 + axis, :] * frequency
        r.cosine[axis] = jnp.cos(angle)
        r.sine[axis] = jnp.sin(angle)


def normalized(block):
    mean = jnp.mean(block, axis=-1, keepdims=True)
    centred = block - mean
    scale = lax.rsqrt(jnp.mean(centred * centred, axis=-1, keepdims=True) + EPSILON)
    return centred * scale, scale


def norm_rows(source, gain, bias, target, rows=32):
    def block(index):
        where = tile_at(index, rows)
        unit, _ = normalized(source[where, :].astype(F32))
        target[where, :] = (unit * gain + bias).astype(target.dtype)

    loop(source.shape[0] // rows, block)


def norm_rows_back(source, grads, base, gain, store, rows=32):
    width = source.shape[1]

    def block(index, carry):
        gain_sum, bias_sum = carry
        where = tile_at(index, rows)
        unit, scale = normalized(source[where, :].astype(F32))
        outer = grads[where, :]
        inner = outer * gain
        first = jnp.mean(inner, axis=-1, keepdims=True)
        second = jnp.mean(inner * unit, axis=-1, keepdims=True)
        store(where, base[where, :].astype(F32) + scale * (inner - first - unit * second))
        return gain_sum + rows_sum(outer * unit), bias_sum + rows_sum(outer)

    zero = jnp.zeros((8, width), F32)
    gain_sum, bias_sum = lax.fori_loop(0, source.shape[0] // rows, block, (zero, zero))
    return jnp.sum(gain_sum, axis=0, keepdims=True), jnp.sum(bias_sum, axis=0, keepdims=True)


def transpose_into(target, source):
    def block(index):
        where = tile_at(index, 128)
        target[where, :] = jnp.transpose(source[:, where])

    loop(source.shape[1] // 128, block)


def head_norm(vectors):
    mean = jnp.mean(vectors, axis=0, keepdims=True)
    centred = vectors - mean
    scale = lax.rsqrt(jnp.mean(centred * centred, axis=0, keepdims=True) + EPSILON)
    return centred * scale, scale


def turn(vectors, r):
    q = HD // 4
    out = []
    for axis in range(2):
        one, two = vectors[2 * axis * q : (2 * axis + 1) * q], vectors[(2 * axis + 1) * q : (2 * axis + 2) * q]
        cosine, sine = r.cosine[axis], r.sine[axis]
        out.append(one * cosine - two * sine)
        out.append(two * cosine + one * sine)
    return jnp.concatenate(out, axis=0) * HD ** (-0.5)


def turn_back(vectors, r):
    q = HD // 4
    out = []
    for axis in range(2):
        one, two = vectors[2 * axis * q : (2 * axis + 1) * q], vectors[(2 * axis + 1) * q : (2 * axis + 2) * q]
        cosine, sine = r.cosine[axis], r.sine[axis]
        out.append(one * cosine + two * sine)
        out.append(two * cosine - one * sine)
    return jnp.concatenate(out, axis=0) * HD ** (-0.5)


PRE_GAIN, PRE_BIAS, QUERY_GAIN, KEY_GAIN, OUT_BIAS, MLP_GAIN, MLP_BIAS, DOWN_BIAS = range(8)


def gain_of(r, head):
    lanes = lax.broadcasted_iota(jnp.int32, (HD, 128), 1)
    return jnp.sum(jnp.where(lanes == head, r.head_gain[...], 0.0), axis=1, keepdims=True)


def spill(r, index):
    return pltpu.make_async_copy(r.chances.at[index % 2], r.chances_kept.at[index], r.chance_sems.at[index % 2])


def fetch(r, index):
    return pltpu.make_async_copy(r.chances_kept.at[index], r.chances.at[index % 2], r.chance_sems.at[index % 2])


def forward_attention(r, gather):
    width = r.tokens.shape[1]
    norm_rows(r.tokens, r.small[PRE_GAIN : PRE_GAIN + 1, :], r.small[PRE_BIAS : PRE_BIAS + 1, :], r.rows)
    transpose_into(r.hidden_pre_t, r.rows)
    gather.finish(0)

    def project(index):
        cols = tile_at(index)
        part = dot_nn(r.rows[...], r.w_qkv[:, cols]) + r.qkv_bias[0:1, cols]
        r.projected_t[cols, :] = jnp.transpose(part.astype(BF16))

    loop_beside(3 * width // TILE, project, gather, 3, 2)

    def prepare(index):
        rows = tile_at(index, HD)
        unit, _ = head_norm(r.projected_t[rows, :].astype(F32))
        r.turned_t[rows, :] = turn(unit * gain_of(r, index), r).astype(BF16)

    loop_beside(2 * H, prepare, gather, 2, 2)

    def attend(index):
        rows = tile_at(index, HD)
        key_rows = tile_at(index + H, HD)
        value_rows = tile_at(index + 2 * H, HD)
        slot = index % 2

        @pl.when(index >= 2)
        def _():
            spill(r, index - 2).wait()

        scores = dot_tn(r.turned_t[key_rows, :], r.turned_t[rows, :])
        scores = jnp.where(r.marks_col[:, 0:1] == r.marks_row[0:1, :], scores, NEGATIVE)
        raised = jnp.exp(scores - jnp.max(scores, axis=0, keepdims=True))
        chances = (raised * (1.0 / jnp.sum(raised, axis=0, keepdims=True))).astype(BF16)
        r.chances[slot] = chances
        spill(r, index).start()
        r.attended_t[rows, :] = dot_nn(r.projected_t[value_rows, :], chances).astype(BF16)

    loop_beside(H, attend, gather, 6, 3)
    for index in (H - 2, H - 1):
        spill(r, index).wait()
    transpose_into_rows(r.rows, r.attended_t)


def transpose_into_rows(target, source):
    def block(index):
        where = tile_at(index, 128)
        target[:, where] = jnp.transpose(source[where, :])

    loop(source.shape[0] // 128, block)


def forward_middle(r):
    width = r.tokens.shape[1]

    def branch(index):
        cols = tile_at(index)
        part = dot_nn(r.rows[...], r.w_out[:, cols]) + r.small[OUT_BIAS : OUT_BIAS + 1, cols]
        r.middle[:, cols] = r.tokens[:, cols].astype(F32) + part

    loop(width // TILE, branch)
    norm_rows(r.middle, r.small[MLP_GAIN : MLP_GAIN + 1, :], r.small[MLP_BIAS : MLP_BIAS + 1, :], r.rows)
    transpose_into(r.hidden_mlp_t, r.rows)


def forward_up(r, gather):
    hidden = r.w_up.shape[1]

    def up(index):
        cols = tile_at(index)
        r.before[...] = dot_nn(r.rows[...], r.w_up[:, cols]) + r.up_bias[0:1, cols]

        def activate(part):
            rows = tile_at(part, 64)
            v = r.before[rows, :]
            half = 0.5 + 0.5 * lax.erf(v * 0.7071067811865476)
            r.active[rows, cols] = (v * half).astype(BF16)
            r.slope[rows, cols] = (half + v * (jnp.exp(-0.5 * v * v) * 0.3989422804014327)).astype(BF16)

        loop(r.before.shape[0] // 64, activate)
        r.active_t[cols, :] = jnp.transpose(r.active[:, cols])

    loop_beside(hidden // TILE, up, gather, 4, 3)


def forward_down(r):
    def down(index):
        cols = tile_at(index)
        part = dot_nn(r.active[...], r.w_down[:, cols]) + r.small[DOWN_BIAS : DOWN_BIAS + 1, cols]
        r.result_rows[:, cols] = (r.middle[:, cols] + part).astype(BF16)

    loop(r.w_down.shape[1] // TILE, down)


def backward_down(r):
    r.grad_small[DOWN_BIAS : DOWN_BIAS + 1, :] = column_sums_exact(r.ones[...], r.cotangent[...])

    def down(index):
        rows = tile_at(index)
        grads = dot_nt(r.cotangent[...], r.w_down[rows, :])
        before = (grads * r.slope[:, rows].astype(F32)).astype(BF16)
        r.slope[:, rows] = before
        r.grad_up_bias[0:1, rows] = column_sums_exact(r.ones[...], before)
        r.w_down[rows, :] = dot_nn(r.active_t[rows, :], r.cotangent[...]).astype(BF16)

    loop(r.w_down.shape[0] // TILE, down)


def backward_up(r, reduce):
    def hidden(index):
        cols = tile_at(index)
        r.grad_hidden[:, cols] = dot_nt(r.slope[...], r.w_up[cols, :])

    loop_beside(r.w_up.shape[0] // TILE, hidden, reduce, 3, 2)

    def weight(index):
        cols = tile_at(index)
        r.w_up[:, cols] = dot_nn(r.hidden_mlp_t[...], r.slope[:, cols]).astype(BF16)

    loop_beside(r.w_up.shape[1] // TILE, weight, reduce, 3, 2)


def backward_middle(r, reduce):
    def store(where, value):
        r.middle[where, :] = value
        r.rows[where, :] = value.astype(BF16)

    gain, bias = norm_rows_back(r.middle, r.grad_hidden, r.cotangent, r.small[MLP_GAIN : MLP_GAIN + 1, :], store)
    r.grad_small[MLP_GAIN : MLP_GAIN + 1, :] = gain
    r.grad_small[MLP_BIAS : MLP_BIAS + 1, :] = bias
    r.grad_small[OUT_BIAS : OUT_BIAS + 1, :] = column_sums_exact(r.ones[...], r.rows[...])
    reduce.advance(2)

    def attended(index):
        rows = tile_at(index)
        r.grad_attended_t[rows, :] = dot_nt(r.w_out[rows, :], r.rows[...]).astype(BF16)
        r.w_out[rows, :] = dot_nn(r.attended_t[rows, :], r.rows[...]).astype(BF16)

    loop_beside(r.w_out.shape[0] // TILE, attended, reduce, 3, 1)


def backward_attention(r, reduce):
    def heads(index):
        rows = tile_at(index, HD)
        key_rows = tile_at(index + H, HD)
        value_rows = tile_at(index + 2 * H, HD)
        outer = r.grad_attended_t[rows, :]
        grads = dot_tn(r.projected_t[value_rows, :], outer)
        fetch(r, index).wait()
        chances = r.chances[index % 2]
        wide = chances.astype(F32)
        inner = jnp.sum(wide * grads, axis=0, keepdims=True)
        scores = (wide * (grads - inner)).astype(BF16)
        r.projected_t[value_rows, :] = dot_nt(outer, chances).astype(BF16)

        @pl.when(index + 2 < H)
        def _():
            fetch(r, index + 2).start()

        for head, target, grad in (
            (index, rows, dot_nn(r.turned_t[key_rows, :], scores)),
            (index + H, key_rows, dot_nt(r.turned_t[rows, :], scores)),
        ):
            unit, scale = head_norm(r.projected_t[target, :].astype(F32))
            outer_turned = turn_back(grad, r)
            weighted = outer_turned * unit
            total = jnp.sum(weighted, axis=1, keepdims=True)
            lanes = lax.broadcasted_iota(jnp.int32, (HD, 128), 1)
            r.head_gain_sums[...] += jnp.where(lanes == head, total, 0.0)
            inner_turned = outer_turned * gain_of(r, head)
            first = jnp.mean(inner_turned, axis=0, keepdims=True)
            second = jnp.mean(inner_turned * unit, axis=0, keepdims=True)
            r.projected_t[target, :] = (scale * (inner_turned - first - unit * second)).astype(BF16)

    loop_beside(H, heads, reduce, 6, 6)


def backward_heads_weight(r, reduce):
    width = r.tokens.shape[1]
    sums = jnp.transpose(r.head_gain_sums[...])
    for head in range(2 * H):
        row = QUERY_GAIN if head < H else KEY_GAIN
        first = head % H * HD
        r.grad_small[row : row + 1, first : first + HD] = sums[head : head + 1, :]
    r.grad_qkv_bias[0:1, :] = dot_nt(r.ones[...], r.projected_t[...])[0:1]

    def hidden(index):
        rows = tile_at(index)
        r.grad_hidden[:, rows] = jnp.transpose(dot_nn(r.w_qkv[rows, :], r.projected_t[...]))

    loop_beside(width // TILE, hidden, reduce, 3, 2)

    def weight(index):
        cols = tile_at(index)
        r.w_qkv[:, cols] = dot_nt(r.hidden_pre_t[...], r.projected_t[cols, :]).astype(BF16)

    loop_beside(3 * width // TILE, weight, reduce, 3, 2)


def backward_inputs(r):
    def store(where, value):
        r.grad_rows[where, :] = value.astype(BF16)

    gain, bias = norm_rows_back(r.tokens, r.grad_hidden, r.middle, r.small[PRE_GAIN : PRE_GAIN + 1, :], store)
    r.grad_small[PRE_GAIN : PRE_GAIN + 1, :] = gain
    r.grad_small[PRE_BIAS : PRE_BIAS + 1, :] = bias


class Refs:
    pass

MESH = pl.DeviceIdType.MESH
GROUPS = ("w_qkv", "w_out", "w_up", "w_down")
LINE = 4


class Place:
    def __init__(self):
        seq, fsdp = lax.axis_index("seq"), lax.axis_index("fsdp")
        self.seq, self.fsdp = seq, fsdp
        self.x, self.c = seq // 2, seq % 2
        self.z, self.y = fsdp // 2, fsdp % 2
        x, c, z, y = self.x, self.c, self.z, self.y
        self.to = dict(
            core=(2 * x + 1 - c, fsdp),
            x=(2 * (1 - x) + c, fsdp),
            y=(seq, 2 * z + 1 - y),
            up=(seq, fsdp + 2),
            down=(seq, fsdp - 2),
        )
        high = z // 2
        low = z + high * (LINE - 1 - 2 * z)
        self.line = [z]
        for i in range(LINE - 1):
            other = (i + 1) - (low if i == 0 else 0)
            self.line.append(other + high * (LINE - 1 - 2 * other))


def push(source, target, to, send_sem, recv_sem):
    return pltpu.make_async_remote_copy(
        src_ref=source, dst_ref=target, send_sem=send_sem, recv_sem=recv_sem, device_id=to, device_id_type=MESH
    )


class Gather:
    def __init__(self, r, place, over_y):
        self.r, self.p, self.over_y = r, place, over_y
        self.sends = {g: [] for g in range(len(GROUPS))}
        self.queue = []
        self.rest = {}
        for g in range(len(GROUPS)):
            self.rest[g] = [functools.partial(self.from_core, g, kind, o) for kind, o in self.kinds()]
        n = LINE
        zs = lambda g, *i: [functools.partial(self.from_line, g, k) for k in i]
        xs = lambda g, *i: [functools.partial(self.from_x, g, k) for k in i]
        ys = lambda g, *i: [functools.partial(self.from_y, g, k) for k in i]
        ds = lambda g, *i: [functools.partial(self.from_corner, g, k) for k in i]
        own = lambda g: [functools.partial(self.own, g)]
        early = lambda g: zs(g, 1) + ys(g, 0) + zs(g, 2) + xs(g, 1) + ys(g, 1) + zs(g, 3)
        late = lambda g: xs(g, 2) + ys(g, 2) + ds(g, 0, 1) + xs(g, 3) + ys(g, 3) + ds(g, 2, 3)
        self.queue = own(0) + early(0) + own(1) + late(0) + [0]
        self.queue += early(1) + own(2) + late(1) + [1]
        self.queue += early(2) + own(3) + late(2) + [2]
        self.queue += early(3) + late(3) + [3]

    def kinds(self):
        return [("z", o) for o in (1, 2, 3)] + [(k, o) for k in ("y", "x", "d") for o in range(LINE) if (k, o) != ("x", 0)]

    def advance(self, count):
        while count and self.queue:
            item = self.queue.pop(0)
            if not isinstance(item, int):
                item()
                count -= 1

    def finish(self, g):
        while self.queue:
            item = self.queue.pop(0)
            if isinstance(item, int):
                if item == g:
                    break
            else:
                item()
        for item in self.rest[g]:
            item()

    def piece(self, g, z, y, h, c):
        ref = getattr(self.r, GROUPS[g])
        shard, cols = ref.shape[0] // (2 * LINE), ref.shape[1] // 2
        rows = shard // 2
        first = pl.multiple_of((z * 2 + y) * shard + h * rows, 16)
        return ref.at[pl.ds(first, rows), pl.ds(pl.multiple_of(c * cols, 128), cols)]

    def ident(self, z, y, h):
        return (z * 2 + y) * 2 + h

    def start(self, g, kind, o, when, to, z, y, h, recv):
        slot = dict(up=0, down=4, x1=8, y1=12, x2=16, y2=20, cz=24, cx=28, cy=32, cd=36)[kind] + o
        piece = self.piece(g, z, y, h, self.p.c)
        copy = push(piece, piece, self.p.to[to], self.r.gather_send.at[g, slot], recv.at[g, self.ident(z, y, h)])
        self.sends[g].append((when, copy))
        if when is None:
            copy.start()
        else:
            pl.when(when)(copy.start)

    def wait(self, g, z, y, h, c, recv):
        piece = self.piece(g, z, y, h, c)
        push(piece, piece, self.p.to["core"], self.r.gather_send.at[g, 0], recv.at[g, self.ident(z, y, h)]).wait_recv()

    def own(self, g):
        p, recv = self.p, self.r.gather_recv
        pltpu.make_async_copy(getattr(self.r, GROUPS[g] + "_in"), self.shard(g), self.r.local_sems.at[g]).wait()
        self.start(g, "up", 0, p.z < LINE - 1, "up", p.z, p.y, p.x, recv)
        self.start(g, "down", 0, p.z > 0, "down", p.z, p.y, p.x, recv)
        self.start(g, "y1", 0, None, "y", p.z, p.y, p.x, recv)
        if 0 in self.over_y[g]:
            self.start(g, "y2", 0, None, "y", p.z, p.y, 1 - p.x, recv)

    def shard(self, g):
        ref = getattr(self.r, GROUPS[g])
        rows = ref.shape[0] // (2 * LINE)
        return ref.at[pl.ds(pl.multiple_of(self.p.fsdp * rows, 16), rows), :]

    def from_line(self, g, o):
        p, recv = self.p, self.r.gather_recv
        z = p.line[o]
        self.wait(g, z, p.y, p.x, p.c, recv)
        self.start(g, "up", o, (z < p.z) & (p.z < LINE - 1), "up", z, p.y, p.x, recv)
        self.start(g, "down", o, (z > p.z) & (p.z > 0), "down", z, p.y, p.x, recv)
        self.start(g, "x1", o, None, "x", z, p.y, p.x, recv)
        self.start(g, "y1", o, None, "y", z, p.y, p.x, recv)
        self.start(g, "cz", o, None, "core", z, p.y, p.x, self.r.gather_core)

    def from_x(self, g, o):
        p, recv = self.p, self.r.gather_recv
        z = p.line[o]
        self.wait(g, z, p.y, 1 - p.x, p.c, recv)
        if o in self.over_y[g]:
            self.start(g, "y2", o, None, "y", z, p.y, 1 - p.x, recv)
        self.start(g, "cx", o, None, "core", z, p.y, 1 - p.x, self.r.gather_core)

    def from_y(self, g, o):
        p, recv = self.p, self.r.gather_recv
        z = p.line[o]
        self.wait(g, z, 1 - p.y, p.x, p.c, recv)
        if o not in self.over_y[g]:
            self.start(g, "x2", o, None, "x", z, 1 - p.y, p.x, recv)
        self.start(g, "cy", o, None, "core", z, 1 - p.y, p.x, self.r.gather_core)

    def from_corner(self, g, o):
        p = self.p
        z = p.line[o]
        self.wait(g, z, 1 - p.y, 1 - p.x, p.c, self.r.gather_recv)
        self.start(g, "cd", o, None, "core", z, 1 - p.y, 1 - p.x, self.r.gather_core)

    def from_core(self, g, kind, o):
        p = self.p
        y = p.y if kind in "zx" else 1 - p.y
        h = p.x if kind in "zy" else 1 - p.x
        self.wait(g, p.line[o], y, h, 1 - p.c, self.r.gather_core)

    def sent(self, g):
        for when, copy in self.sends[g]:
            if when is None:
                copy.wait_send()
            else:
                pl.when(when)(copy.wait_send)


class Reduce:
    def __init__(self, r, place, over_y):
        self.r, self.p, self.over_y = r, place, over_y
        self.sends = []
        self.queue = []
        self.last = []

    def rows_of(self, g):
        ref = getattr(self.r, GROUPS[g])
        return ref.shape[0] // (4 * LINE)

    def piece(self, g, z, y, h):
        ref = getattr(self.r, GROUPS[g])
        rows, cols = self.rows_of(g), ref.shape[1] // 2
        first = pl.multiple_of(((z * 2 + y) * 2 + h) * rows, 16)
        return ref.at[pl.ds(first, rows), pl.ds(pl.multiple_of(self.p.c * cols, 128), cols)]

    def spot(self, kind, o):
        p = self.p
        y = p.y if kind in "ox" else 1 - p.y
        h = p.x if kind in "oy" else 1 - p.x
        return p.line[o], y, h

    def from_core(self, g, kind, o):
        z, y, h = self.spot(kind, o)
        rows = self.rows_of(g)
        return getattr(self.r, "core_" + GROUPS[g]).at[pl.ds(pl.multiple_of(((z * 2 + y) * 2 + h) * rows, 16), rows), :]

    def box(self, g, kind, slot):
        return getattr(self.r, "box_" + GROUPS[g]).at[dict(corner=0, x=4, y=8, line=12)[kind] + slot]

    def send(self, g, source, target, to, slot, when=None, recv=None):
        copy = push(
            source, target, self.p.to[to], self.r.reduce_send.at[g, slot], self.r.reduce_recv.at[g, slot if recv is None else recv]
        )
        self.sends.append((when, copy))
        if when is None:
            copy.start()
        else:
            pl.when(when)(copy.start)

    def arrive(self, g, target, slot):
        push(target, target, self.p.to["core"], self.r.reduce_send.at[g, 0], self.r.reduce_recv.at[g, slot]).wait_recv()

    def add(self, target, *others):
        total = target[...].astype(F32)
        for other in others:
            total = total + other[...].astype(F32)
        target[...] = total.astype(BF16)

    def begin(self, g):
        ref = getattr(self.r, GROUPS[g])
        rows, cols = self.rows_of(g), ref.shape[1] // 2
        far = (3, 2, 1, 0)
        base = dict(d=0, y=4, x=8, o=12)
        for kind in "dyxo":
            for o in far:
                z, y, h = self.spot(kind, o)
                first = pl.multiple_of(((z * 2 + y) * 2 + h) * rows, 16)
                other = pl.multiple_of((1 - self.p.c) * cols, 128)
                self.send(g, ref.at[pl.ds(first, rows), pl.ds(other, cols)], self.from_core(g, kind, o), "core", base[kind] + o)
        part = functools.partial
        fresh = [part(self.corner, g, o) for o in far]
        for o in far:
            fresh += [part(self.side, g, "y", o), part(self.side, g, "x", o)]
        for o in far:
            fresh += [part(self.centre, g, o), part(self.along, g, o)]
        fresh.append(part(self.share, g))
        self.last.append(part(self.done, g))
        old, self.queue = self.queue, []
        while old or fresh:
            if old:
                self.queue.append(old.pop(0))
            if fresh:
                self.queue.append(fresh.pop(0))

    def corner(self, g, o):
        source = self.from_core(g, "d", o)
        self.arrive(g, source, o)
        piece = self.piece(g, *self.spot("d", o))
        self.add(piece, source)
        self.send(g, piece, self.box(g, "corner", o), "y" if o in self.over_y[g] else "x", 16 + o)

    def side(self, g, kind, o):
        source = self.from_core(g, kind, o)
        self.arrive(g, source, dict(y=4, x=8)[kind] + o)
        piece = self.piece(g, *self.spot(kind, o))
        if (o in self.over_y[g]) == (kind == "x"):
            box = self.box(g, "corner", o)
            self.arrive(g, box, 16 + o)
            self.add(piece, source, box)
        else:
            self.add(piece, source)
        self.send(g, piece, self.box(g, kind, o), kind, dict(y=20, x=24)[kind] + o)

    def centre(self, g, o):
        source, along_x, along_y = self.from_core(g, "o", o), self.box(g, "x", o), self.box(g, "y", o)
        self.arrive(g, source, 12 + o)
        self.arrive(g, along_y, 20 + o)
        self.arrive(g, along_x, 24 + o)
        self.add(self.piece(g, *self.spot("o", o)), source, along_x, along_y)

    def along(self, g, o):
        p = self.p
        z = p.line[o]
        piece = self.piece(g, z, p.y, p.x)
        for to, came, goes, first in (
            ("up", (z >= p.z) & (p.z > 0), z > p.z, 28),
            ("down", (z <= p.z) & (p.z < LINE - 1), z < p.z, 32),
        ):
            box = self.box(g, "line", z if o or to == "up" else LINE)

            @pl.when(came)
            def _():
                self.arrive(g, box, first + z)
                self.add(piece, box)

            if o and to == "up":
                self.send(g, piece, box, to, first + o, goes, first + z)
            elif o:
                last = z == p.z - 1
                self.send(g, piece, box, to, first + o, goes & jnp.logical_not(last), first + z)
                self.send(g, piece, self.box(g, "line", LINE), to, first + o, goes & last, first + z)

    def quarter(self, g, x, c):
        ref = getattr(self.r, GROUPS[g] + "_grad")
        rows, cols = ref.shape[0] // 2, ref.shape[1] // 2
        return ref.at[pl.ds(pl.multiple_of(x * rows, 16), rows), pl.ds(pl.multiple_of(c * cols, 128), cols)]

    def share(self, g):
        p = self.p
        mine = self.quarter(g, p.x, p.c)
        mine[...] = self.piece(g, p.z, p.y, p.x)[...]
        self.send(g, mine, mine, "x", 36)
        self.send(g, mine, mine, "core", 37)

    def done(self, g):
        p = self.p
        other = self.quarter(g, 1 - p.x, p.c)
        self.arrive(g, other, 36)
        self.send(g, other, other, "core", 38)
        self.arrive(g, self.quarter(g, p.x, 1 - p.c), 37)

    def finish(self):
        self.advance(len(self.queue))
        for item in self.last:
            item()
        for g in range(len(GROUPS)):
            self.arrive(g, self.quarter(g, 1 - self.p.x, 1 - self.p.c), 38)
        for when, copy in self.sends:
            if when is None:
                copy.wait_send()
            else:
                pl.when(when)(copy.wait_send)

    def advance(self, count):
        for item in self.queue[:count]:
            item()
        self.queue = self.queue[count:]


def pack_small(r):
    peers = 2 * LINE
    width = r.tokens.shape[1]
    part = width // peers
    r.owners[...] = jnp.zeros(r.owners.shape, F32)
    for shard in range(peers):
        r.owners[shard, 0:8, 0:part] = r.grad_small[:, shard * part : (shard + 1) * part]
        for i in range(2):
            first = (shard * 2 + i) * part
            r.owners[shard, 8 + i : 9 + i, 0:part] = r.grad_qkv_bias[0:1, first : first + part]
        first = 2 * width + shard * part
        r.owners[shard, 10:11, 0:part] = r.grad_qkv_bias[0:1, first : first + part]
        for i in range(4):
            first = (shard * 4 + i) * part
            r.owners[shard, 11 + i : 12 + i, 0:part] = r.grad_up_bias[0:1, first : first + part]


def owner_copy(r, place, k, receive=False):
    other = (place.fsdp + k) % (2 * LINE)
    slot = other if receive else place.fsdp
    return push(
        r.owners.at[other], r.owned.at[slot], (place.seq, other), r.small_send.at[k], r.owned_recv.at[slot]
    )


def small_reduce_start(r, place):
    pack_small(r)
    lax.fori_loop(1, 2 * LINE, lambda k, carry: (owner_copy(r, place, k).start(), carry)[1], 0)


def small_reduce_middle(r, place):
    def receive(k, total):
        owner_copy(r, place, k, True).wait_recv()
        owner_copy(r, place, k).wait_send()
        return total + r.owned[(place.fsdp + k) % (2 * LINE)]

    r.shared[place.seq] = lax.fori_loop(1, 2 * LINE, receive, r.owners[place.fsdp])
    for k in range(1, 4):
        shared_copy(r, place, k).start()


def shared_copy(r, place, k, receive=False):
    other = (place.seq + k) % 4
    slot = other if receive else place.seq
    return push(
        r.shared.at[place.seq], r.shared.at[slot], (other, place.fsdp), r.shared_send.at[k], r.shared_recv.at[slot]
    )


def small_reduce_finish(r, place):
    for k in range(1, 4):
        shared_copy(r, place, k, True).wait_recv()
        shared_copy(r, place, k).wait_send()
    r.small_total[...] = r.shared[0] + r.shared[1] + r.shared[2] + r.shared[3]


class Home:
    def __init__(self, r, place, both, target, index):
        self.r, self.p, self.both, self.target, self.index = r, place, both, target, index
        rows = both.shape[0] // 2
        self.rows = both.at[pl.ds(pl.multiple_of(place.c * rows, 16), rows), :]

    def across(self, c):
        rows = self.both.shape[0] // 2
        part = self.both.at[pl.ds(pl.multiple_of(c * rows, 16), rows), :]
        return push(part, part, self.p.to["core"], self.r.home_send.at[self.index, 0], self.r.home_recv.at[self.index, 0])

    def along_x(self, x):
        send, recv = self.r.home_send, self.r.home_recv
        return push(
            self.r.leaving, self.target.at[x], self.p.to["x"], send.at[self.index, 1], recv.at[self.index, 1]
        )

    def start(self):
        self.across(self.p.c).start()

    def turn(self):
        self.across(1 - self.p.c).wait_recv()
        ordered = dot_nn(self.r.place[...], self.both[...]).astype(BF16)
        half = ordered.shape[0] // 2
        self.r.leaving[...] = ordered[half:]
        self.along_x(self.p.x).start()
        self.target[self.p.x] = ordered[:half]

    def left(self):
        self.along_x(self.p.x).wait_send()

    def finish(self):
        self.along_x(1 - self.p.x).wait_recv()
        self.across(self.p.c).wait_send()


def place_back(r, place):
    bundle, length = r.place.shape
    start = r.start[0:1, 0:1]
    quarter = length // 4

    def block(index):
        rows = tile_at(index, 128)
        shape = (128, length)
        mine = lax.broadcasted_iota(jnp.int32, shape, 0) + index * 128
        away = mine >= quarter
        mine = jnp.where(away, mine - quarter + quarter * (2 * (1 - place.x) + place.c), mine + quarter * (2 * place.x + place.c))
        source = mine.astype(F32) - start
        source = jnp.where(source < 0, source + length, source)
        here = lax.broadcasted_iota(jnp.int32, shape, 1).astype(F32)
        r.place[rows, :] = jnp.where(here == source, 1.0, 0.0).astype(BF16)

    loop(bundle // 128, block)


def greet(place):
    barrier = pltpu.get_barrier_semaphore()
    seq, fsdp = place.seq, place.fsdp
    peers = 2 * LINE

    def others(k, carry):
        pl.semaphore_signal(barrier, inc=1, device_id=(seq, (fsdp + k) % peers), device_id_type=MESH)
        return carry

    lax.fori_loop(1, peers, others, 0)
    for k in range(1, 4):
        pl.semaphore_signal(barrier, inc=1, device_id=((seq + k) % 4, fsdp), device_id_type=MESH)
    pl.semaphore_wait(barrier, peers + 2)


def small_send(r, place, k):
    peers = 2 * LINE
    other = (place.fsdp + k) % peers
    return push(
        r.packed_in, r.packed.at[place.fsdp], (place.seq, other), r.small_send.at[k], r.small_recv.at[place.fsdp]
    )


def small_start(r, place):
    lax.fori_loop(1, 2 * LINE, lambda k, carry: (small_send(r, place, k).start(), carry)[1], 0)
    r.packed[place.fsdp] = r.packed_in[...]


def small_finish(r, place):
    def receive(k, carry):
        other = (place.fsdp + k) % (2 * LINE)
        push(
            r.packed_in, r.packed.at[other], (place.seq, other), r.small_send.at[k], r.small_recv.at[other]
        ).wait_recv()
        small_send(r, place, k).wait_send()
        return carry

    lax.fori_loop(1, 2 * LINE, receive, 0)
    part = r.tokens.shape[1] // (2 * LINE)
    for shard in range(2 * LINE):
        rows = r.packed[shard].astype(F32)
        for i in range(8):
            r.small[i : i + 1, shard * part : (shard + 1) * part] = rows[i : i + 1, 0:part]
        for i in range(3):
            first = (shard * 3 + i) * part
            r.qkv_bias[0:1, first : first + part] = rows[8 + i : 9 + i, 0:part]
        for i in range(4):
            first = (shard * 4 + i) * part
            r.up_bias[0:1, first : first + part] = rows[11 + i : 12 + i, 0:part]


class Exchange:
    def __init__(self, r, place, source, target, index):
        self.p, self.target = place, target
        rows = target.shape[0] // 4
        p = place

        def quarter(x, c):
            return target.at[pl.ds(pl.multiple_of((2 * x + c) * rows, 16), rows), :]

        self.keep = pltpu.make_async_copy(source.at[p.x], quarter(p.x, p.c), r.local_sems.at[4 + index])
        send, recv = r.rows_send, r.rows_recv
        self.along_x = push(source.at[1 - p.x], quarter(p.x, p.c), p.to["x"], send.at[index, 0], recv.at[index, 0])
        self.own = push(source.at[p.x], quarter(p.x, p.c), p.to["core"], send.at[index, 1], recv.at[index, 1])
        passed = quarter(1 - p.x, p.c)
        self.passed = push(passed, passed, p.to["core"], send.at[index, 2], recv.at[index, 2])
        there = quarter(1 - p.x, p.c)
        self.arrive_x = push(there, there, p.to["x"], send.at[index, 0], recv.at[index, 0])
        one, two = quarter(p.x, 1 - p.c), quarter(1 - p.x, 1 - p.c)
        self.arrive = [
            push(one, one, p.to["core"], send.at[index, 1], recv.at[index, 1]),
            push(two, two, p.to["core"], send.at[index, 2], recv.at[index, 2]),
        ]

    def start(self):
        self.keep.start()
        self.along_x.start()
        self.own.start()

    def forward(self):
        self.arrive_x.wait_recv()
        self.passed.start()

    def finish(self):
        self.keep.wait()
        for copy in self.arrive:
            copy.wait_recv()
        for copy in (self.along_x, self.own, self.passed):
            copy.wait_send()


def collect_meta(r, place):
    r.meta_rows[...] = jnp.zeros(r.meta_rows.shape, F32)
    r.meta_rows[0:1, :] = r.segments[pl.ds(place.x, 1), :].astype(F32)
    for axis in range(2):
        r.meta_rows[1 + axis : 2 + axis, :] = r.positions[axis, pl.ds(place.x, 1), :].astype(F32)
    r.meta[...] = r.meta_rows[...].astype(BF16)


WEIGHTS = ("w_qkv", "w_out", "w_up", "w_down")


class Whole:
    def __init__(self, r):
        self.copies = [
            pltpu.make_async_copy(getattr(r, name + "_in"), getattr(r, name), r.local_sems.at[i])
            for i, name in enumerate(WEIGHTS)
        ]
        for copy in self.copies:
            copy.start()

    def advance(self, count):
        pass

    def finish(self, g):
        self.copies[g].wait()

    def sent(self, g):
        pass


def spread_head_gains(r):
    columns = jnp.transpose(r.small[...])
    r.head_gain[...] = jnp.zeros(r.head_gain.shape, F32)
    r.head_gain_sums[...] = jnp.zeros(r.head_gain_sums.shape, F32)
    for head in range(2 * H):
        row = head % H * HD
        column = QUERY_GAIN if head < H else KEY_GAIN
        r.head_gain[:, head : head + 1] = columns[row : row + HD, column : column + 1]


def forward(r, gather, arrive_cotangent):
    rope_tables(r)
    forward_attention(r, gather)
    gather.finish(1)
    forward_middle(r)
    gather.finish(2)
    arrive_cotangent()
    forward_up(r, gather)
    gather.finish(3)
    forward_down(r)


class Alone:
    def __init__(self, r):
        self.r, self.copies = r, []

    def begin(self, g):
        name = WEIGHTS[g]
        copy = pltpu.make_async_copy(getattr(self.r, name), getattr(self.r, name + "_grad"), self.r.local_sems.at[g])
        copy.start()
        self.copies.append(copy)

    def advance(self, count):
        pass

    def finish(self):
        for copy in self.copies:
            copy.wait()


def backward(r, gather, reduce, hooks):
    for index in (0, 1):
        fetch(r, index).start()
    gather.sent(3)
    backward_down(r)
    reduce.begin(3)
    hooks.after_down()
    gather.sent(2)
    backward_up(r, reduce)
    reduce.begin(2)
    gather.sent(1)
    backward_middle(r, reduce)
    reduce.begin(1)
    hooks.before_heads()
    backward_attention(r, reduce)
    gather.sent(0)
    backward_heads_weight(r, reduce)
    reduce.begin(0)
    backward_inputs(r)
    hooks.after_inputs()
    reduce.finish()


class Hooks:
    def after_down(self):
        pass

    def before_heads(self):
        pass

    def after_inputs(self):
        pass


class HomeHooks(Hooks):
    def __init__(self, r, place):
        self.r, self.p = r, place
        self.result = Home(r, place, r.seq_tokens, r.result, 0)
        self.grads = Home(r, place, r.seq_cotangent, r.grad_result, 1)

    def after_down(self):
        place_back(self.r, self.p)
        self.result.turn()

    def after_inputs(self):
        self.grads.start()
        small_reduce_start(self.r, self.p)
        self.result.left()
        self.grads.turn()
        small_reduce_middle(self.r, self.p)


def place_rows(r, source, target):
    target[...] = dot_nn(r.place[...], source[...]).astype(BF16)


def whole_kernel(names, *refs):
    r = Refs()
    for name, ref in zip(names, refs, strict=True):
        setattr(r, name, ref)
    gather = Whole(r)
    r.ones[...] = jnp.ones(r.ones.shape, BF16)
    place_tokens(r)
    place_rows(r, r.seq_tokens, r.tokens)
    spread_head_gains(r)
    r.result_rows, r.grad_rows = r.result, r.grad_result
    forward(r, gather, lambda: place_rows(r, r.seq_cotangent, r.cotangent))
    backward(r, gather, Alone(r), Hooks())


def fused_kernel(names, *refs):
    r = Refs()
    for name, ref in zip(names, refs, strict=True):
        setattr(r, name, ref)
    place = Place()
    gather = Gather(r, place, {0: (0, 1), 1: (0,), 2: (0, 1), 3: (0,)})
    for g, name in enumerate(WEIGHTS):
        pltpu.make_async_copy(getattr(r, name + "_in"), gather.shard(g), r.local_sems.at[g]).start()
    tokens = Exchange(r, place, r.tokens_in, r.seq_tokens, 0)
    cotangent = Exchange(r, place, r.cotangent_in, r.seq_cotangent, 1)
    greet(place)
    gather.advance(1)
    tokens.start()
    small_start(r, place)
    r.ones[...] = jnp.ones(r.ones.shape, BF16)
    collect_meta(r, place)
    place_tokens(r)
    gather.advance(2)
    tokens.forward()
    gather.advance(2)
    small_finish(r, place)
    spread_head_gains(r)
    gather.advance(2)
    tokens.finish()
    place_rows(r, r.seq_tokens, r.tokens)
    gather.advance(4)
    cotangent.start()

    def arrive_cotangent():
        cotangent.forward()
        cotangent.finish()
        place_rows(r, r.seq_cotangent, r.cotangent)

    hooks = HomeHooks(r, place)
    r.result_rows, r.grad_rows = hooks.result.rows, hooks.grads.rows
    forward(r, gather, arrive_cotangent)
    hooks.result.start()
    backward(r, gather, Reduce(r, place, {0: (0, 1), 1: (0, 1), 2: (0,), 3: (0, 1)}), hooks)
    small_reduce_finish(r, place)
    hooks.result.finish()
    hooks.grads.finish()
    hooks.grads.left()


def layer(fused, tokens, cotangent, segments, positions, small, qkv_bias, up_bias, *weights):
    peers = 2 * LINE
    scale = peers if fused else 1
    width = tokens.shape[-1]
    length = segments.shape[1]
    bundle = length // 2
    hidden = weights[2].shape[1]
    shape = jax.ShapeDtypeStruct
    vmem = pl.BlockSpec(memory_space=pltpu.VMEM)
    hbm = pl.BlockSpec(memory_space=pl.ANY)
    inputs = {}
    if fused:
        inputs.update(
            tokens_in=(tokens, hbm),
            cotangent_in=(cotangent, hbm),
            segments=(segments, vmem),
            positions=(positions, vmem),
            packed_in=(small, vmem),
        )
    else:
        inputs.update(
            seq_tokens=(tokens, vmem),
            seq_cotangent=(cotangent, vmem),
            meta=(segments, vmem),
            small=(small, vmem),
            qkv_bias=(qkv_bias, vmem),
            up_bias=(up_bias, vmem),
        )
    full = [(w.shape[0] * scale, w.shape[1]) for w in weights]
    for name, w in zip(WEIGHTS, weights):
        inputs[name + "_in"] = (w, hbm)
    outputs = dict(
        result=(shape(tokens.shape if fused else (bundle, width), BF16), vmem),
        grad_result=(shape(tokens.shape if fused else (bundle, width), BF16), vmem),
        chances_kept=(shape((H, bundle, bundle), BF16), hbm),
    )
    scratch = {}
    vectors = dict(grad_small=(8, width), grad_qkv_bias=(8, 3 * width), grad_up_bias=(8, hidden))
    if fused:
        outputs["small_total"] = (shape((16, 128), F32), vmem)
        scratch.update({name: pltpu.VMEM(size, F32) for name, size in vectors.items()})
    else:
        outputs.update({name: (shape(size, F32), vmem) for name, size in vectors.items()})
    for name, size in zip(WEIGHTS, full):
        outputs[name + "_grad"] = (shape((size[0] // scale, size[1]), BF16), vmem if fused else hbm)
        scratch[name] = pltpu.VMEM(size, BF16)
    if fused:
        groups, pieces = len(WEIGHTS), 2 * peers
        scratch.update(
            seq_tokens=pltpu.VMEM((length, width), BF16),
            seq_cotangent=pltpu.VMEM((length, width), BF16),
            meta_rows=pltpu.VMEM((8, length), F32),
            meta=pltpu.VMEM((8, length), BF16),
            packed=pltpu.VMEM((peers, 16, 128), BF16),
            small=pltpu.VMEM((8, width), F32),
            qkv_bias=pltpu.VMEM((1, 3 * width), F32),
            up_bias=pltpu.VMEM((1, hidden), F32),
            small_send=pltpu.SemaphoreType.DMA((peers,)),
            small_recv=pltpu.SemaphoreType.DMA((peers,)),
            rows_send=pltpu.SemaphoreType.DMA((2, 3)),
            rows_recv=pltpu.SemaphoreType.DMA((2, 3)),
            gather_send=pltpu.SemaphoreType.DMA((groups, 40)),
            gather_recv=pltpu.SemaphoreType.DMA((groups, pieces)),
            gather_core=pltpu.SemaphoreType.DMA((groups, pieces)),
            reduce_send=pltpu.SemaphoreType.DMA((groups, 40)),
            reduce_recv=pltpu.SemaphoreType.DMA((groups, 40)),
            home_send=pltpu.SemaphoreType.DMA((2, 2)),
            home_recv=pltpu.SemaphoreType.DMA((2, 2)),
            leaving=pltpu.VMEM((length // 4, width), BF16),
            owners=pltpu.VMEM((peers, 16, 128), F32),
            owned=pltpu.VMEM((peers, 16, 128), F32),
            owned_recv=pltpu.SemaphoreType.DMA((peers,)),
            shared=pltpu.VMEM((4, 16, 128), F32),
            shared_send=pltpu.SemaphoreType.DMA((4,)),
            shared_recv=pltpu.SemaphoreType.DMA((4,)),
        )
        for name, size in zip(WEIGHTS, full):
            scratch["core_" + name] = pltpu.VMEM((size[0], size[1] // 2), BF16)
            scratch["box_" + name] = pltpu.VMEM((17, size[0] // (2 * peers), size[1] // 2), BF16)
    scratch.update(
        local_sems=pltpu.SemaphoreType.DMA((8,)),
        ones=pltpu.VMEM((8, bundle), BF16),
        start=pltpu.VMEM((8, 128), F32),
        place=pltpu.VMEM((bundle, length), BF16),
        marks_row=pltpu.VMEM((8, bundle), F32),
        marks_col=pltpu.VMEM((bundle, 8), F32),
        cosine=pltpu.VMEM((2, HD // 4, bundle), F32),
        sine=pltpu.VMEM((2, HD // 4, bundle), F32),
        head_gain=pltpu.VMEM((HD, 128), F32),
        head_gain_sums=pltpu.VMEM((HD, 128), F32),
        tokens=pltpu.VMEM((bundle, width), BF16),
        cotangent=pltpu.VMEM((bundle, width), BF16),
        hidden_pre_t=pltpu.VMEM((width, bundle), BF16),
        projected_t=pltpu.VMEM((3 * width, bundle), BF16),
        turned_t=pltpu.VMEM((2 * width, bundle), BF16),
        chances=pltpu.VMEM((2, bundle, bundle), BF16),
        chance_sems=pltpu.SemaphoreType.DMA((2,)),
        attended_t=pltpu.VMEM((width, bundle), BF16),
        middle=pltpu.VMEM((bundle, width), F32),
        hidden_mlp_t=pltpu.VMEM((width, bundle), BF16),
        before=pltpu.VMEM((bundle, TILE), F32),
        active=pltpu.VMEM((bundle, hidden), BF16),
        active_t=pltpu.VMEM((hidden, bundle), BF16),
        slope=pltpu.VMEM((bundle, hidden), BF16),
        grad_hidden=pltpu.VMEM((bundle, width), F32),
        rows=pltpu.VMEM((bundle, width), BF16),
        grad_attended_t=pltpu.VMEM((width, bundle), BF16),
    )
    names = tuple(inputs) + tuple(outputs) + tuple(scratch)
    params = dict(vmem_limit_bytes=63 << 20)
    if fused:
        params.update(collective_id=0, has_side_effects=True)
    return pl.pallas_call(
        functools.partial(fused_kernel if fused else whole_kernel, names),
        out_shape=tuple(o[0] for o in outputs.values()),
        in_specs=[i[1] for i in inputs.values()],
        out_specs=tuple(o[1] for o in outputs.values()),
        scratch_shapes=list(scratch.values()),
        compiler_params=pltpu.CompilerParams(**params),
        name="layer",
    )(*(i[0] for i in inputs.values()))


def finish_kernel(rows, *refs):
    (result, grad_result, small, *weights), outs = refs[:7], refs[7:]
    outs[0][...] = result[...]
    outs[1][...] = grad_result[...]
    for source, target in zip(weights, outs[2:6]):
        target[...] = source[...].astype(F32)
    part = rows
    for target, first, count in zip(outs[6:], (0, 1, 2, 3, 4, 5, 6, 7, 8, 10, 11), (1,) * 8 + (2, 1, 4)):
        for i in range(count):
            target[0:1, i * part : (i + 1) * part] = small[first + i : first + i + 1, 0:part]


def finish(part, result, grad_result, small, *weights):
    shape = jax.ShapeDtypeStruct
    vmem = pl.BlockSpec(memory_space=pltpu.VMEM)
    outs = [shape(result.shape, BF16), shape(grad_result.shape, BF16)] + [shape(w.shape, F32) for w in weights]
    outs += [shape((1, part * count), F32) for count in (1,) * 8 + (2, 1, 4)]
    return pl.pallas_call(
        functools.partial(finish_kernel, part),
        out_shape=tuple(outs),
        in_specs=[vmem] * 7,
        out_specs=tuple([vmem] * len(outs)),
        compiler_params=pltpu.CompilerParams(vmem_limit_bytes=40 << 20),
        name="finish",
    )(result, grad_result, small, *weights)


def shards(
    tokens,
    pre_gain,
    pre_bias,
    query_key_value_weight,
    query_key_value_bias,
    query_gain,
    key_gain,
    output_weight,
    output_bias,
    mlp_gain,
    mlp_bias,
    up_matrix_weight,
    up_offset_bias,
    down_matrix_weight,
    down_offset_bias,
    segments,
    positions,
    cotangent,
):
    rank = lax.axis_index("seq")
    x = rank // 2
    width = tokens.shape[2]
    length = segments.shape[1]
    fsdp = lax.axis_size("fsdp")
    part = width // fsdp
    weights_in = (query_key_value_weight, output_weight, up_matrix_weight, down_matrix_weight)
    vectors = (
        pre_gain, pre_bias, query_gain, key_gain, output_bias, mlp_gain, mlp_bias, down_offset_bias,
        query_key_value_bias, up_offset_bias,
    )
    if fsdp == 2 * LINE:
        packed = jnp.concatenate(vectors).reshape(-1, part)
        packed = jnp.pad(packed, ((0, 16 - packed.shape[0]), (0, 128 - part)))
        result, grad_result, _, small_total, *weight_grads = layer(
            True, tokens, cotangent, segments, positions, packed, None, None, *weights_in
        )
        result, grad_result, g0, g1, g2, g3, *v = finish(part, result, grad_result, small_total, *weight_grads)
        v = [vector.reshape(-1) for vector in v]
        return (
            result, grad_result, v[PRE_GAIN], v[PRE_BIAS], g0, v[8], v[9], v[QUERY_GAIN], v[KEY_GAIN], g1, v[OUT_BIAS],
            v[MLP_GAIN], v[MLP_BIAS], g2, v[10], g3, v[DOWN_BIAS],
        )
    else:
        gather = functools.partial(lax.all_gather, axis_name="fsdp", axis=0, tiled=True)
        packed = gather(jnp.concatenate(vectors)[None]).astype(F32)
        small = jnp.stack([packed[:, i * part : (i + 1) * part].reshape(width) for i in range(8)])
        qkv_bias = packed[:, 8 * part : 11 * part].reshape(1, 3 * width)
        up_bias = packed[:, 11 * part :].reshape(1, -1)
        seq_tokens = lax.dynamic_index_in_dim(lax.all_gather(tokens, "seq", axis=1, tiled=True), x, 0, False)
        seq_cotangent = lax.dynamic_index_in_dim(lax.all_gather(cotangent, "seq", axis=1, tiled=True), x, 0, False)
        labels = lax.dynamic_index_in_dim(segments, x, 0, True)
        places = lax.dynamic_index_in_dim(positions, x, 1, False)
        meta = jnp.concatenate([labels, places, jnp.zeros((5, length), jnp.int32)], axis=0).astype(BF16)
        results = layer(False, seq_tokens, seq_cotangent, meta, None, small, qkv_bias, up_bias, *map(gather, weights_in))
    result, grad_result, _, grad_small, grad_qkv_bias, grad_up_bias, *weight_grads = results
    counts = jnp.stack([jnp.sum(segments == v, axis=1) for v in range(4)])
    first = jnp.argmax(counts == length // 2, axis=0)
    starts = jnp.sum(segments < first[:, None], axis=1)

    def home(bundle):
        every = lax.all_gather(bundle, "seq").reshape(2, length, width)
        own = rank * (length // 4) + jnp.arange(length // 4)
        index = (own[None] - starts[:, None]) % length
        return jnp.take_along_axis(every, index[..., None], axis=1)

    scatter = functools.partial(lax.psum_scatter, axis_name="fsdp", scatter_dimension=0, tiled=True)

    def total_of(grad):
        return lax.psum(scatter(grad).astype(BF16), "seq").astype(F32)

    weights = [total_of(g) for g in weight_grads]
    pieces = [grad_small[i].reshape(fsdp, part) for i in range(8)]
    pieces += [grad_qkv_bias[0, : 2 * width].reshape(fsdp, -1), grad_qkv_bias[0, 2 * width :].reshape(fsdp, -1)]
    pieces += [grad_up_bias[0].reshape(fsdp, -1)]
    total = lax.psum(scatter(jnp.concatenate(pieces, axis=1)), "seq")[0]
    s = [total[i * part : (i + 1) * part] for i in range(8)]
    query_key_bias, value_bias, up_total = total[8 * part : 10 * part], total[10 * part : 11 * part], total[11 * part :]
    return (
        home(result), home(grad_result), s[PRE_GAIN], s[PRE_BIAS], weights[0], query_key_bias, value_bias,
        s[QUERY_GAIN], s[KEY_GAIN], weights[1], s[OUT_BIAS], s[MLP_GAIN], s[MLP_BIAS], weights[2], up_total,
        weights[3], s[DOWN_BIAS],
    )


def solution(mesh):
    rows, matrix, activations = P("fsdp"), P("fsdp", None), P("fsdp", "seq", None)
    placed = (
        activations, rows, rows, matrix, rows, rows, rows, matrix, rows, rows, rows, matrix, rows, matrix, rows,
        P("fsdp", None), P(None, "fsdp", None), activations,
    )
    given = (
        activations, activations, rows, rows, matrix, rows, rows, rows, rows, matrix, rows, rows, rows, matrix, rows,
        matrix, rows,
    )
    return jax.shard_map(shards, mesh=mesh, in_specs=placed, out_specs=given, check_vma=False)
```

```python
import functools

import jax
import jax.numpy as jnp
from jax import lax
from jax.experimental import pallas as pl
from jax.experimental.pallas import tpu as pltpu
from jax.sharding import PartitionSpec as P

H = 12
HD = 64
EPSILON = 1e-06
NEGATIVE = -1e30
ROPE_BASE = 100.0
F32 = jnp.float32
BF16 = jnp.bfloat16
TILE = 256


def dot_nn(a, b):
    return lax.dot_general(a, b, (((1,), (0,)), ((), ())), preferred_element_type=F32)


def dot_nt(a, b):
    return lax.dot_general(a, b, (((1,), (1,)), ((), ())), preferred_element_type=F32)


def dot_tn(a, b):
    return lax.dot_general(a, b, (((0,), (0,)), ((), ())), preferred_element_type=F32)


def tile_at(index, size=TILE):
    return pl.ds(pl.multiple_of(index * size, size), size)


def loop(count, body, first=0):
    def step(index, carry):
        body(index)
        return carry

    lax.fori_loop(first, first + count, step, 0)


def rows_sum(block):
    rows, width = block.shape
    return jnp.sum(block.reshape(rows // 8, 8, width), axis=0)


def column_sums_exact(ones, block):
    return dot_nn(ones, block)[0:1]


def place_tokens(r):
    bundle, length = r.place.shape
    labels = r.meta[0:1, :].astype(F32)
    start = jnp.zeros((1, 1), F32)
    found = jnp.zeros((1, 1), F32)
    for value in range(4):
        here = jnp.sum(jnp.where(labels == value, 1.0, 0.0), axis=1, keepdims=True)
        below = jnp.sum(jnp.where(labels < value, 1.0, 0.0), axis=1, keepdims=True)
        hit = jnp.where(here == bundle, 1.0, 0.0) * (1.0 - found)
        start = start + hit * below
        found = found + hit
    r.start[...] = jnp.broadcast_to(start, r.start.shape)
    core = lax.axis_index("seq") % 2

    def block(index):
        rows = tile_at(index, 128)
        shape = (128, length)
        mine = lax.broadcasted_iota(jnp.int32, shape, 0) + (index * 128 + core * bundle)
        target = mine.astype(F32) + start
        target = jnp.where(target >= length, target - length, target)
        source = lax.broadcasted_iota(jnp.int32, shape, 1).astype(F32)
        r.place[rows, :] = jnp.where(source == target, 1.0, 0.0).astype(BF16)

    loop(bundle // 128, block)
    r.marks_row[...] = dot_nt(r.meta[...], r.place[...])
    r.marks_col[...] = dot_nt(r.place[...], r.meta[...])


def rope_tables(r):
    quarter = HD // 4
    bundle = r.cosine.shape[-1]
    step = lax.broadcasted_iota(jnp.int32, (quarter, bundle), 0).astype(F32)
    frequency = jnp.exp(step * (-jnp.log(jnp.float32(ROPE_BASE)) / quarter))
    for axis in range(2):
        angle = r.marks_row[1 + axis : 2 + axis, :] * frequency
        r.cosine[axis] = jnp.cos(angle)
        r.sine[axis] = jnp.sin(angle)


def normalized(block):
    mean = jnp.mean(block, axis=-1, keepdims=True)
    centred = block - mean
    scale = lax.rsqrt(jnp.mean(centred * centred, axis=-1, keepdims=True) + EPSILON)
    return centred * scale, scale


def norm_rows(source, gain, bias, target, rows=32):
    def block(index):
        where = tile_at(index, rows)
        unit, _ = normalized(source[where, :].astype(F32))
        target[where, :] = (unit * gain + bias).astype(target.dtype)

    loop(source.shape[0] // rows, block)


def norm_rows_back(source, grads, base, gain, store, rows=32):
    width = source.shape[1]

    def block(index, carry):
        gain_sum, bias_sum = carry
        where = tile_at(index, rows)
        unit, scale = normalized(source[where, :].astype(F32))
        outer = grads[where, :]
        inner = outer * gain
        first = jnp.mean(inner, axis=-1, keepdims=True)
        second = jnp.mean(inner * unit, axis=-1, keepdims=True)
        store(where, base[where, :].astype(F32) + scale * (inner - first - unit * second))
        return gain_sum + rows_sum(outer * unit), bias_sum + rows_sum(outer)

    zero = jnp.zeros((8, width), F32)
    gain_sum, bias_sum = lax.fori_loop(0, source.shape[0] // rows, block, (zero, zero))
    return jnp.sum(gain_sum, axis=0, keepdims=True), jnp.sum(bias_sum, axis=0, keepdims=True)


def transpose_into(target, source):
    def block(index):
        where = tile_at(index, 128)
        target[where, :] = jnp.transpose(source[:, where])

    loop(source.shape[1] // 128, block)


def head_norm(vectors):
    mean = jnp.mean(vectors, axis=0, keepdims=True)
    centred = vectors - mean
    scale = lax.rsqrt(jnp.mean(centred * centred, axis=0, keepdims=True) + EPSILON)
    return centred * scale, scale


def turn(vectors, r):
    q = HD // 4
    out = []
    for axis in range(2):
        one, two = vectors[2 * axis * q : (2 * axis + 1) * q], vectors[(2 * axis + 1) * q : (2 * axis + 2) * q]
        cosine, sine = r.cosine[axis], r.sine[axis]
        out.append(one * cosine - two * sine)
        out.append(two * cosine + one * sine)
    return jnp.concatenate(out, axis=0) * HD ** (-0.5)


def turn_back(vectors, r):
    q = HD // 4
    out = []
    for axis in range(2):
        one, two = vectors[2 * axis * q : (2 * axis + 1) * q], vectors[(2 * axis + 1) * q : (2 * axis + 2) * q]
        cosine, sine = r.cosine[axis], r.sine[axis]
        out.append(one * cosine + two * sine)
        out.append(two * cosine - one * sine)
    return jnp.concatenate(out, axis=0) * HD ** (-0.5)


PRE_GAIN, PRE_BIAS, QUERY_GAIN, KEY_GAIN, OUT_BIAS, MLP_GAIN, MLP_BIAS, DOWN_BIAS = range(8)


def gain_of(r, head):
    lanes = lax.broadcasted_iota(jnp.int32, (HD, 128), 1)
    return jnp.sum(jnp.where(lanes == head, r.head_gain[...], 0.0), axis=1, keepdims=True)


def spill(r, index):
    return pltpu.make_async_copy(r.chances.at[index % 2], r.chances_kept.at[index], r.chance_sems.at[index % 2])


def fetch(r, index):
    return pltpu.make_async_copy(r.chances_kept.at[index], r.chances.at[index % 2], r.chance_sems.at[index % 2])


def norm_tokens(r):
    norm_rows(r.tokens, r.small[PRE_GAIN : PRE_GAIN + 1, :], r.small[PRE_BIAS : PRE_BIAS + 1, :], r.rows)
    transpose_into(r.hidden_pre_t, r.rows)


def project(r, index):
    cols = tile_at(index)
    part = dot_nn(r.rows[...], r.w_qkv[:, cols]) + r.qkv_bias[0:1, cols]
    r.projected_t[cols, :] = jnp.transpose(part.astype(BF16))


def prepare(r, part):
    def head(index):
        rows = tile_at(index, HD)
        unit, _ = head_norm(r.projected_t[rows, :].astype(F32))
        r.turned_t[rows, :] = turn(unit * gain_of(r, index), r).astype(BF16)

    loop(H // 2, head, part * (H // 2))


def attend(r, index):
    rows = tile_at(index, HD)
    key_rows = tile_at(index + H, HD)
    value_rows = tile_at(index + 2 * H, HD)
    slot = index % 2

    @pl.when(index >= 2)
    def _():
        spill(r, index - 2).wait()

    scores = dot_tn(r.turned_t[key_rows, :], r.turned_t[rows, :])
    scores = jnp.where(r.marks_col[:, 0:1] == r.marks_row[0:1, :], scores, NEGATIVE)
    raised = jnp.exp(scores - jnp.max(scores, axis=0, keepdims=True))
    chances = (raised * (1.0 / jnp.sum(raised, axis=0, keepdims=True))).astype(BF16)
    r.chances[slot] = chances
    spill(r, index).start()
    r.attended_t[rows, :] = dot_nn(r.projected_t[value_rows, :], chances).astype(BF16)


def attended_rows(r):
    for index in (H - 2, H - 1):
        spill(r, index).wait()
    transpose_into_rows(r.rows, r.attended_t)


def transpose_into_rows(target, source):
    def block(index):
        where = tile_at(index, 128)
        target[:, where] = jnp.transpose(source[where, :])

    loop(source.shape[0] // 128, block)


def branch(r, index):
    cols = tile_at(index)
    part = dot_nn(r.rows[...], r.w_out[:, cols]) + r.small[OUT_BIAS : OUT_BIAS + 1, cols]
    r.middle[:, cols] = r.tokens[:, cols].astype(F32) + part


def norm_middle(r):
    norm_rows(r.middle, r.small[MLP_GAIN : MLP_GAIN + 1, :], r.small[MLP_BIAS : MLP_BIAS + 1, :], r.rows)
    transpose_into(r.hidden_mlp_t, r.rows)


def up(r, index, give):
    cols = tile_at(index)
    r.before[...] = dot_nn(r.rows[...], r.w_up[:, cols]) + r.up_bias[0:1, cols]

    def activate(part):
        rows = tile_at(part, 64)
        v = r.before[rows, :]
        half = 0.5 + 0.5 * lax.erf(v * 0.7071067811865476)
        r.active[rows, cols] = (v * half).astype(BF16)
        r.slope[rows, cols] = (half + v * (jnp.exp(-0.5 * v * v) * 0.3989422804014327)).astype(BF16)

    loop(r.before.shape[0] // 64, activate)
    give(index, dot_nn(jnp.transpose(r.active[:, cols]), r.cotangent[...]).astype(BF16))


def down(r, index):
    cols = tile_at(index)
    part = dot_nn(r.active[...], r.w_down[:, cols]) + r.small[DOWN_BIAS : DOWN_BIAS + 1, cols]
    r.result_rows[:, cols] = (r.middle[:, cols] + part).astype(BF16)


def grad_before(r, index):
    rows = tile_at(index)
    grads = dot_nt(r.cotangent[...], r.w_down[rows, :]) * r.slope[:, rows].astype(F32)
    r.slope[:, rows] = grads.astype(BF16)
    r.grad_up_bias[0:1, rows] = jnp.sum(rows_sum(grads), axis=0, keepdims=True)


def grad_hidden_up(r, index):
    cols = tile_at(index)
    r.grad_hidden[:, cols] = dot_nt(r.slope[...], r.w_up[cols, :])


def weight_up(r, index):
    cols = tile_at(index)
    r.w_up[:, cols] = dot_nn(r.hidden_mlp_t[...], r.slope[:, cols]).astype(BF16)


def norm_middle_back(r):
    def store(where, value):
        r.middle[where, :] = value
        r.rows[where, :] = value.astype(BF16)

    gain, bias = norm_rows_back(r.middle, r.grad_hidden, r.cotangent, r.small[MLP_GAIN : MLP_GAIN + 1, :], store)
    r.grad_small[MLP_GAIN : MLP_GAIN + 1, :] = gain
    r.grad_small[MLP_BIAS : MLP_BIAS + 1, :] = bias
    r.grad_small[OUT_BIAS : OUT_BIAS + 1, :] = column_sums_exact(r.ones[...], r.rows[...])
    r.grad_small[DOWN_BIAS : DOWN_BIAS + 1, :] = column_sums_exact(r.ones[...], r.cotangent[...])


def out_back(r, index):
    rows = tile_at(index)
    r.grad_attended_t[rows, :] = dot_nt(r.w_out[rows, :], r.rows[...]).astype(BF16)
    r.w_out[rows, :] = dot_nn(r.attended_t[rows, :], r.rows[...]).astype(BF16)


def attend_back(r, index):
    rows = tile_at(index, HD)
    key_rows = tile_at(index + H, HD)
    value_rows = tile_at(index + 2 * H, HD)
    outer = r.grad_attended_t[rows, :]
    grads = dot_tn(r.projected_t[value_rows, :], outer)
    fetch(r, index).wait()
    chances = r.chances[index % 2]
    wide = chances.astype(F32)
    inner = jnp.sum(wide * grads, axis=0, keepdims=True)
    scores = (wide * (grads - inner)).astype(BF16)
    r.projected_t[value_rows, :] = dot_nt(outer, chances).astype(BF16)

    @pl.when(index + 2 < H)
    def _():
        fetch(r, index + 2).start()

    for head, target, grad in (
        (index, rows, dot_nn(r.turned_t[key_rows, :], scores)),
        (index + H, key_rows, dot_nt(r.turned_t[rows, :], scores)),
    ):
        unit, scale = head_norm(r.projected_t[target, :].astype(F32))
        outer_turned = turn_back(grad, r)
        weighted = outer_turned * unit
        total = jnp.sum(weighted, axis=1, keepdims=True)
        lanes = lax.broadcasted_iota(jnp.int32, (HD, 128), 1)
        r.head_gain_sums[...] += jnp.where(lanes == head, total, 0.0)
        inner_turned = outer_turned * gain_of(r, head)
        first = jnp.mean(inner_turned, axis=0, keepdims=True)
        second = jnp.mean(inner_turned * unit, axis=0, keepdims=True)
        r.projected_t[target, :] = (scale * (inner_turned - first - unit * second)).astype(BF16)


def head_sums(r):
    width = r.tokens.shape[1]
    sums = jnp.transpose(r.head_gain_sums[...])
    for head in range(2 * H):
        row = QUERY_GAIN if head < H else KEY_GAIN
        first = head % H * HD
        r.grad_small[row : row + 1, first : first + HD] = sums[head : head + 1, :]
    r.grad_qkv_bias[0:1, :] = dot_nt(r.ones[...], r.projected_t[...])[0:1]


def grad_hidden_in(r, index):
    rows = tile_at(index)
    r.grad_hidden[:, rows] = jnp.transpose(dot_nn(r.w_qkv[rows, :], r.projected_t[...]))


def weight_in(r, index):
    cols = tile_at(index)
    r.w_qkv[:, cols] = dot_nt(r.hidden_pre_t[...], r.projected_t[cols, :]).astype(BF16)


def norm_tokens_back(r):
    def store(where, value):
        r.grad_rows[where, :] = value.astype(BF16)

    gain, bias = norm_rows_back(r.tokens, r.grad_hidden, r.middle, r.small[PRE_GAIN : PRE_GAIN + 1, :], store)
    r.grad_small[PRE_GAIN : PRE_GAIN + 1, :] = gain
    r.grad_small[PRE_BIAS : PRE_BIAS + 1, :] = bias


class Refs:
    pass

MESH = pl.DeviceIdType.MESH
GROUPS = ("w_qkv", "w_out", "w_up", "w_down")
LINE = 4


class Place:
    def __init__(self):
        seq, fsdp = lax.axis_index("seq"), lax.axis_index("fsdp")
        self.seq, self.fsdp = seq, fsdp
        self.x, self.c = seq // 2, seq % 2
        self.z, self.y = fsdp // 2, fsdp % 2
        self.other_x, self.other_y, self.other_c = 1 - self.x, 1 - self.y, 1 - self.c
        self.line_slot = 32 + self.z
        x, c, z, y = self.x, self.c, self.z, self.y
        self.to = dict(
            core=(2 * x + 1 - c, fsdp),
            x=(2 * (1 - x) + c, fsdp),
            y=(seq, 2 * z + 1 - y),
        )
        high = z // 2
        low = z + high * (LINE - 1 - 2 * z)
        self.line = [z]
        for i in range(LINE - 1):
            other = (i + 1) - (low if i == 0 else 0)
            self.line.append(other + high * (LINE - 1 - 2 * other))
            self.to[i + 1] = (seq, self.line[i + 1] * 2 + y)


def push(source, target, to, send_sem, recv_sem):
    return pltpu.make_async_remote_copy(
        src_ref=source, dst_ref=target, send_sem=send_sem, recv_sem=recv_sem, device_id=to, device_id_type=MESH
    )


class Gather:
    def __init__(self, r, place, over_y):
        self.r, self.p, self.over_y = r, place, over_y
        self.sends = {g: [] for g in range(len(GROUPS))}
    def kinds(self):
        return [("z", o) for o in (1, 2, 3)] + [(k, o) for k in ("y", "x", "d") for o in range(LINE) if (k, o) != ("x", 0)]

    def have(self, g):
        for kind, o in self.kinds():
            self.from_core(g, kind, o)

    def piece(self, g, z, y, h, c):
        ref = getattr(self.r, GROUPS[g])
        shard, cols = ref.shape[0] // (2 * LINE), ref.shape[1] // 2
        rows = shard // 2
        first = pl.multiple_of((z * 2 + y) * shard + h * rows, 16)
        return ref.at[pl.ds(first, rows), pl.ds(pl.multiple_of(c * cols, 128), cols)]

    def ident(self, z, y, h):
        return (z * 2 + y) * 2 + h

    def start(self, *what):
        self.sends[what[0]].append(what)
        self.copy(*what).start()

    def copy(self, g, kind, o, to, z, y, h, recv):
        slot = dict(line=0, x1=4, y1=8, x2=12, y2=16, cz=20, cx=24, cy=28, cd=32)[kind] + o
        piece = self.piece(g, z, y, h, self.p.c)
        return push(piece, piece, self.p.to[to], self.r.gather_send.at[g, slot], recv.at[g, self.ident(z, y, h)])

    def wait(self, g, z, y, h, c, recv):
        piece = self.piece(g, z, y, h, c)
        push(piece, piece, self.p.to["core"], self.r.gather_send.at[g, 0], recv.at[g, self.ident(z, y, h)]).wait_recv()

    def own(self, g):
        p, recv = self.p, self.r.gather_recv
        pltpu.make_async_copy(getattr(self.r, GROUPS[g] + "_in"), self.shard(g), self.r.local_sems.at[g]).wait()
        self.start(g, "y1", 0, "y", p.z, p.y, p.x, recv)
        for o in range(1, LINE):
            self.start(g, "line", o, o, p.z, p.y, p.x, recv)
        if 0 in self.over_y[g]:
            self.start(g, "y2", 0, "y", p.z, p.y, p.other_x, recv)

    def shard(self, g):
        ref = getattr(self.r, GROUPS[g])
        rows = ref.shape[0] // (2 * LINE)
        return ref.at[pl.ds(pl.multiple_of(self.p.fsdp * rows, 16), rows), :]

    def from_line(self, g, o):
        p, recv = self.p, self.r.gather_recv
        z = p.line[o]
        self.wait(g, z, p.y, p.x, p.c, recv)
        self.start(g, "x1", o, "x", z, p.y, p.x, recv)
        self.start(g, "y1", o, "y", z, p.y, p.x, recv)
        self.start(g, "cz", o, "core", z, p.y, p.x, self.r.gather_core)

    def from_x(self, g, o):
        p, recv = self.p, self.r.gather_recv
        z = p.line[o]
        self.wait(g, z, p.y, p.other_x, p.c, recv)
        if o in self.over_y[g]:
            self.start(g, "y2", o, "y", z, p.y, p.other_x, recv)
        self.start(g, "cx", o, "core", z, p.y, p.other_x, self.r.gather_core)

    def from_y(self, g, o):
        p, recv = self.p, self.r.gather_recv
        z = p.line[o]
        self.wait(g, z, p.other_y, p.x, p.c, recv)
        if o not in self.over_y[g]:
            self.start(g, "x2", o, "x", z, p.other_y, p.x, recv)
        self.start(g, "cy", o, "core", z, p.other_y, p.x, self.r.gather_core)

    def from_corner(self, g, o):
        p = self.p
        z = p.line[o]
        self.wait(g, z, p.other_y, p.other_x, p.c, self.r.gather_recv)
        self.start(g, "cd", o, "core", z, p.other_y, p.other_x, self.r.gather_core)

    def from_core(self, g, kind, o):
        p = self.p
        y = p.y if kind in "zx" else p.other_y
        h = p.x if kind in "zy" else p.other_x
        self.wait(g, p.line[o], y, h, p.other_c, self.r.gather_core)

    def sent(self, g):
        for what in self.sends[g]:
            self.copy(*what).wait_send()


class Reduce:
    def __init__(self, r, place, over_y):
        self.r, self.p, self.over_y = r, place, over_y
        self.sends = []

    def rows_of(self, g):
        ref = getattr(self.r, GROUPS[g])
        return ref.shape[0] // (4 * LINE)

    def piece(self, g, z, y, h):
        ref = getattr(self.r, GROUPS[g])
        rows, cols = self.rows_of(g), ref.shape[1] // 2
        first = pl.multiple_of(((z * 2 + y) * 2 + h) * rows, 16)
        if g == 3:
            return self.r.own_down.at[pl.ds(first, rows), :]
        return ref.at[pl.ds(first, rows), pl.ds(pl.multiple_of(self.p.c * cols, 128), cols)]

    def spot(self, kind, o):
        p = self.p
        y = p.y if kind in "ox" else p.other_y
        h = p.x if kind in "oy" else p.other_x
        return p.line[o], y, h

    def from_core(self, g, kind, o):
        z, y, h = self.spot(kind, o)
        rows = self.rows_of(g)
        return getattr(self.r, "core_" + GROUPS[g]).at[pl.ds(pl.multiple_of(((z * 2 + y) * 2 + h) * rows, 16), rows), :]

    def box(self, g, kind, slot):
        return getattr(self.r, "box_" + GROUPS[g]).at[dict(corner=0, x=4, y=8, line=12)[kind] + slot]

    def send(self, g, what, to, slot, recv=None):
        self.sends.append((g, what, to, slot, recv))
        self.copy(g, what, to, slot, recv).start()

    def copy(self, g, what, to, slot, recv):
        source, target = what()
        return push(
            source, target, self.p.to[to], self.r.reduce_send.at[g, slot], self.r.reduce_recv.at[g, slot if recv is None else recv]
        )

    def arrive(self, g, target, slot):
        push(target, target, self.p.to["core"], self.r.reduce_send.at[g, 0], self.r.reduce_recv.at[g, slot]).wait_recv()

    def arrive_core(self, g, target, slot):
        if g < 3:
            self.arrive(g, target, slot)

    def add(self, target, *others):
        total = target[...].astype(F32)
        for other in others:
            total = total + other[...].astype(F32)
        target[...] = total.astype(BF16)

    def give(self, index, tile):
        slot = index % 2

        @pl.when(index >= 2)
        def _():
            self.given(index - 2).wait_send()

        self.r.stage[slot] = tile
        self.given(index).start()
        cols = self.r.own_down.shape[1]
        first = pl.multiple_of(self.p.c * cols, 128)
        self.r.own_down[tile_at(index), :] = self.r.stage[slot, :, pl.ds(first, cols)]

    def given(self, index):
        cols = self.r.own_down.shape[1]
        first = pl.multiple_of((self.p.other_c) * cols, 128)
        return push(
            self.r.stage.at[index % 2, :, pl.ds(first, cols)], self.r.core_w_down.at[tile_at(index), :], self.p.to["core"],
            self.r.stage_sems.at[index % 2], self.r.given_recv.at[index],
        )

    def all_given(self):
        tiles = self.r.own_down.shape[0] // TILE
        for index in (tiles - 2, tiles - 1):
            self.given(index).wait_send()
        for index in range(tiles):
            self.given(index).wait_recv()

    def begin(self, g):
        far = (3, 2, 1, 0)
        base = dict(d=0, y=4, x=8, o=12)
        if g == 3:
            self.all_given()
        for kind in "dyxo" if g < 3 else "":
            for o in far:
                self.send(g, functools.partial(self.across, g, kind, o), "core", base[kind] + o)

    def across(self, g, kind, o):
        ref = getattr(self.r, GROUPS[g])
        rows, cols = self.rows_of(g), ref.shape[1] // 2
        z, y, h = self.spot(kind, o)
        first = pl.multiple_of(((z * 2 + y) * 2 + h) * rows, 16)
        other = pl.multiple_of((self.p.other_c) * cols, 128)
        return ref.at[pl.ds(first, rows), pl.ds(other, cols)], self.from_core(g, kind, o)

    def boxed(self, g, kind, box, o):
        return self.piece(g, *self.spot(kind, o)), self.box(g, box, o)

    def corner(self, g, o):
        source = self.from_core(g, "d", o)
        self.arrive_core(g, source, o)
        piece = self.piece(g, *self.spot("d", o))
        self.add(piece, source)
        self.send(g, functools.partial(self.boxed, g, "d", "corner", o), "y" if o in self.over_y[g] else "x", 16 + o)

    def side(self, g, kind, o):
        source = self.from_core(g, kind, o)
        self.arrive_core(g, source, dict(y=4, x=8)[kind] + o)
        piece = self.piece(g, *self.spot(kind, o))
        if (o in self.over_y[g]) == (kind == "x"):
            box = self.box(g, "corner", o)
            self.arrive(g, box, 16 + o)
            self.add(piece, source, box)
        else:
            self.add(piece, source)
        self.send(g, functools.partial(self.boxed, g, kind, kind, o), kind, dict(y=20, x=24)[kind] + o)

    def centre(self, g, o):
        source, along_x, along_y = self.from_core(g, "o", o), self.box(g, "x", o), self.box(g, "y", o)
        self.arrive_core(g, source, 12 + o)
        self.arrive(g, along_y, 20 + o)
        self.arrive(g, along_x, 24 + o)
        self.add(self.piece(g, *self.spot("o", o)), source, along_x, along_y)

        if o:
            self.send(g, functools.partial(self.straight, g, o), o, 28 + o, self.p.line_slot)

    def straight(self, g, o):
        return self.piece(g, *self.spot("o", o)), self.box(g, "line", self.p.z)

    def collect(self, g, o):
        z = self.p.line[o]
        box = self.box(g, "line", z)
        self.arrive(g, box, 32 + z)
        self.add(self.piece(g, self.p.z, self.p.y, self.p.x), box)

    def quarter(self, g, x, c):
        ref = getattr(self.r, GROUPS[g] + "_grad")
        rows, cols = ref.shape[0] // 2, ref.shape[1] // 2
        return ref.at[pl.ds(pl.multiple_of(x * rows, 16), rows), pl.ds(pl.multiple_of(c * cols, 128), cols)]

    def share(self, g):
        p = self.p
        mine = self.quarter(g, p.x, p.c)
        mine[...] = self.piece(g, p.z, p.y, p.x)[...]
        for to, slot in (("x", 36), ("core", 37)):
            self.send(g, lambda: (self.quarter(g, p.x, p.c),) * 2, to, slot)

    def done(self, g):
        p = self.p
        other = self.quarter(g, p.other_x, p.c)
        self.arrive(g, other, 36)
        self.send(g, lambda: (self.quarter(g, p.other_x, p.c),) * 2, "core", 38)

    def finish(self):
        p = self.p
        for g in range(len(GROUPS)):
            self.arrive(g, self.quarter(g, p.x, p.other_c), 37)
            self.arrive(g, self.quarter(g, p.other_x, p.other_c), 38)
        for what in self.sends:
            self.copy(*what).wait_send()


def pack_small(r):
    peers = 2 * LINE
    width = r.tokens.shape[1]
    part = width // peers
    r.owners[...] = jnp.zeros(r.owners.shape, F32)
    for shard in range(peers):
        r.owners[shard, 0:8, 0:part] = r.grad_small[:, shard * part : (shard + 1) * part]
        for i in range(2):
            first = (shard * 2 + i) * part
            r.owners[shard, 8 + i : 9 + i, 0:part] = r.grad_qkv_bias[0:1, first : first + part]
        first = 2 * width + shard * part
        r.owners[shard, 10:11, 0:part] = r.grad_qkv_bias[0:1, first : first + part]
        for i in range(4):
            first = (shard * 4 + i) * part
            r.owners[shard, 11 + i : 12 + i, 0:part] = r.grad_up_bias[0:1, first : first + part]


def owner_copy(r, place, k, receive=False):
    other = (place.fsdp + k) % (2 * LINE)
    slot = other if receive else place.fsdp
    return push(
        r.owners.at[other], r.owned.at[slot], (place.seq, other), r.small_send.at[k], r.owned_recv.at[slot]
    )


def small_reduce_start(r, place):
    pack_small(r)
    lax.fori_loop(1, 2 * LINE, lambda k, carry: (owner_copy(r, place, k).start(), carry)[1], 0)


def small_reduce_middle(r, place):
    def receive(k, total):
        owner_copy(r, place, k, True).wait_recv()
        owner_copy(r, place, k).wait_send()
        return total + r.owned[(place.fsdp + k) % (2 * LINE)]

    r.shared[place.seq] = lax.fori_loop(1, 2 * LINE, receive, r.owners[place.fsdp])
    for k in range(1, 4):
        shared_copy(r, place, k).start()


def shared_copy(r, place, k, receive=False):
    other = (place.seq + k) % 4
    slot = other if receive else place.seq
    return push(
        r.shared.at[place.seq], r.shared.at[slot], (other, place.fsdp), r.shared_send.at[k], r.shared_recv.at[slot]
    )


def small_reduce_finish(r, place):
    for k in range(1, 4):
        shared_copy(r, place, k, True).wait_recv()
        shared_copy(r, place, k).wait_send()
    r.small_total[...] = r.shared[0] + r.shared[1] + r.shared[2] + r.shared[3]


class Home:
    def __init__(self, r, place, both, target, index):
        self.r, self.p, self.both, self.target, self.index = r, place, both, target, index
        rows = both.shape[0] // 2
        self.rows = both.at[pl.ds(pl.multiple_of(place.c * rows, 16), rows), :]

    def across(self, c):
        rows = self.both.shape[0] // 2
        part = self.both.at[pl.ds(pl.multiple_of(c * rows, 16), rows), :]
        return push(part, part, self.p.to["core"], self.r.home_send.at[self.index, 0], self.r.home_recv.at[self.index, 0])

    def along_x(self, x):
        send, recv = self.r.home_send, self.r.home_recv
        return push(
            self.r.leaving, self.target.at[x], self.p.to["x"], send.at[self.index, 1], recv.at[self.index, 1]
        )

    def start(self):
        self.across(self.p.c).start()

    def turn(self):
        self.across(self.p.other_c).wait_recv()
        ordered = dot_nn(self.r.place[...], self.both[...]).astype(BF16)
        half = ordered.shape[0] // 2
        self.r.leaving[...] = ordered[half:]
        self.along_x(self.p.x).start()
        self.target[self.p.x] = ordered[:half]

    def left(self):
        self.along_x(self.p.x).wait_send()

    def finish(self):
        self.along_x(self.p.other_x).wait_recv()
        self.across(self.p.c).wait_send()


def place_back(r, place):
    bundle, length = r.place.shape
    start = r.start[0:1, 0:1]
    quarter = length // 4

    def block(index):
        rows = tile_at(index, 128)
        shape = (128, length)
        mine = lax.broadcasted_iota(jnp.int32, shape, 0) + index * 128
        away = mine >= quarter
        mine = jnp.where(away, mine - quarter + quarter * (2 * (1 - place.x) + place.c), mine + quarter * (2 * place.x + place.c))
        source = mine.astype(F32) - start
        source = jnp.where(source < 0, source + length, source)
        here = lax.broadcasted_iota(jnp.int32, shape, 1).astype(F32)
        r.place[rows, :] = jnp.where(here == source, 1.0, 0.0).astype(BF16)

    loop(bundle // 128, block)


def greet(place):
    barrier = pltpu.get_barrier_semaphore()
    seq, fsdp = place.seq, place.fsdp
    peers = 2 * LINE

    def others(k, carry):
        pl.semaphore_signal(barrier, inc=1, device_id=(seq, (fsdp + k) % peers), device_id_type=MESH)
        return carry

    lax.fori_loop(1, peers, others, 0)
    for k in range(1, 4):
        pl.semaphore_signal(barrier, inc=1, device_id=((seq + k) % 4, fsdp), device_id_type=MESH)
    pl.semaphore_wait(barrier, peers + 2)


VECTORS = ("v0", "v1", "v2", "v3", "v4", "v5", "v6", "v7", "v8", "v9")


def pack_vectors(r):
    part = r.v0.shape[0]
    r.vector_rows[...] = jnp.zeros(r.vector_rows.shape, F32)
    row = 0
    for name in VECTORS:
        values = getattr(r, name)[...].astype(F32)
        for i in range(values.shape[0] // part):
            r.vector_rows[row : row + 1, 0:part] = values[i * part : (i + 1) * part].reshape(1, part)
            row += 1
    r.packed_in[...] = r.vector_rows[...].astype(BF16)


def small_send(r, place, k):
    peers = 2 * LINE
    other = (place.fsdp + k) % peers
    return push(
        r.packed_in, r.packed.at[place.fsdp], (place.seq, other), r.small_send.at[k], r.small_recv.at[place.fsdp]
    )


def small_start(r, place):
    lax.fori_loop(1, 2 * LINE, lambda k, carry: (small_send(r, place, k).start(), carry)[1], 0)
    r.packed[place.fsdp] = r.packed_in[...]


def small_finish(r, place):
    def receive(k, carry):
        other = (place.fsdp + k) % (2 * LINE)
        push(
            r.packed_in, r.packed.at[other], (place.seq, other), r.small_send.at[k], r.small_recv.at[other]
        ).wait_recv()
        small_send(r, place, k).wait_send()
        return carry

    lax.fori_loop(1, 2 * LINE, receive, 0)
    part = r.tokens.shape[1] // (2 * LINE)
    for shard in range(2 * LINE):
        rows = r.packed[shard].astype(F32)
        for i in range(8):
            r.small[i : i + 1, shard * part : (shard + 1) * part] = rows[i : i + 1, 0:part]
        for i in range(3):
            first = (shard * 3 + i) * part
            r.qkv_bias[0:1, first : first + part] = rows[8 + i : 9 + i, 0:part]
        for i in range(4):
            first = (shard * 4 + i) * part
            r.up_bias[0:1, first : first + part] = rows[11 + i : 12 + i, 0:part]


class Exchange:
    def __init__(self, r, place, source, target, index):
        self.p, self.target = place, target
        rows = target.shape[0] // 4
        p = place

        def quarter(x, c):
            return target.at[pl.ds(pl.multiple_of((2 * x + c) * rows, 16), rows), :]

        self.keep = pltpu.make_async_copy(source.at[p.x], quarter(p.x, p.c), r.local_sems.at[4 + index])
        send, recv = r.rows_send, r.rows_recv
        self.along_x = push(source.at[1 - p.x], quarter(p.x, p.c), p.to["x"], send.at[index, 0], recv.at[index, 0])
        self.own = push(source.at[p.x], quarter(p.x, p.c), p.to["core"], send.at[index, 1], recv.at[index, 1])
        passed = quarter(1 - p.x, p.c)
        self.passed = push(passed, passed, p.to["core"], send.at[index, 2], recv.at[index, 2])
        there = quarter(1 - p.x, p.c)
        self.arrive_x = push(there, there, p.to["x"], send.at[index, 0], recv.at[index, 0])
        one, two = quarter(p.x, 1 - p.c), quarter(1 - p.x, 1 - p.c)
        self.arrive = [
            push(one, one, p.to["core"], send.at[index, 1], recv.at[index, 1]),
            push(two, two, p.to["core"], send.at[index, 2], recv.at[index, 2]),
        ]

    def start(self):
        self.keep.start()
        self.along_x.start()
        self.own.start()

    def forward(self):
        self.arrive_x.wait_recv()
        self.passed.start()

    def finish(self):
        self.keep.wait()
        for copy in self.arrive:
            copy.wait_recv()
        for copy in (self.along_x, self.own, self.passed):
            copy.wait_send()


def collect_meta(r, place):
    r.meta_rows[...] = jnp.zeros(r.meta_rows.shape, F32)
    r.meta_rows[0:1, :] = r.segments[pl.ds(place.x, 1), :].astype(F32)
    for axis in range(2):
        r.meta_rows[1 + axis : 2 + axis, :] = r.positions[axis, pl.ds(place.x, 1), :].astype(F32)
    r.meta[...] = r.meta_rows[...].astype(BF16)


WEIGHTS = ("w_qkv", "w_out", "w_up", "w_down")


def spread_head_gains(r):
    columns = jnp.transpose(r.small[...])
    r.head_gain[...] = jnp.zeros(r.head_gain.shape, F32)
    r.head_gain_sums[...] = jnp.zeros(r.head_gain_sums.shape, F32)
    for head in range(2 * H):
        row = head % H * HD
        column = QUERY_GAIN if head < H else KEY_GAIN
        r.head_gain[:, head : head + 1] = columns[row : row + HD, column : column + 1]


TILES = dict(project=9, prepare=4, attend=12, branch=3, up=12, grad_before=12, down=3, grad_hidden_up=3, weight_up=12, out_back=3,
             attend_back=12, grad_hidden_in=3, weight_in=9)
ORDER = ("place", "vectors", "rows", "norm", "project", "prepare", "attend", "attended_rows", "branch", "norm_middle", "cotangent", "up",
         "grad_before", "down", "grad_hidden_up", "weight_up", "norm_middle_back", "out_back", "attend_back", "head_sums",
         "grad_hidden_in", "weight_in", "norm_tokens_back")


def place_rows(r, source, target):
    target[...] = dot_nn(r.place[...], source[...]).astype(BF16)


def computes(r, give):
    part = functools.partial

    def norm():
        rope_tables(r)
        norm_tokens(r)

    table = dict(
        place=part(place_tokens, r), vectors=part(spread_head_gains, r), rows=lambda: place_rows(r, r.seq_tokens, r.tokens),
        norm=norm, attended_rows=part(attended_rows, r), norm_middle=part(norm_middle, r),
        cotangent=lambda: place_rows(r, r.seq_cotangent, r.cotangent), norm_middle_back=part(norm_middle_back, r),
        head_sums=part(head_sums, r), norm_tokens_back=part(norm_tokens_back, r), up=part(up, r, give=give),
    )
    for function in (
        project, prepare, attend, branch, grad_before, down, grad_hidden_up, weight_up, out_back, attend_back, grad_hidden_in, weight_in
    ):
        table[function.__name__] = part(function, r)
    return table


def whole_kernel(names, *refs):
    r = Refs()
    for name, ref in zip(names, refs, strict=True):
        setattr(r, name, ref)
    r.result_rows, r.grad_rows = r.result, r.grad_result
    copies = [
        pltpu.make_async_copy(getattr(r, name + "_in"), getattr(r, name), r.local_sems.at[i]) for i, name in enumerate(WEIGHTS)
    ]
    for copy in copies:
        copy.start()
    r.ones[...] = jnp.ones(r.ones.shape, BF16)

    def out(index):
        return pltpu.make_async_copy(r.stage.at[index % 2], r.w_down_grad.at[tile_at(index), :], r.stage_sems.at[index % 2])

    def give(index, tile):
        @pl.when(index >= 2)
        def _():
            out(index - 2).wait()

        r.stage[index % 2] = tile
        out(index).start()

    for copy in copies:
        copy.wait()
    table = computes(r, give)
    for name in ORDER:
        if name == "attend_back":
            for index in (0, 1):
                fetch(r, index).start()
        if name in TILES:
            loop(TILES[name], table[name])
        else:
            table[name]()
    for index in range(2):
        out(index).wait()
    back = [pltpu.make_async_copy(getattr(r, name), getattr(r, name + "_grad"), r.local_sems.at[i]) for i, name in enumerate(WEIGHTS[:3])]
    for copy in back:
        copy.start()
    for copy in back:
        copy.wait()


SCHEDULE = (
    ("own", 0), ("tokens_start",), ("z", 0, 1), ("z", 0, 2), ("d", 0, 0), ("tokens_pass",), ("z", 0, 3), ("place",),
    ("small_have",), ("y", 0, 1), ("y", 0, 0), ("x", 0, 1), ("own", 1), ("x", 0, 2), ("vectors",), ("tokens_have",),
    ("y", 0, 2), ("x", 0, 3), ("y", 0, 3), ("rows",), ("norm",), ("d", 0, 1), ("d", 0, 2), ("own", 2), ("d", 0, 3), ("z", 1, 2),
    ("z", 1, 3), ("z", 1, 1), ("cotangent_start",), ("have", 0), ("project",), ("project",), ("project",), ("project",),
    ("project",), ("project",), ("project",), ("project",), ("project",), ("prepare",), ("y", 1, 3), ("z", 2, 1), ("prepare",),
    ("y", 1, 1), ("prepare",), ("y", 1, 2), ("own", 3), ("prepare",), ("attend",), ("attend",), ("x", 1, 1), ("attend",),
    ("attend",), ("attend",), ("attend",), ("z", 2, 3), ("z", 2, 2), ("d", 2, 0), ("attend",), ("attend",), ("d", 1, 3),
    ("x", 1, 2), ("attend",), ("d", 1, 0), ("y", 1, 0), ("d", 1, 2), ("d", 1, 1), ("attend",), ("x", 1, 3), ("attend",),
    ("z", 3, 1), ("attend",), ("attended_rows",), ("x", 2, 1), ("have", 1), ("branch",), ("cotangent_pass",), ("branch",),
    ("y", 2, 2), ("x", 2, 3), ("branch",), ("y", 2, 3), ("y", 3, 0), ("norm_middle",), ("y", 2, 1), ("y", 2, 0), ("y", 3, 1),
    ("x", 2, 2), ("x", 3, 1), ("d", 3, 0), ("cotangent_have",), ("cotangent",), ("z", 3, 3), ("d", 2, 1), ("place_back",),
    ("d", 2, 2), ("d", 2, 3), ("z", 3, 2), ("have", 2), ("up",), ("up",), ("up",), ("up",), ("x", 3, 3), ("up",), ("x", 3, 2),
    ("up",), ("y", 3, 3), ("d", 3, 1), ("up",), ("up",), ("up",), ("up",), ("d", 3, 3), ("d", 3, 2), ("up",), ("y", 3, 2),
    ("up",), ("begin", 3), ("have", 3), ("grad_before",), ("grad_before",), ("grad_before",), ("corner", 3, 3),
    ("grad_before",), ("grad_before",), ("grad_before",), ("grad_before",), ("grad_before",), ("side", 3, "y", 3),
    ("grad_before",), ("corner", 3, 0), ("grad_before",), ("grad_before",), ("grad_before",), ("grad_hidden_up",),
    ("side", 3, "x", 3), ("grad_hidden_up",), ("grad_hidden_up",), ("sent", 2), ("corner", 3, 2), ("weight_up",),
    ("weight_up",), ("weight_up",), ("weight_up",), ("weight_up",), ("side", 3, "y", 2), ("side", 3, "y", 1), ("weight_up",),
    ("corner", 3, 1), ("weight_up",), ("weight_up",), ("weight_up",), ("weight_up",), ("weight_up",), ("weight_up",),
    ("begin", 2), ("down",), ("down",), ("side", 3, "x", 2), ("down",), ("norm_middle_back",), ("corner", 2, 3),
    ("side", 2, "y", 3), ("sent", 1), ("fetch",), ("out_back",), ("corner", 2, 2), ("side", 3, "y", 0), ("out_back",),
    ("out_back",), ("begin", 1), ("centre", 3, 2), ("attend_back",), ("result_start",), ("side", 2, "y", 2),
    ("side", 3, "x", 0), ("side", 2, "x", 2), ("attend_back",), ("side", 3, "x", 1), ("attend_back",), ("attend_back",),
    ("attend_back",), ("side", 2, "y", 1), ("attend_back",), ("attend_back",), ("side", 1, "x", 1), ("corner", 2, 0),
    ("result_turn",), ("corner", 1, 0), ("attend_back",), ("attend_back",), ("corner", 2, 1), ("attend_back",),
    ("attend_back",), ("side", 2, "x", 3), ("centre", 3, 3), ("attend_back",), ("side", 1, "x", 0), ("corner", 1, 1),
    ("head_sums",), ("grad_hidden_in",), ("grad_hidden_in",), ("side", 2, "y", 0), ("grad_hidden_in",), ("side", 1, "x", 3),
    ("corner", 1, 2), ("sent", 0), ("side", 1, "x", 2), ("weight_in",), ("weight_in",), ("weight_in",), ("weight_in",),
    ("centre", 2, 2), ("weight_in",), ("weight_in",), ("corner", 1, 3), ("side", 2, "x", 0), ("weight_in",), ("weight_in",),
    ("weight_in",), ("begin", 0), ("side", 1, "y", 2), ("corner", 0, 3), ("centre", 2, 3), ("corner", 0, 2),
    ("side", 2, "x", 1), ("norm_tokens_back",), ("side", 0, "x", 3), ("grads_start",), ("corner", 0, 1), ("side", 0, "x", 2),
    ("small_start",), ("side", 1, "y", 1), ("side", 0, "y", 3), ("side", 1, "y", 3), ("grads_turn",), ("centre", 3, 1),
    ("collect", 3, 2), ("centre", 1, 2), ("collect", 2, 3), ("collect", 2, 2), ("side", 0, "y", 2), ("centre", 1, 3),
    ("corner", 0, 0), ("centre", 1, 1), ("centre", 2, 1), ("centre", 0, 3), ("centre", 3, 0), ("side", 0, "y", 1),
    ("side", 1, "y", 0), ("small_middle",), ("collect", 3, 3), ("side", 0, "x", 1), ("centre", 0, 2), ("side", 0, "x", 0),
    ("small_finish",), ("centre", 1, 0), ("side", 0, "y", 0), ("collect", 1, 3), ("collect", 3, 1), ("share", 3),
    ("centre", 0, 1), ("centre", 2, 0), ("collect", 1, 2), ("collect", 2, 1), ("collect", 1, 1), ("share", 2), ("centre", 0, 0),
    ("collect", 0, 3), ("share", 1), ("result_have",), ("collect", 0, 2), ("collect", 0, 1), ("share", 0), ("grads_have",),
    ("done", 2), ("grads_left",), ("done", 3), ("done", 1), ("done", 0), ("sent", 3), ("finish",),
)
GATHER_OVER_Y = ((0, 2), (0,), (0, 1), (0, 1, 2))
REDUCE_OVER_Y = ((0, 1, 2), (0,), (1, 3), (1, 2, 3))


def fused_kernel(names, *refs):
    r = Refs()
    for name, ref in zip(names, refs, strict=True):
        setattr(r, name, ref)
    place = Place()
    gather = Gather(r, place, dict(enumerate(GATHER_OVER_Y)))
    reduce = Reduce(r, place, dict(enumerate(REDUCE_OVER_Y)))
    for g, name in enumerate(WEIGHTS):
        pltpu.make_async_copy(getattr(r, name + "_in"), gather.shard(g), r.local_sems.at[g]).start()
    tokens = Exchange(r, place, r.tokens_in, r.seq_tokens, 0)
    cotangent = Exchange(r, place, r.cotangent_in, r.seq_cotangent, 1)
    result = Home(r, place, r.seq_tokens, r.result, 0)
    grads = Home(r, place, r.seq_cotangent, r.grad_result, 1)
    r.result_rows, r.grad_rows = result.rows, grads.rows
    pack_vectors(r)
    greet(place)
    small_start(r, place)
    r.ones[...] = jnp.ones(r.ones.shape, BF16)
    collect_meta(r, place)

    def fetch_first():
        for index in (0, 1):
            fetch(r, index).start()

    def grads_turn():
        result.left()
        grads.turn()

    plain = dict(
        own=gather.own, z=gather.from_line, x=gather.from_x, y=gather.from_y, d=gather.from_corner, have=gather.have, sent=gather.sent,
        tokens_start=tokens.start, tokens_pass=tokens.forward, tokens_have=tokens.finish,
        cotangent_start=cotangent.start, cotangent_pass=cotangent.forward, cotangent_have=cotangent.finish,
        small_have=functools.partial(small_finish, r, place), fetch=fetch_first,
        begin=reduce.begin, corner=reduce.corner, side=reduce.side, centre=reduce.centre, collect=reduce.collect, share=reduce.share,
        done=reduce.done, finish=reduce.finish,
        place_back=functools.partial(place_back, r, place), result_start=result.start, result_turn=result.turn,
        result_have=result.finish, grads_start=grads.start, grads_turn=grads_turn, grads_have=grads.finish, grads_left=grads.left,
        small_start=functools.partial(small_reduce_start, r, place), small_middle=functools.partial(small_reduce_middle, r, place),
        small_finish=functools.partial(small_reduce_finish, r, place),
    )
    table = computes(r, reduce.give)
    items = list(SCHEDULE)
    while items:
        name, *args = items.pop(0)
        if name in plain:
            plain[name](*args)
        elif name not in TILES:
            table[name]()
        else:
            between = {}
            tile = 0
            while tile < TILES[name] - 1:
                item = items.pop(0)
                if item[0] == name:
                    tile += 1
                else:
                    between.setdefault(tile, []).append(item)
            tiled_loop(TILES[name], table[name], between, plain)


def tiled_loop(count, body, between, plain):
    def step(index):
        body(index)
        for tile, todo in between.items():

            @pl.when(index == tile)
            def _():
                for name, *args in todo:
                    plain[name](*args)

    loop(count, step)


def layer(fused, tokens, cotangent, segments, positions, small, qkv_bias, up_bias, *weights):
    peers = 2 * LINE
    scale = peers if fused else 1
    width = tokens.shape[-1]
    length = segments.shape[1]
    bundle = length // 2
    hidden = weights[2].shape[1]
    shape = jax.ShapeDtypeStruct
    vmem = pl.BlockSpec(memory_space=pltpu.VMEM)
    hbm = pl.BlockSpec(memory_space=pl.ANY)
    inputs = {}
    if fused:
        inputs.update(
            tokens_in=(tokens, hbm),
            cotangent_in=(cotangent, hbm),
            segments=(segments, vmem),
            positions=(positions, vmem),
            **{name: (v, vmem) for name, v in zip(VECTORS, small)},
        )
    else:
        inputs.update(
            seq_tokens=(tokens, vmem),
            seq_cotangent=(cotangent, vmem),
            meta=(segments, vmem),
            small=(small, vmem),
            qkv_bias=(qkv_bias, vmem),
            up_bias=(up_bias, vmem),
        )
    full = [(w.shape[0] * scale, w.shape[1]) for w in weights]
    for name, w in zip(WEIGHTS, weights):
        inputs[name + "_in"] = (w, hbm)
    outputs = dict(
        result=(shape(tokens.shape if fused else (bundle, width), BF16), vmem),
        grad_result=(shape(tokens.shape if fused else (bundle, width), BF16), vmem),
        chances_kept=(shape((H, bundle, bundle), BF16), hbm),
    )
    scratch = {}
    vectors = dict(grad_small=(8, width), grad_qkv_bias=(8, 3 * width), grad_up_bias=(8, hidden))
    if fused:
        outputs["small_total"] = (shape((16, 128), F32), vmem)
        scratch.update({name: pltpu.VMEM(size, F32) for name, size in vectors.items()})
    else:
        outputs.update({name: (shape(size, F32), vmem) for name, size in vectors.items()})
    for name, size in zip(WEIGHTS, full):
        outputs[name + "_grad"] = (shape((size[0] // scale, size[1]), BF16), vmem if fused else hbm)
        scratch[name] = pltpu.VMEM(size, BF16)
    if fused:
        groups, pieces = len(WEIGHTS), 2 * peers
        scratch.update(
            seq_tokens=pltpu.VMEM((length, width), BF16),
            seq_cotangent=pltpu.VMEM((length, width), BF16),
            meta_rows=pltpu.VMEM((8, length), F32),
            meta=pltpu.VMEM((8, length), BF16),
            vector_rows=pltpu.VMEM((16, 128), F32),
            packed_in=pltpu.VMEM((16, 128), BF16),
            packed=pltpu.VMEM((peers, 16, 128), BF16),
            small=pltpu.VMEM((8, width), F32),
            qkv_bias=pltpu.VMEM((1, 3 * width), F32),
            up_bias=pltpu.VMEM((1, hidden), F32),
            small_send=pltpu.SemaphoreType.DMA((peers,)),
            small_recv=pltpu.SemaphoreType.DMA((peers,)),
            rows_send=pltpu.SemaphoreType.DMA((2, 3)),
            rows_recv=pltpu.SemaphoreType.DMA((2, 3)),
            gather_send=pltpu.SemaphoreType.DMA((groups, 36)),
            gather_recv=pltpu.SemaphoreType.DMA((groups, pieces)),
            gather_core=pltpu.SemaphoreType.DMA((groups, pieces)),
            own_down=pltpu.VMEM((hidden, width // 2), BF16),
            given_recv=pltpu.SemaphoreType.DMA((hidden // TILE,)),
            reduce_send=pltpu.SemaphoreType.DMA((groups, 40)),
            reduce_recv=pltpu.SemaphoreType.DMA((groups, 40)),
            home_send=pltpu.SemaphoreType.DMA((2, 2)),
            home_recv=pltpu.SemaphoreType.DMA((2, 2)),
            leaving=pltpu.VMEM((length // 4, width), BF16),
            owners=pltpu.VMEM((peers, 16, 128), F32),
            owned=pltpu.VMEM((peers, 16, 128), F32),
            owned_recv=pltpu.SemaphoreType.DMA((peers,)),
            shared=pltpu.VMEM((4, 16, 128), F32),
            shared_send=pltpu.SemaphoreType.DMA((4,)),
            shared_recv=pltpu.SemaphoreType.DMA((4,)),
        )
        for name, size in zip(WEIGHTS, full):
            scratch["core_" + name] = pltpu.VMEM((size[0], size[1] // 2), BF16)
            scratch["box_" + name] = pltpu.VMEM((16, size[0] // (2 * peers), size[1] // 2), BF16)
    scratch.update(
        local_sems=pltpu.SemaphoreType.DMA((8,)),
        ones=pltpu.VMEM((8, bundle), BF16),
        start=pltpu.VMEM((8, 128), F32),
        place=pltpu.VMEM((bundle, length), BF16),
        marks_row=pltpu.VMEM((8, bundle), F32),
        marks_col=pltpu.VMEM((bundle, 8), F32),
        cosine=pltpu.VMEM((2, HD // 4, bundle), F32),
        sine=pltpu.VMEM((2, HD // 4, bundle), F32),
        head_gain=pltpu.VMEM((HD, 128), F32),
        head_gain_sums=pltpu.VMEM((HD, 128), F32),
        tokens=pltpu.VMEM((bundle, width), BF16),
        cotangent=pltpu.VMEM((bundle, width), BF16),
        hidden_pre_t=pltpu.VMEM((width, bundle), BF16),
        projected_t=pltpu.VMEM((3 * width, bundle), BF16),
        turned_t=pltpu.VMEM((2 * width, bundle), BF16),
        chances=pltpu.VMEM((2, bundle, bundle), BF16),
        chance_sems=pltpu.SemaphoreType.DMA((2,)),
        attended_t=pltpu.VMEM((width, bundle), BF16),
        middle=pltpu.VMEM((bundle, width), F32),
        hidden_mlp_t=pltpu.VMEM((width, bundle), BF16),
        before=pltpu.VMEM((bundle, TILE), F32),
        active=pltpu.VMEM((bundle, hidden), BF16),
        stage=pltpu.VMEM((2, TILE, width), BF16),
        stage_sems=pltpu.SemaphoreType.DMA((2,)),
        slope=pltpu.VMEM((bundle, hidden), BF16),
        grad_hidden=pltpu.VMEM((bundle, width), F32),
        rows=pltpu.VMEM((bundle, width), BF16),
        grad_attended_t=pltpu.VMEM((width, bundle), BF16),
    )
    names = tuple(inputs) + tuple(outputs) + tuple(scratch)
    params = dict(vmem_limit_bytes=63 << 20)
    if fused:
        params.update(collective_id=0, has_side_effects=True)
    return pl.pallas_call(
        functools.partial(fused_kernel if fused else whole_kernel, names),
        out_shape=tuple(o[0] for o in outputs.values()),
        in_specs=[i[1] for i in inputs.values()],
        out_specs=tuple(o[1] for o in outputs.values()),
        scratch_shapes=list(scratch.values()),
        compiler_params=pltpu.CompilerParams(**params),
        name="layer",
    )(*(i[0] for i in inputs.values()))


def finish_kernel(part, result, grad_result, small, *refs):
    weights, outs = refs[:4], refs[4:]
    outs[0][...] = result[...]
    outs[1][...] = grad_result[...]
    for source, target in zip(weights, outs[2:6]):
        target[...] = source[...].astype(F32)
    for target, first, count in zip(outs[6:], (0, 1, 2, 3, 4, 5, 6, 7, 8, 10, 11), (1,) * 8 + (2, 1, 4)):
        for i in range(count):
            target[i * part : (i + 1) * part] = small[first + i : first + i + 1, 0:part].reshape(part)


def finish(part, result, grad_result, small, *weights):
    shape = jax.ShapeDtypeStruct
    vmem = pl.BlockSpec(memory_space=pltpu.VMEM)
    outs = [shape(result.shape, BF16), shape(grad_result.shape, BF16)] + [shape(w.shape, F32) for w in weights]
    outs += [shape((part * count,), F32) for count in (1,) * 8 + (2, 1, 4)]
    return pl.pallas_call(
        functools.partial(finish_kernel, part),
        out_shape=tuple(outs),
        in_specs=[vmem] * 7,
        out_specs=tuple([vmem] * len(outs)),
        compiler_params=pltpu.CompilerParams(vmem_limit_bytes=63 << 20),
        name="finish",
    )(result, grad_result, small, *weights)


def shards(
    tokens,
    pre_gain,
    pre_bias,
    query_key_value_weight,
    query_key_value_bias,
    query_gain,
    key_gain,
    output_weight,
    output_bias,
    mlp_gain,
    mlp_bias,
    up_matrix_weight,
    up_offset_bias,
    down_matrix_weight,
    down_offset_bias,
    segments,
    positions,
    cotangent,
):
    rank = lax.axis_index("seq")
    x = rank // 2
    width = tokens.shape[2]
    length = segments.shape[1]
    fsdp = lax.axis_size("fsdp")
    part = width // fsdp
    weights_in = (query_key_value_weight, output_weight, up_matrix_weight, down_matrix_weight)
    vectors = (
        pre_gain, pre_bias, query_gain, key_gain, output_bias, mlp_gain, mlp_bias, down_offset_bias,
        query_key_value_bias, up_offset_bias,
    )
    if fsdp == 2 * LINE:
        result, grad_result, _, small_total, *weight_grads = layer(
            True, tokens, cotangent, segments, positions, vectors, None, None, *weights_in
        )
        result, grad_result, g0, g1, g2, g3, *v = finish(part, result, grad_result, small_total, *weight_grads)
        return (
            result, grad_result, v[PRE_GAIN], v[PRE_BIAS], g0, v[8], v[9], v[QUERY_GAIN], v[KEY_GAIN], g1, v[OUT_BIAS],
            v[MLP_GAIN], v[MLP_BIAS], g2, v[10], g3, v[DOWN_BIAS],
        )
    else:
        gather = functools.partial(lax.all_gather, axis_name="fsdp", axis=0, tiled=True)
        packed = gather(jnp.concatenate(vectors)[None]).astype(F32)
        small = jnp.stack([packed[:, i * part : (i + 1) * part].reshape(width) for i in range(8)])
        qkv_bias = packed[:, 8 * part : 11 * part].reshape(1, 3 * width)
        up_bias = packed[:, 11 * part :].reshape(1, -1)
        seq_tokens = lax.dynamic_index_in_dim(lax.all_gather(tokens, "seq", axis=1, tiled=True), x, 0, False)
        seq_cotangent = lax.dynamic_index_in_dim(lax.all_gather(cotangent, "seq", axis=1, tiled=True), x, 0, False)
        labels = lax.dynamic_index_in_dim(segments, x, 0, True)
        places = lax.dynamic_index_in_dim(positions, x, 1, False)
        meta = jnp.concatenate([labels, places, jnp.zeros((5, length), jnp.int32)], axis=0).astype(BF16)
        results = layer(False, seq_tokens, seq_cotangent, meta, None, small, qkv_bias, up_bias, *map(gather, weights_in))
    result, grad_result, _, grad_small, grad_qkv_bias, grad_up_bias, *weight_grads = results
    counts = jnp.stack([jnp.sum(segments == v, axis=1) for v in range(4)])
    first = jnp.argmax(counts == length // 2, axis=0)
    starts = jnp.sum(segments < first[:, None], axis=1)

    def home(bundle):
        every = lax.all_gather(bundle, "seq").reshape(2, length, width)
        own = rank * (length // 4) + jnp.arange(length // 4)
        index = (own[None] - starts[:, None]) % length
        return jnp.take_along_axis(every, index[..., None], axis=1)

    scatter = functools.partial(lax.psum_scatter, axis_name="fsdp", scatter_dimension=0, tiled=True)

    def total_of(grad):
        return lax.psum(scatter(grad).astype(BF16), "seq").astype(F32)

    weights = [total_of(g) for g in weight_grads]
    pieces = [grad_small[i].reshape(fsdp, part) for i in range(8)]
    pieces += [grad_qkv_bias[0, : 2 * width].reshape(fsdp, -1), grad_qkv_bias[0, 2 * width :].reshape(fsdp, -1)]
    pieces += [grad_up_bias[0].reshape(fsdp, -1)]
    total = lax.psum(scatter(jnp.concatenate(pieces, axis=1)), "seq")[0]
    s = [total[i * part : (i + 1) * part] for i in range(8)]
    query_key_bias, value_bias, up_total = total[8 * part : 10 * part], total[10 * part : 11 * part], total[11 * part :]
    return (
        home(result), home(grad_result), s[PRE_GAIN], s[PRE_BIAS], weights[0], query_key_bias, value_bias,
        s[QUERY_GAIN], s[KEY_GAIN], weights[1], s[OUT_BIAS], s[MLP_GAIN], s[MLP_BIAS], weights[2], up_total,
        weights[3], s[DOWN_BIAS],
    )


def solution(mesh):
    rows, matrix, activations = P("fsdp"), P("fsdp", None), P("fsdp", "seq", None)
    placed = (
        activations, rows, rows, matrix, rows, rows, rows, matrix, rows, rows, rows, matrix, rows, matrix, rows,
        P("fsdp", None), P(None, "fsdp", None), activations,
    )
    given = (
        activations, activations, rows, rows, matrix, rows, rows, rows, rows, matrix, rows, rows, rows, matrix, rows,
        matrix, rows,
    )
    return jax.shard_map(shards, mesh=mesh, in_specs=placed, out_specs=given, check_vma=False)
```

```python
import functools

import jax
import jax.numpy as jnp
from jax import lax
from jax.experimental import pallas as pl
from jax.experimental.pallas import tpu as pltpu
from jax.sharding import PartitionSpec as P

H = 12
HD = 64
EPSILON = 1e-06
MASK = 128.0
ROPE_BASE = 100.0
F32 = jnp.float32
BF16 = jnp.bfloat16
TILE = 256
UP_TILE = 512


def dot_nn(a, b):
    return lax.dot_general(a, b, (((1,), (0,)), ((), ())), preferred_element_type=F32)


def dot_nt(a, b):
    return lax.dot_general(a, b, (((1,), (1,)), ((), ())), preferred_element_type=F32)


def dot_tn(a, b):
    return lax.dot_general(a, b, (((0,), (0,)), ((), ())), preferred_element_type=F32)


def tile_at(index, size=TILE):
    return pl.ds(pl.multiple_of(index * size, size), size)


def loop(count, body, first=0):
    def step(index, carry):
        body(index)
        return carry

    lax.fori_loop(first, first + count, step, 0)


def rows_sum(block):
    rows, width = block.shape
    return jnp.sum(block.reshape(rows // 8, 8, width), axis=0)


def column_sums_exact(ones, block):
    return dot_nn(ones, block)[0:1]


def place_tokens(r):
    bundle, length = r.place.shape
    labels = r.meta[0:1, :].astype(F32)
    start = jnp.zeros((1, 1), F32)
    found = jnp.zeros((1, 1), F32)
    for value in range(4):
        here = jnp.sum(jnp.where(labels == value, 1.0, 0.0), axis=1, keepdims=True)
        below = jnp.sum(jnp.where(labels < value, 1.0, 0.0), axis=1, keepdims=True)
        hit = jnp.where(here == bundle, 1.0, 0.0) * (1.0 - found)
        start = start + hit * below
        found = found + hit
    r.start[...] = jnp.broadcast_to(start, r.start.shape)
    core = lax.axis_index("seq") % 2

    def block(index):
        rows = tile_at(index, 128)
        shape = (128, length)
        mine = lax.broadcasted_iota(jnp.int32, shape, 0) + (index * 128 + core * bundle)
        target = mine.astype(F32) + start
        target = jnp.where(target >= length, target - length, target)
        source = lax.broadcasted_iota(jnp.int32, shape, 1).astype(F32)
        r.place[rows, :] = jnp.where(source == target, 1.0, 0.0).astype(BF16)

    loop(bundle // 128, block)
    r.marks_row[...] = dot_nt(r.meta[...], r.place[...])


def mask_channels(r):
    rows = lax.broadcasted_iota(jnp.int32, r.mask_keys.shape, 0).astype(F32)
    same = jnp.where(rows == r.marks_row[0:1, :], 1.0, 0.0)
    r.mask_keys[...] = jnp.where(rows == 4.0, 1.0, same).astype(BF16)
    r.mask_queries[...] = jnp.where(rows == 4.0, -MASK, same * MASK).astype(BF16)


def rope_tables(r):
    quarter = HD // 4
    bundle = r.cosine.shape[-1]
    step = lax.broadcasted_iota(jnp.int32, (quarter, bundle), 0).astype(F32)
    frequency = jnp.exp(step * (-jnp.log(jnp.float32(ROPE_BASE)) / quarter))
    for axis in range(2):
        angle = r.marks_row[1 + axis : 2 + axis, :] * frequency
        r.cosine[axis] = jnp.cos(angle)
        r.sine[axis] = jnp.sin(angle)


def normalized(block):
    mean = jnp.mean(block, axis=-1, keepdims=True)
    centred = block - mean
    scale = lax.rsqrt(jnp.mean(centred * centred, axis=-1, keepdims=True) + EPSILON)
    return centred * scale, scale


def norm_rows(source, gain, bias, target, rows=128):
    def block(index):
        where = tile_at(index, rows)
        unit, _ = normalized(source[where, :].astype(F32))
        target[where, :] = (unit * gain + bias).astype(target.dtype)

    loop(source.shape[0] // rows, block)


def norm_rows_back(source, grads, base, gain, store, rows=128):
    width = source.shape[1]

    def block(index, carry):
        gain_sum, bias_sum = carry
        where = tile_at(index, rows)
        unit, scale = normalized(source[where, :].astype(F32))
        outer = grads[where, :]
        inner = outer * gain
        first = jnp.mean(inner, axis=-1, keepdims=True)
        second = jnp.mean(inner * unit, axis=-1, keepdims=True)
        store(where, base[where, :].astype(F32) + scale * (inner - first - unit * second))
        return gain_sum + rows_sum(outer * unit), bias_sum + rows_sum(outer)

    zero = jnp.zeros((8, width), F32)
    gain_sum, bias_sum = lax.fori_loop(0, source.shape[0] // rows, block, (zero, zero))
    return jnp.sum(gain_sum, axis=0, keepdims=True), jnp.sum(bias_sum, axis=0, keepdims=True)


def transpose_into(target, source):
    def block(index):
        where = tile_at(index, 128)
        target[where, :] = jnp.transpose(source[:, where])

    loop(source.shape[1] // 128, block)


def head_norm(vectors):
    mean = jnp.mean(vectors, axis=0, keepdims=True)
    centred = vectors - mean
    scale = lax.rsqrt(jnp.mean(centred * centred, axis=0, keepdims=True) + EPSILON)
    return centred * scale, scale


def turn(vectors, r):
    q = HD // 4
    out = []
    for axis in range(2):
        one, two = vectors[2 * axis * q : (2 * axis + 1) * q], vectors[(2 * axis + 1) * q : (2 * axis + 2) * q]
        cosine, sine = r.cosine[axis], r.sine[axis]
        out.append(one * cosine - two * sine)
        out.append(two * cosine + one * sine)
    return jnp.concatenate(out, axis=0) * HD ** (-0.5)


def turn_back(vectors, r):
    q = HD // 4
    out = []
    for axis in range(2):
        one, two = vectors[2 * axis * q : (2 * axis + 1) * q], vectors[(2 * axis + 1) * q : (2 * axis + 2) * q]
        cosine, sine = r.cosine[axis], r.sine[axis]
        out.append(one * cosine + two * sine)
        out.append(two * cosine - one * sine)
    return jnp.concatenate(out, axis=0) * HD ** (-0.5)


PRE_GAIN, PRE_BIAS, QUERY_GAIN, KEY_GAIN, OUT_BIAS, MLP_GAIN, MLP_BIAS, DOWN_BIAS = range(8)


def gain_of(r, head):
    lanes = lax.broadcasted_iota(jnp.int32, (HD, 128), 1)
    return jnp.sum(jnp.where(lanes == head, r.head_gain[...], 0.0), axis=1, keepdims=True)


def spill(r, index):
    return pltpu.make_async_copy(r.chances.at[index % 2], r.chances_kept.at[index], r.chance_sems.at[index % 2])


def fetch(r, index):
    return pltpu.make_async_copy(r.chances_kept.at[index], r.chances.at[index % 2], r.chance_sems.at[index % 2])


def norm_tokens(r):
    norm_rows(r.tokens, r.small[PRE_GAIN : PRE_GAIN + 1, :], r.small[PRE_BIAS : PRE_BIAS + 1, :], r.rows)
    transpose_into(r.hidden_pre_t, r.rows)


def project(r, index):
    cols = tile_at(index, H // 2 * HD)
    part = dot_nn(r.rows[...], r.w_qkv[:, cols]) + r.qkv_bias[0:1, cols]
    r.projected_t[cols, :] = jnp.transpose(part.astype(BF16))

    def head(which):
        rows = tile_at(which, HD)
        unit, _ = head_norm(r.projected_t[rows, :].astype(F32))
        r.turned_t[rows, :] = turn(unit * gain_of(r, which), r).astype(BF16)

    @pl.when(index < 4)
    def _():
        loop(H // 2, head, index * (H // 2))


def attend(r, index):
    rows = tile_at(index, HD)
    key_rows = tile_at(index + H, HD)
    value_rows = tile_at(index + 2 * H, HD)
    slot = index % 2

    @pl.when(index >= 2)
    def _():
        spill(r, index - 2).wait()

    keys = jnp.concatenate([r.turned_t[key_rows, :], r.mask_keys[...]], axis=0)
    queries = jnp.concatenate([r.turned_t[rows, :], r.mask_queries[...]], axis=0)
    raised = jnp.exp(dot_tn(keys, queries))
    share = 1.0 / jnp.sum(raised, axis=0, keepdims=True)
    low = raised.astype(BF16)
    r.chances[slot] = low
    spill(r, index).start()
    r.shares[pl.ds(index, 1)] = share.reshape(1, 1, -1)
    r.attended_t[rows, :] = (dot_nn(r.projected_t[value_rows, :], low) * share).astype(BF16)


def attended_rows(r):
    for index in (H - 2, H - 1):
        spill(r, index).wait()
    transpose_into_rows(r.rows, r.attended_t)


def transpose_into_rows(target, source):
    def block(index):
        where = tile_at(index, 128)
        target[:, where] = jnp.transpose(source[where, :])

    loop(source.shape[0] // 128, block)


def branch(r, index):
    cols = tile_at(index)
    part = dot_nn(r.rows[...], r.w_out[:, cols]) + r.small[OUT_BIAS : OUT_BIAS + 1, cols]
    r.middle[:, cols] = r.tokens[:, cols].astype(F32) + part


def norm_middle(r):
    norm_rows(r.middle, r.small[MLP_GAIN : MLP_GAIN + 1, :], r.small[MLP_BIAS : MLP_BIAS + 1, :], r.rows)
    transpose_into(r.hidden_mlp_t, r.rows)


def up(r, index, give):
    cols = tile_at(index, UP_TILE)
    before = r.grad_hidden.at[:, pl.ds(0, UP_TILE)]
    before[...] = dot_nn(r.rows[...], r.w_up[:, cols]) + r.up_bias[0:1, cols]

    def activate(part):
        rows = tile_at(part, 64)
        v = before[rows, :]
        half = 0.5 + 0.5 * lax.erf(v * 0.7071067811865476)
        r.active[rows, cols] = (v * half).astype(BF16)
        r.slope[rows, cols] = (half + v * (jnp.exp(-0.5 * v * v) * 0.3989422804014327)).astype(BF16)

    loop(before.shape[0] // 64, activate)
    give(index, dot_nn(jnp.transpose(r.active[:, cols]), r.cotangent[...]).astype(BF16))


def down(r, index):
    cols = tile_at(index)
    part = dot_nn(r.active[...], r.w_down[:, cols]) + r.small[DOWN_BIAS : DOWN_BIAS + 1, cols]
    r.result_rows[:, cols] = (r.middle[:, cols] + part).astype(BF16)


def grad_before(r, index):
    rows = tile_at(index, 512)
    grads = dot_nt(r.cotangent[...], r.w_down[rows, :]) * r.slope[:, rows].astype(F32)
    r.slope[:, rows] = grads.astype(BF16)
    r.grad_up_bias[0:1, rows] = jnp.sum(rows_sum(grads), axis=0, keepdims=True)


def grad_hidden_up(r, index):
    cols = tile_at(index)
    r.grad_hidden[:, cols] = dot_nt(r.slope[...], r.w_up[cols, :])


def weight_up(r, index):
    cols = tile_at(index, 512)
    r.w_up[:, cols] = dot_nn(r.hidden_mlp_t[...], r.slope[:, cols]).astype(BF16)


def norm_middle_back(r):
    def store(where, value):
        r.middle[where, :] = value
        r.rows[where, :] = value.astype(BF16)

    gain, bias = norm_rows_back(r.middle, r.grad_hidden, r.cotangent, r.small[MLP_GAIN : MLP_GAIN + 1, :], store)
    r.grad_small[MLP_GAIN : MLP_GAIN + 1, :] = gain
    r.grad_small[MLP_BIAS : MLP_BIAS + 1, :] = bias
    r.grad_small[OUT_BIAS : OUT_BIAS + 1, :] = column_sums_exact(r.ones[...], r.rows[...])
    r.grad_small[DOWN_BIAS : DOWN_BIAS + 1, :] = column_sums_exact(r.ones[...], r.cotangent[...])


def out_back(r, index):
    rows = tile_at(index)
    r.grad_attended_t[rows, :] = dot_nt(r.w_out[rows, :], r.rows[...]).astype(BF16)
    r.w_out[rows, :] = dot_nn(r.attended_t[rows, :], r.rows[...]).astype(BF16)


def attend_back(r, index):
    rows = tile_at(index, HD)
    key_rows = tile_at(index + H, HD)
    value_rows = tile_at(index + 2 * H, HD)
    share = r.shares[pl.ds(index, 1)].reshape(1, -1)
    outer = (r.grad_attended_t[rows, :].astype(F32) * share).astype(BF16)
    grads = dot_tn(r.projected_t[value_rows, :], outer)
    fetch(r, index).wait()
    chances = r.chances[index % 2]
    wide = chances.astype(F32)
    inner = jnp.sum(wide * grads, axis=0, keepdims=True) * share
    scores = (wide * (grads - inner)).astype(BF16)
    r.projected_t[value_rows, :] = dot_nt(outer, chances).astype(BF16)

    @pl.when(index + 2 < H)
    def _():
        fetch(r, index + 2).start()

    for head, target, grad in (
        (index, rows, dot_nn(r.turned_t[key_rows, :], scores)),
        (index + H, key_rows, dot_nt(r.turned_t[rows, :], scores)),
    ):
        unit, scale = head_norm(r.projected_t[target, :].astype(F32))
        outer_turned = turn_back(grad, r)
        weighted = outer_turned * unit
        total = jnp.sum(weighted, axis=1, keepdims=True)
        lanes = lax.broadcasted_iota(jnp.int32, (HD, 128), 1)
        r.head_gain_sums[...] += jnp.where(lanes == head, total, 0.0)
        inner_turned = outer_turned * gain_of(r, head)
        first = jnp.mean(inner_turned, axis=0, keepdims=True)
        second = jnp.mean(inner_turned * unit, axis=0, keepdims=True)
        r.projected_t[target, :] = (scale * (inner_turned - first - unit * second)).astype(BF16)


def head_sums(r):
    width = r.tokens.shape[1]
    sums = jnp.transpose(r.head_gain_sums[...])
    for head in range(2 * H):
        row = QUERY_GAIN if head < H else KEY_GAIN
        first = head % H * HD
        r.grad_small[row : row + 1, first : first + HD] = sums[head : head + 1, :]
    r.grad_qkv_bias[0:1, :] = dot_nt(r.ones[...], r.projected_t[...])[0:1]


def grad_hidden_in(r, index):
    rows = tile_at(index)
    r.grad_hidden[:, rows] = jnp.transpose(dot_nn(r.w_qkv[rows, :], r.projected_t[...]))


def weight_in(r, third):
    width = r.tokens.shape[1]
    part = width // 6
    rows = [
        r.projected_t[block * width + (2 * third + half) * part : block * width + (2 * third + half + 1) * part, :]
        for half in range(2)
        for block in range(3)
    ]
    columns = jnp.concatenate(rows, axis=0)

    def block(index):
        part = dot_nt(r.hidden_pre_t[tile_at(index), :], columns)
        r.w_down[pl.ds(pl.multiple_of(third * width + index * TILE, TILE), TILE), :] = part.astype(BF16)

    loop(width // TILE, block)


def norm_tokens_back(r):
    def store(where, value):
        r.grad_rows[where, :] = value.astype(BF16)

    gain, bias = norm_rows_back(r.tokens, r.grad_hidden, r.middle, r.small[PRE_GAIN : PRE_GAIN + 1, :], store)
    r.grad_small[PRE_GAIN : PRE_GAIN + 1, :] = gain
    r.grad_small[PRE_BIAS : PRE_BIAS + 1, :] = bias


class Refs:
    pass

MESH = pl.DeviceIdType.MESH
GATHERED = (("w_qkv", 0, 1), ("w_qkv", 1, 1), ("w_qkv", 2, 1), ("w_out", 0, 1), ("w_up", 0, 4), ("w_down", 0, 1))
REDUCED = ("third0", "third1", "third2", "w_out", "w_up", "w_down")
LINE = 4


class Place:
    def __init__(self):
        seq, fsdp = lax.axis_index("seq"), lax.axis_index("fsdp")
        self.seq, self.fsdp = seq, fsdp
        self.x, self.c = seq // 2, seq % 2
        self.z, self.y = fsdp // 2, fsdp % 2
        self.other_x, self.other_y, self.other_c = 1 - self.x, 1 - self.y, 1 - self.c
        self.line_slot, self.other_slot = 32 + self.z, 24 + self.z
        x, c, z, y = self.x, self.c, self.z, self.y
        self.to = dict(
            core=(2 * x + 1 - c, fsdp),
            x=(2 * (1 - x) + c, fsdp),
            y=(seq, 2 * z + 1 - y),
        )
        high = z // 2
        low = z + high * (LINE - 1 - 2 * z)
        self.line = [z]
        for i in range(LINE - 1):
            other = (i + 1) - (low if i == 0 else 0)
            self.line.append(other + high * (LINE - 1 - 2 * other))
            self.to[i + 1] = (seq, self.line[i + 1] * 2 + y)


def push(source, target, to, send_sem, recv_sem):
    return pltpu.make_async_remote_copy(
        src_ref=source, dst_ref=target, send_sem=send_sem, recv_sem=recv_sem, device_id=to, device_id_type=MESH
    )


class Gather:
    def __init__(self, r, place, over_y, wide):
        self.r, self.p, self.over_y, self.wide = r, place, over_y, wide
        self.sends = {g: [] for g in range(len(GATHERED))}
    def kinds(self):
        return [("z", o) for o in (1, 2, 3)] + [(k, o) for k in ("y", "x", "d") for o in range(LINE) if (k, o) != ("x", 0)]

    def have(self, g):
        for kind, o in self.kinds():
            self.from_core(g, kind, o)

    def piece(self, g, z, y, h, c):
        name, column, count = GATHERED[g]
        ref, width = getattr(self.r, name), self.r.tokens.shape[1]
        shard, cols = ref.shape[0] // (2 * LINE), count * width // 2
        rows = shard // 2
        first = pl.multiple_of((z * 2 + y) * shard, 16) if h is None else pl.multiple_of((z * 2 + y) * shard + h * rows, 16)
        rows = shard if h is None else rows
        return ref.at[pl.ds(first, rows), pl.ds(pl.multiple_of(column * width + c * cols, 128), cols)]

    def ident(self, z, y, h):
        return (z * 2 + y) * 2 + (self.p.x if h is None else h)

    def start(self, *what):
        self.sends[what[0]].append(what)
        self.copy(*what).start()

    def copy(self, g, kind, o, to, z, y, h, recv):
        slot = dict(line=0, x1=4, y1=8, x2=12, y2=16, cz=20, cx=24, cy=28, cd=32)[kind] + o
        piece = self.piece(g, z, y, h, self.p.c)
        return push(piece, piece, self.p.to[to], self.r.gather_send.at[g, slot], recv.at[g, self.ident(z, y, h)])

    def wait(self, g, z, y, h, c, recv):
        piece = self.piece(g, z, y, h, c)
        push(piece, piece, self.p.to["core"], self.r.gather_send.at[g, 0], recv.at[g, self.ident(z, y, h)]).wait_recv()

    def own(self, g):
        p, recv = self.p, self.r.gather_recv
        self.load(g).wait()
        self.start(g, "y1", 0, "y", p.z, p.y, p.x, recv)
        for o in range(1, LINE):
            self.start(g, "line", o, o, p.z, p.y, None if g in self.wide else p.x, recv)
        if 0 in self.over_y[g]:
            self.start(g, "y2", 0, "y", p.z, p.y, p.other_x, recv)

    def load(self, g):
        name, column, count = GATHERED[g]
        ref, width = getattr(self.r, name), self.r.tokens.shape[1]
        rows = ref.shape[0] // (2 * LINE)
        cols = pl.ds(column * width, count * width)
        first = pl.multiple_of(self.p.fsdp * rows, 16)
        return pltpu.make_async_copy(getattr(self.r, name + "_in").at[:, cols], ref.at[pl.ds(first, rows), cols], self.r.local_sems.at[g])

    def from_line(self, g, o):
        p, recv = self.p, self.r.gather_recv
        z = p.line[o]
        half = None if g in self.wide else p.x
        self.wait(g, z, p.y, half, p.c, recv)
        if g not in self.wide:
            self.start(g, "x1", o, "x", z, p.y, p.x, recv)
        elif o in self.over_y[g]:
            self.start(g, "y2", o, "y", z, p.y, p.other_x, recv)
        self.start(g, "y1", o, "y", z, p.y, p.x, recv)
        self.start(g, "cz", o, "core", z, p.y, half, self.r.gather_core)

    def from_x(self, g, o):
        p, recv = self.p, self.r.gather_recv
        z = p.line[o]
        self.wait(g, z, p.y, p.other_x, p.c, recv)
        if o in self.over_y[g]:
            self.start(g, "y2", o, "y", z, p.y, p.other_x, recv)
        self.start(g, "cx", o, "core", z, p.y, p.other_x, self.r.gather_core)

    def from_y(self, g, o):
        p, recv = self.p, self.r.gather_recv
        z = p.line[o]
        self.wait(g, z, p.other_y, p.x, p.c, recv)
        if o not in self.over_y[g]:
            self.start(g, "x2", o, "x", z, p.other_y, p.x, recv)
        self.start(g, "cy", o, "core", z, p.other_y, p.x, self.r.gather_core)

    def from_corner(self, g, o):
        p = self.p
        z = p.line[o]
        self.wait(g, z, p.other_y, p.other_x, p.c, self.r.gather_recv)
        self.start(g, "cd", o, "core", z, p.other_y, p.other_x, self.r.gather_core)

    def from_core(self, g, kind, o):
        p = self.p
        if kind == "x" and g in self.wide:
            return
        y = p.y if kind in "zx" else p.other_y
        h = p.x if kind in "zy" else p.other_x
        if kind == "z" and g in self.wide:
            h = None
        self.wait(g, p.line[o], y, h, p.other_c, self.r.gather_core)

    def sent(self, g):
        for what in self.sends[g]:
            self.copy(*what).wait_send()


class Reduce:
    def __init__(self, r, place, over_y, wide):
        self.r, self.p, self.over_y, self.wide = r, place, over_y, wide
        self.sends = []

    def home(self, g):
        r, name = self.r, REDUCED[g]
        width = r.tokens.shape[1]
        if name == "w_down":
            return r.own_down, 0, r.own_down.shape[0] // (4 * LINE), width // 2
        if name.startswith("third"):
            return r.w_down, g * width, width // (4 * LINE), width // 2
        ref = getattr(r, name)
        return ref, 0, ref.shape[0] // (4 * LINE), ref.shape[1] // 2

    def rows_of(self, g):
        return self.home(g)[2]

    def piece(self, g, z, y, h):
        ref, base, rows, cols = self.home(g)
        first = pl.multiple_of(base + ((z * 2 + y) * 2 + h) * rows, 16)
        if REDUCED[g] == "w_down":
            return ref.at[pl.ds(first, rows), :]
        return ref.at[pl.ds(first, rows), pl.ds(pl.multiple_of(self.p.c * cols, 128), cols)]

    def spot(self, kind, o):
        p = self.p
        y = p.y if kind in "ox" else p.other_y
        h = p.x if kind in "oy" else p.other_x
        return p.line[o], y, h

    def from_core(self, g, kind, o):
        z, y, h = self.spot(kind, o)
        rows = self.rows_of(g)
        return getattr(self.r, "core_" + REDUCED[g]).at[pl.ds(pl.multiple_of(((z * 2 + y) * 2 + h) * rows, 16), rows), :]

    def box(self, g, kind, slot):
        return getattr(self.r, "box_" + REDUCED[g]).at[dict(corner=0, x=4, y=8, line=12)[kind] + slot]

    def send(self, g, what, to, slot, recv=None):
        self.sends.append((g, what, to, slot, recv))
        self.copy(g, what, to, slot, recv).start()

    def copy(self, g, what, to, slot, recv):
        source, target = what()
        return push(
            source, target, self.p.to[to], self.r.reduce_send.at[g, slot], self.r.reduce_recv.at[g, slot if recv is None else recv]
        )

    def arrive(self, g, target, slot):
        push(target, target, self.p.to["core"], self.r.reduce_send.at[g, 0], self.r.reduce_recv.at[g, slot]).wait_recv()

    def arrive_core(self, g, target, slot):
        if REDUCED[g] != "w_down":
            self.arrive(g, target, slot)

    def add(self, target, *others):
        total = target[...].astype(F32)
        for other in others:
            total = total + other[...].astype(F32)
        target[...] = total.astype(BF16)

    def give(self, index, tile):
        slot = index % 2

        @pl.when(index >= 2)
        def _():
            self.given(index - 2).wait_send()

        self.r.stage[slot] = tile
        self.given(index).start()
        cols = self.r.own_down.shape[1]
        first = pl.multiple_of(self.p.c * cols, 128)
        self.r.own_down[tile_at(index, UP_TILE), :] = self.r.stage[slot, :, pl.ds(first, cols)]

    def given(self, index):
        cols = self.r.own_down.shape[1]
        first = pl.multiple_of((self.p.other_c) * cols, 128)
        return push(
            self.r.stage.at[index % 2, :, pl.ds(first, cols)], self.r.core_w_down.at[tile_at(index, UP_TILE), :], self.p.to["core"],
            self.r.stage_sems.at[index % 2], self.r.given_recv.at[index],
        )

    def all_given(self):
        tiles = self.r.own_down.shape[0] // UP_TILE
        for index in (tiles - 2, tiles - 1):
            self.given(index).wait_send()
        for index in range(tiles):
            self.given(index).wait_recv()

    def begin(self, g):
        far = (3, 2, 1, 0)
        base = dict(d=0, y=4, x=8, o=12)
        if REDUCED[g] == "w_down":
            self.all_given()
            return
        for kind in "dyxo":
            for o in far:
                self.send(g, functools.partial(self.across, g, kind, o), "core", base[kind] + o)

    def across(self, g, kind, o):
        ref, base, rows, cols = self.home(g)
        z, y, h = self.spot(kind, o)
        first = pl.multiple_of(base + ((z * 2 + y) * 2 + h) * rows, 16)
        other = pl.multiple_of(self.p.other_c * cols, 128)
        return ref.at[pl.ds(first, rows), pl.ds(other, cols)], self.from_core(g, kind, o)

    def boxed(self, g, kind, box, o):
        return self.piece(g, *self.spot(kind, o)), self.box(g, box, o)

    def corner(self, g, o):
        source = self.from_core(g, "d", o)
        self.arrive_core(g, source, o)
        piece = self.piece(g, *self.spot("d", o))
        self.add(piece, source)
        self.send(g, functools.partial(self.boxed, g, "d", "corner", o), "y" if o in self.over_y[g] else "x", 16 + o)

    def side(self, g, kind, o):
        source = self.from_core(g, kind, o)
        self.arrive_core(g, source, dict(y=4, x=8)[kind] + o)
        piece = self.piece(g, *self.spot(kind, o))
        if (o in self.over_y[g]) == (kind == "x"):
            box = self.box(g, "corner", o)
            self.arrive(g, box, 16 + o)
            self.add(piece, source, box)
        else:
            self.add(piece, source)
        self.send(g, functools.partial(self.boxed, g, kind, kind, o), kind, dict(y=20, x=24)[kind] + o)

    def centre(self, g, o):
        source, along_y = self.from_core(g, "o", o), self.box(g, "y", o)
        self.arrive_core(g, source, 12 + o)
        self.arrive(g, along_y, 20 + o)
        if g in self.wide:
            self.add(self.piece(g, *self.spot("o", o)), source, along_y)
            other = [self.from_core(g, "x", o)]
            self.arrive_core(g, other[0], 8 + o)
            if o in self.over_y[g]:
                other.append(self.box(g, "corner", o))
                self.arrive(g, other[1], 16 + o)
            self.add(self.piece(g, *self.spot("x", o)), *other)
            if o:
                self.send(g, functools.partial(self.straight_other, g, o), o, 24 + o, self.p.other_slot)
        else:
            along_x = self.box(g, "x", o)
            self.arrive(g, along_x, 24 + o)
            self.add(self.piece(g, *self.spot("o", o)), source, along_x, along_y)
        if o:
            self.send(g, functools.partial(self.straight, g, o), o, 28 + o, self.p.line_slot)

    def straight_other(self, g, o):
        return self.piece(g, *self.spot("x", o)), self.box(g, "x", self.p.z)

    def cross(self, g):
        self.send(g, functools.partial(self.crossing, g), "x", 39)

    def crossing(self, g):
        p = self.p
        return self.piece(g, p.z, p.y, p.other_x), self.box(g, "x", p.z)

    def straight(self, g, o):
        return self.piece(g, *self.spot("o", o)), self.box(g, "line", self.p.z)

    def collect(self, g, o):
        p = self.p
        z = p.line[o]
        box = self.box(g, "line", z)
        self.arrive(g, box, 32 + z)
        self.add(self.piece(g, p.z, p.y, p.x), box)
        if g in self.wide:
            box = self.box(g, "x", z)
            self.arrive(g, box, 24 + z)
            self.add(self.piece(g, p.z, p.y, p.other_x), box)

    def quarter(self, g, x, c):
        ref = getattr(self.r, REDUCED[g] + "_grad")
        rows, cols = ref.shape[0] // 2, ref.shape[1] // 2
        return ref.at[pl.ds(pl.multiple_of(x * rows, 16), rows), pl.ds(pl.multiple_of(c * cols, 128), cols)]

    def share(self, g):
        p = self.p
        if g in self.wide:
            box = self.box(g, "x", p.z)
            self.arrive(g, box, 39)
            self.add(self.piece(g, p.z, p.y, p.x), box)
        mine = self.quarter(g, p.x, p.c)
        mine[...] = self.piece(g, p.z, p.y, p.x)[...]
        for to, slot in (("x", 36), ("core", 37)):
            self.send(g, lambda: (self.quarter(g, p.x, p.c),) * 2, to, slot)

    def done(self, g):
        p = self.p
        other = self.quarter(g, p.other_x, p.c)
        self.arrive(g, other, 36)
        self.send(g, lambda: (self.quarter(g, p.other_x, p.c),) * 2, "core", 38)

    def finish(self):
        p = self.p
        for g in range(len(REDUCED)):
            self.arrive(g, self.quarter(g, p.x, p.other_c), 37)
            self.arrive(g, self.quarter(g, p.other_x, p.other_c), 38)
        for what in self.sends:
            self.copy(*what).wait_send()


def pack_small(r):
    peers = 2 * LINE
    width = r.tokens.shape[1]
    part = width // peers
    r.owners[...] = jnp.zeros(r.owners.shape, F32)
    for shard in range(peers):
        r.owners[shard, 0:8, 0:part] = r.grad_small[:, shard * part : (shard + 1) * part]
        for i in range(2):
            first = (shard * 2 + i) * part
            r.owners[shard, 8 + i : 9 + i, 0:part] = r.grad_qkv_bias[0:1, first : first + part]
        first = 2 * width + shard * part
        r.owners[shard, 10:11, 0:part] = r.grad_qkv_bias[0:1, first : first + part]
        for i in range(4):
            first = (shard * 4 + i) * part
            r.owners[shard, 11 + i : 12 + i, 0:part] = r.grad_up_bias[0:1, first : first + part]


def owner_copy(r, place, k, receive=False):
    other = (place.fsdp + k) % (2 * LINE)
    slot = other if receive else place.fsdp
    return push(
        r.owners.at[other], r.owned.at[slot], (place.seq, other), r.small_send.at[k], r.owned_recv.at[slot]
    )


def small_reduce_start(r, place):
    pack_small(r)
    lax.fori_loop(1, 2 * LINE, lambda k, carry: (owner_copy(r, place, k).start(), carry)[1], 0)


def small_reduce_middle(r, place):
    def receive(k, total):
        owner_copy(r, place, k, True).wait_recv()
        owner_copy(r, place, k).wait_send()
        return total + r.owned[(place.fsdp + k) % (2 * LINE)]

    r.shared[place.seq] = lax.fori_loop(1, 2 * LINE, receive, r.owners[place.fsdp])
    for k in range(1, 4):
        shared_copy(r, place, k).start()


def shared_copy(r, place, k, receive=False):
    other = (place.seq + k) % 4
    slot = other if receive else place.seq
    return push(
        r.shared.at[place.seq], r.shared.at[slot], (other, place.fsdp), r.shared_send.at[k], r.shared_recv.at[slot]
    )


def small_reduce_finish(r, place):
    for k in range(1, 4):
        shared_copy(r, place, k, True).wait_recv()
        shared_copy(r, place, k).wait_send()
    r.small_total[...] = r.shared[0] + r.shared[1] + r.shared[2] + r.shared[3]


class Home:
    def __init__(self, r, place, both, target, index):
        self.r, self.p, self.both, self.target, self.index = r, place, both, target, index
        rows = both.shape[0] // 2
        self.rows = both.at[pl.ds(pl.multiple_of(place.c * rows, 16), rows), :]

    def across(self, c):
        rows = self.both.shape[0] // 2
        part = self.both.at[pl.ds(pl.multiple_of(c * rows, 16), rows), :]
        return push(part, part, self.p.to["core"], self.r.home_send.at[self.index, 0], self.r.home_recv.at[self.index, 0])

    def along_x(self, x):
        send, recv = self.r.home_send, self.r.home_recv
        return push(
            self.r.leaving, self.target.at[x], self.p.to["x"], send.at[self.index, 1], recv.at[self.index, 1]
        )

    def start(self):
        self.across(self.p.c).start()

    def turn(self):
        self.across(self.p.other_c).wait_recv()
        ordered = dot_nn(self.r.place[...], self.both[...]).astype(BF16)
        half = ordered.shape[0] // 2
        self.r.leaving[...] = ordered[half:]
        self.along_x(self.p.x).start()
        self.target[self.p.x] = ordered[:half]

    def left(self):
        self.along_x(self.p.x).wait_send()

    def finish(self):
        self.along_x(self.p.other_x).wait_recv()
        self.across(self.p.c).wait_send()


def place_back(r, place):
    bundle, length = r.place.shape
    start = r.start[0:1, 0:1]
    quarter = length // 4

    def block(index):
        rows = tile_at(index, 128)
        shape = (128, length)
        mine = lax.broadcasted_iota(jnp.int32, shape, 0) + index * 128
        away = mine >= quarter
        mine = jnp.where(away, mine - quarter + quarter * (2 * (1 - place.x) + place.c), mine + quarter * (2 * place.x + place.c))
        source = mine.astype(F32) - start
        source = jnp.where(source < 0, source + length, source)
        here = lax.broadcasted_iota(jnp.int32, shape, 1).astype(F32)
        r.place[rows, :] = jnp.where(here == source, 1.0, 0.0).astype(BF16)

    loop(bundle // 128, block)


def greet(place):
    barrier = pltpu.get_barrier_semaphore()
    seq, fsdp = place.seq, place.fsdp
    peers = 2 * LINE

    def others(k, carry):
        pl.semaphore_signal(barrier, inc=1, device_id=(seq, (fsdp + k) % peers), device_id_type=MESH)
        return carry

    lax.fori_loop(1, peers, others, 0)
    for k in range(1, 4):
        pl.semaphore_signal(barrier, inc=1, device_id=((seq + k) % 4, fsdp), device_id_type=MESH)


def greeted():
    pl.semaphore_wait(pltpu.get_barrier_semaphore(), 2 * LINE + 2)


VECTORS = ("v0", "v1", "v2", "v3", "v4", "v5", "v6", "v7", "v8", "v9")


def pack_vectors(r):
    part = r.v0.shape[0]
    r.vector_rows[...] = jnp.zeros(r.vector_rows.shape, F32)
    row = 0
    for name in VECTORS:
        values = getattr(r, name)[...].astype(F32)
        for i in range(values.shape[0] // part):
            r.vector_rows[row : row + 1, 0:part] = values[i * part : (i + 1) * part].reshape(1, part)
            row += 1
    r.packed_in[...] = r.vector_rows[...].astype(BF16)


def small_send(r, place, k):
    peers = 2 * LINE
    other = (place.fsdp + k) % peers
    return push(
        r.packed_in, r.packed.at[place.fsdp], (place.seq, other), r.small_send.at[k], r.small_recv.at[place.fsdp]
    )


def small_start(r, place):
    lax.fori_loop(1, 2 * LINE, lambda k, carry: (small_send(r, place, k).start(), carry)[1], 0)
    r.packed[place.fsdp] = r.packed_in[...]


def small_finish(r, place):
    def receive(k, carry):
        other = (place.fsdp + k) % (2 * LINE)
        push(
            r.packed_in, r.packed.at[other], (place.seq, other), r.small_send.at[k], r.small_recv.at[other]
        ).wait_recv()
        small_send(r, place, k).wait_send()
        return carry

    lax.fori_loop(1, 2 * LINE, receive, 0)
    part = r.tokens.shape[1] // (2 * LINE)
    for shard in range(2 * LINE):
        rows = r.packed[shard].astype(F32)
        for i in range(8):
            r.small[i : i + 1, shard * part : (shard + 1) * part] = rows[i : i + 1, 0:part]
        for i in range(3):
            first = (shard * 3 + i) * part
            r.qkv_bias[0:1, first : first + part] = rows[8 + i : 9 + i, 0:part]
        for i in range(4):
            first = (shard * 4 + i) * part
            r.up_bias[0:1, first : first + part] = rows[11 + i : 12 + i, 0:part]


class Exchange:
    def __init__(self, r, place, source, target, index):
        self.p, self.target = place, target
        rows = target.shape[0] // 4
        p = place

        def quarter(x, c):
            return target.at[pl.ds(pl.multiple_of((2 * x + c) * rows, 16), rows), :]

        self.keep = pltpu.make_async_copy(source.at[p.x], quarter(p.x, p.c), r.local_sems.at[len(GATHERED) + index])
        send, recv = r.rows_send, r.rows_recv
        self.along_x = push(source.at[1 - p.x], quarter(p.x, p.c), p.to["x"], send.at[index, 0], recv.at[index, 0])
        self.own = push(source.at[p.x], quarter(p.x, p.c), p.to["core"], send.at[index, 1], recv.at[index, 1])
        passed = quarter(1 - p.x, p.c)
        self.passed = push(passed, passed, p.to["core"], send.at[index, 2], recv.at[index, 2])
        there = quarter(1 - p.x, p.c)
        self.arrive_x = push(there, there, p.to["x"], send.at[index, 0], recv.at[index, 0])
        one, two = quarter(p.x, 1 - p.c), quarter(1 - p.x, 1 - p.c)
        self.arrive = [
            push(one, one, p.to["core"], send.at[index, 1], recv.at[index, 1]),
            push(two, two, p.to["core"], send.at[index, 2], recv.at[index, 2]),
        ]

    def start(self):
        self.keep.start()
        self.along_x.start()
        self.own.start()

    def forward(self):
        self.arrive_x.wait_recv()
        self.passed.start()

    def finish(self):
        self.keep.wait()
        for copy in self.arrive:
            copy.wait_recv()
        for copy in (self.along_x, self.own, self.passed):
            copy.wait_send()


def collect_meta(r, place):
    r.meta_rows[...] = jnp.zeros(r.meta_rows.shape, F32)
    r.meta_rows[0:1, :] = r.segments[pl.ds(place.x, 1), :].astype(F32)
    for axis in range(2):
        r.meta_rows[1 + axis : 2 + axis, :] = r.positions[axis, pl.ds(place.x, 1), :].astype(F32)
    r.meta[...] = r.meta_rows[...].astype(BF16)


WEIGHTS = ("w_qkv", "w_out", "w_up", "w_down")


def spread_head_gains(r):
    columns = jnp.transpose(r.small[...])
    r.head_gain[...] = jnp.zeros(r.head_gain.shape, F32)
    r.head_gain_sums[...] = jnp.zeros(r.head_gain_sums.shape, F32)
    for head in range(2 * H):
        row = head % H * HD
        column = QUERY_GAIN if head < H else KEY_GAIN
        r.head_gain[:, head : head + 1] = columns[row : row + HD, column : column + 1]


TILES = dict(project=6, attend=12, branch=3, up=6, grad_before=6, down=3, grad_hidden_up=3, weight_up=6, out_back=3,
             attend_back=12, grad_hidden_in=3)
ORDER = ("place", "vectors", "rows", "norm", "project", "attend", "attended_rows", "branch", "norm_middle", "cotangent", "up",
         "grad_before", "down", "grad_hidden_up", "weight_up", "norm_middle_back", "out_back", "attend_back", "head_sums",
         "grad_hidden_in", "norm_tokens_back")


def place_rows(r, source, target):
    target[...] = dot_nn(r.place[...], source[...]).astype(BF16)


def computes(r, give):
    part = functools.partial

    def norm():
        rope_tables(r)
        mask_channels(r)
        norm_tokens(r)

    def attend_back_first(index):
        attend_back(r, index)

    table = dict(
        place=part(place_tokens, r), vectors=part(spread_head_gains, r), rows=lambda: place_rows(r, r.seq_tokens, r.tokens),
        norm=norm, attended_rows=part(attended_rows, r), norm_middle=part(norm_middle, r),
        cotangent=lambda: place_rows(r, r.seq_cotangent, r.cotangent), norm_middle_back=part(norm_middle_back, r),
        head_sums=part(head_sums, r), norm_tokens_back=part(norm_tokens_back, r), up=part(up, r, give=give),
    )
    for function in (
        project, attend, branch, grad_before, down, grad_hidden_up, weight_up, out_back, attend_back, grad_hidden_in
    ):
        table[function.__name__] = part(function, r)
    return table


def whole_kernel(names, *refs):
    r = Refs()
    for name, ref in zip(names, refs, strict=True):
        setattr(r, name, ref)
    r.result_rows, r.grad_rows = r.result, r.grad_result
    copies = [
        pltpu.make_async_copy(getattr(r, name + "_in"), getattr(r, name), r.local_sems.at[i]) for i, name in enumerate(WEIGHTS)
    ]
    for copy in copies:
        copy.start()
    r.ones[...] = jnp.ones(r.ones.shape, BF16)

    def out(index):
        return pltpu.make_async_copy(r.stage.at[index % 2], r.w_down_grad.at[tile_at(index, UP_TILE), :], r.stage_sems.at[index % 2])

    def give(index, tile):
        @pl.when(index >= 2)
        def _():
            out(index - 2).wait()

        r.stage[index % 2] = tile
        out(index).start()

    for copy in copies:
        copy.wait()
    table = computes(r, give)
    for name in ORDER:
        if name == "attend_back":
            for index in (0, 1):
                fetch(r, index).start()
        if name in TILES:
            loop(TILES[name], table[name])
        else:
            table[name]()
    for third in range(3):
        weight_in(r, third)
    for index in range(2):
        out(index).wait()
    kept = {"w_out": r.w_out, "w_up": r.w_up}
    kept["thirds"] = r.w_down.at[pl.ds(0, r.thirds_grad.shape[0]), :]
    back = [pltpu.make_async_copy(ref, getattr(r, name + "_grad"), r.local_sems.at[i]) for i, (name, ref) in enumerate(kept.items())]
    for copy in back:
        copy.start()
    for copy in back:
        copy.wait()


SCHEDULE = (
    ("tokens_start",), ("own", 0), ("place",), ("own", 2), ("small_have",), ("y", 0, 0), ("own", 1), ("z", 0, 2), ("z", 0, 1),
    ("vectors",), ("z", 0, 3), ("tokens_pass",), ("z", 2, 1), ("y", 0, 2), ("y", 2, 0), ("tokens_have",), ("x", 0, 1),
    ("rows",), ("y", 0, 3), ("y", 0, 1), ("z", 1, 1), ("d", 1, 0), ("x", 0, 3), ("z", 2, 3), ("z", 1, 2), ("norm",),
    ("d", 2, 0), ("d", 0, 2), ("x", 0, 2), ("d", 0, 0), ("z", 2, 2), ("y", 1, 0), ("d", 0, 1), ("z", 1, 3), ("d", 0, 3),
    ("have", 0), ("project",), ("own", 3), ("x", 2, 1), ("y", 2, 3), ("y", 1, 2), ("project",), ("y", 2, 1), ("own", 4),
    ("y", 1, 3), ("y", 1, 1), ("d", 1, 2), ("y", 2, 2), ("z", 3, 1), ("x", 2, 3), ("cotangent_start",), ("d", 2, 2),
    ("d", 2, 1), ("y", 3, 0), ("d", 2, 3), ("d", 1, 1), ("x", 2, 2), ("z", 3, 3), ("d", 1, 3), ("z", 3, 2), ("have", 1),
    ("x", 3, 1), ("project",), ("project",), ("have", 2), ("project",), ("project",), ("z", 4, 1), ("attend",), ("y", 3, 2),
    ("attend",), ("attend",), ("y", 3, 3), ("attend",), ("attend",), ("z", 4, 3), ("attend",), ("y", 3, 1), ("attend",),
    ("attend",), ("z", 4, 2), ("d", 3, 3), ("attend",), ("y", 4, 0), ("attend",), ("x", 3, 3), ("attend",), ("own", 5),
    ("y", 4, 3), ("d", 3, 2), ("attend",), ("cotangent_pass",), ("d", 3, 0), ("x", 3, 2), ("d", 3, 1), ("y", 4, 1),
    ("attended_rows",), ("have", 3), ("branch",), ("x", 4, 3), ("y", 4, 2), ("x", 4, 1), ("branch",), ("x", 4, 2), ("branch",),
    ("norm_middle",), ("cotangent_have",), ("cotangent",), ("d", 4, 2), ("d", 4, 3), ("d", 5, 0), ("z", 5, 1), ("d", 4, 0),
    ("d", 4, 1), ("have", 4), ("up",), ("z", 5, 2), ("up",), ("y", 5, 1), ("z", 5, 3), ("up",), ("y", 5, 0), ("up",),
    ("y", 5, 2), ("x", 5, 1), ("up",), ("x", 5, 2), ("y", 5, 3), ("x", 5, 3), ("up",), ("begin", 5), ("place_back",),
    ("corner", 5, 3), ("d", 5, 1), ("corner", 5, 0), ("fetch",), ("d", 5, 2), ("d", 5, 3), ("corner", 5, 1), ("have", 5),
    ("grad_before",), ("corner", 5, 2), ("grad_before",), ("grad_before",), ("grad_before",), ("grad_before",),
    ("side", 5, "x", 3), ("grad_before",), ("side", 5, "y", 3), ("grad_hidden_up",), ("grad_hidden_up",), ("side", 5, "y", 2),
    ("side", 5, "x", 2), ("grad_hidden_up",), ("sent", 4), ("weight_up",), ("side", 5, "y", 1), ("weight_up",), ("weight_up",),
    ("side", 5, "x", 1), ("centre", 5, 3), ("weight_up",), ("weight_up",), ("weight_up",), ("begin", 4), ("side", 5, "y", 0),
    ("side", 5, "x", 0), ("down",), ("centre", 5, 2), ("centre", 5, 1), ("down",), ("down",), ("corner", 4, 3),
    ("norm_middle_back",), ("sent", 3), ("centre", 5, 0), ("out_back",), ("side", 4, "x", 3), ("corner", 4, 1),
    ("side", 4, "y", 1), ("corner", 4, 2), ("side", 4, "x", 2), ("out_back",), ("result_start",), ("out_back",),
    ("corner", 4, 0), ("collect", 5, 2), ("collect", 5, 1), ("begin", 3), ("sent", 5), ("attend_back",), ("collect", 5, 3),
    ("attend_back",), ("share", 5), ("attend_back",), ("corner", 3, 0), ("attend_back",), ("side", 4, "y", 3), ("weight_in", 0),
    ("side", 3, "y", 3), ("begin", 0), ("corner", 3, 1), ("corner", 3, 3), ("result_turn",), ("attend_back",), ("attend_back",),
    ("side", 4, "y", 2), ("attend_back",), ("side", 3, "y", 2), ("corner", 0, 2), ("attend_back",), ("weight_in", 1),
    ("side", 4, "x", 1), ("begin", 1), ("corner", 0, 1), ("corner", 0, 0), ("attend_back",), ("attend_back",), ("corner", 1, 3),
    ("attend_back",), ("side", 0, "x", 2), ("centre", 3, 3), ("side", 4, "x", 0), ("attend_back",), ("side", 0, "y", 0),
    ("side", 1, "x", 3), ("centre", 4, 2), ("side", 3, "y", 0), ("weight_in", 2), ("begin", 2), ("corner", 1, 2), ("done", 5),
    ("corner", 1, 1), ("side", 0, "y", 2), ("head_sums",), ("grad_hidden_in",), ("grad_hidden_in",), ("corner", 0, 3),
    ("grad_hidden_in",), ("side", 1, "y", 0), ("norm_tokens_back",), ("grads_start",), ("side", 0, "x", 1), ("side", 0, "x", 3),
    ("side", 2, "y", 0), ("corner", 1, 0), ("side", 4, "y", 0), ("side", 1, "x", 2), ("corner", 2, 2), ("centre", 4, 3),
    ("corner", 3, 2), ("small_start",), ("side", 0, "x", 0), ("centre", 4, 1), ("side", 0, "y", 1), ("side", 1, "x", 1),
    ("grads_turn",), ("centre", 0, 2), ("side", 2, "y", 1), ("centre", 3, 2), ("side", 0, "y", 3), ("centre", 0, 0),
    ("side", 2, "y", 3), ("centre", 0, 1), ("small_middle",), ("side", 1, "y", 3), ("corner", 2, 3), ("side", 3, "y", 1),
    ("small_finish",), ("side", 1, "y", 2), ("corner", 2, 1), ("centre", 0, 3), ("result_have",), ("grads_have",),
    ("grads_left",), ("corner", 2, 0), ("side", 2, "x", 2), ("centre", 3, 0), ("collect", 0, 1), ("centre", 1, 3),
    ("side", 2, "x", 3), ("centre", 4, 0), ("sent", 0), ("sent", 1), ("sent", 2), ("centre", 3, 1), ("side", 2, "y", 2),
    ("centre", 1, 2), ("collect", 0, 2), ("collect", 0, 3), ("side", 2, "x", 1), ("side", 1, "y", 1), ("side", 1, "x", 0),
    ("collect", 4, 2), ("side", 2, "x", 0), ("collect", 4, 3), ("centre", 2, 3), ("centre", 2, 2), ("collect", 3, 2),
    ("centre", 2, 1), ("collect", 4, 1), ("centre", 1, 1), ("collect", 3, 3), ("share", 0), ("collect", 3, 1), ("centre", 2, 0),
    ("centre", 1, 0), ("collect", 1, 3), ("cross", 3), ("share", 4), ("collect", 1, 2), ("collect", 2, 3), ("done", 0),
    ("collect", 1, 1), ("collect", 2, 2), ("collect", 2, 1), ("share", 2), ("share", 1), ("share", 3), ("done", 2), ("done", 1),
    ("done", 4), ("done", 3), ("finish",),
)
GATHER_OVER_Y = ((0, 1), (0, 1, 2), (0,), (0, 1), (0, 1), (0, 1))
REDUCE_OVER_Y = ((0,), (0, 1, 2), (0, 1, 2, 3), (0, 1, 2, 3), (0, 1), (0, 1))
GATHER_WIDE = (1,)
REDUCE_WIDE = (3,)


def fused_kernel(names, *refs):
    r = Refs()
    for name, ref in zip(names, refs, strict=True):
        setattr(r, name, ref)
    place = Place()
    gather = Gather(r, place, dict(enumerate(GATHER_OVER_Y)), GATHER_WIDE)
    reduce = Reduce(r, place, dict(enumerate(REDUCE_OVER_Y)), REDUCE_WIDE)
    for g in range(len(GATHERED)):
        gather.load(g).start()
    tokens = Exchange(r, place, r.tokens_in, r.seq_tokens, 0)
    cotangent = Exchange(r, place, r.cotangent_in, r.seq_cotangent, 1)
    result = Home(r, place, r.seq_tokens, r.result, 0)
    grads = Home(r, place, r.seq_cotangent, r.grad_result, 1)
    r.result_rows, r.grad_rows = result.rows, grads.rows
    greet(place)
    pack_vectors(r)
    r.ones[...] = jnp.ones(r.ones.shape, BF16)
    collect_meta(r, place)
    greeted()
    small_start(r, place)

    def fetch_first():
        for index in (0, 1):
            fetch(r, index).start()

    def grads_turn():
        result.left()
        grads.turn()

    plain = dict(
        own=gather.own, z=gather.from_line, x=gather.from_x, y=gather.from_y, d=gather.from_corner, have=gather.have, sent=gather.sent,
        tokens_start=tokens.start, tokens_pass=tokens.forward, tokens_have=tokens.finish,
        cotangent_start=cotangent.start, cotangent_pass=cotangent.forward, cotangent_have=cotangent.finish,
        small_have=functools.partial(small_finish, r, place), fetch=fetch_first, weight_in=functools.partial(weight_in, r),
        begin=reduce.begin, corner=reduce.corner, side=reduce.side, centre=reduce.centre, collect=reduce.collect, share=reduce.share, cross=reduce.cross,
        done=reduce.done, finish=reduce.finish,
        place_back=functools.partial(place_back, r, place), result_start=result.start, result_turn=result.turn,
        result_have=result.finish, grads_start=grads.start, grads_turn=grads_turn, grads_have=grads.finish, grads_left=grads.left,
        small_start=functools.partial(small_reduce_start, r, place), small_middle=functools.partial(small_reduce_middle, r, place),
        small_finish=functools.partial(small_reduce_finish, r, place),
    )
    table = computes(r, reduce.give)
    items = list(SCHEDULE)
    while items:
        name, *args = items.pop(0)
        if name in plain:
            plain[name](*args)
        elif name not in TILES:
            table[name]()
        else:
            between = {}
            tile = 0
            while tile < TILES[name] - 1:
                item = items.pop(0)
                if item[0] == name:
                    tile += 1
                else:
                    between.setdefault(tile, []).append(item)
            tiled_loop(TILES[name], table[name], between, plain)


def tiled_loop(count, body, between, plain):
    def step(index):
        body(index)
        for tile, todo in between.items():

            @pl.when(index == tile)
            def _():
                for name, *args in todo:
                    plain[name](*args)

    loop(count, step)


def layer(fused, tokens, cotangent, segments, positions, small, qkv_bias, up_bias, *weights):
    peers = 2 * LINE
    scale = peers if fused else 1
    width = tokens.shape[-1]
    length = segments.shape[1]
    bundle = length // 2
    hidden = weights[2].shape[1]
    shape = jax.ShapeDtypeStruct
    vmem = pl.BlockSpec(memory_space=pltpu.VMEM)
    hbm = pl.BlockSpec(memory_space=pl.ANY)
    inputs = {}
    if fused:
        inputs.update(
            tokens_in=(tokens, hbm),
            cotangent_in=(cotangent, hbm),
            segments=(segments, vmem),
            positions=(positions, vmem),
            **{name: (v, vmem) for name, v in zip(VECTORS, small)},
        )
    else:
        inputs.update(
            seq_tokens=(tokens, vmem),
            seq_cotangent=(cotangent, vmem),
            meta=(segments, vmem),
            small=(small, vmem),
            qkv_bias=(qkv_bias, vmem),
            up_bias=(up_bias, vmem),
        )
    full = [(w.shape[0] * scale, w.shape[1]) for w in weights]
    for name, w in zip(WEIGHTS, weights):
        inputs[name + "_in"] = (w, hbm)
    outputs = dict(
        result=(shape(tokens.shape if fused else (bundle, width), BF16), vmem),
        grad_result=(shape(tokens.shape if fused else (bundle, width), BF16), vmem),
        chances_kept=(shape((H, bundle, bundle), BF16), hbm),
    )
    scratch = {}
    vectors = dict(grad_small=(8, width), grad_qkv_bias=(8, 3 * width), grad_up_bias=(8, hidden))
    if fused:
        outputs["small_total"] = (shape((16, 128), F32), vmem)
        scratch.update({name: pltpu.VMEM(size, F32) for name, size in vectors.items()})
    else:
        outputs.update({name: (shape(size, F32), vmem) for name, size in vectors.items()})
    reduced = {name: (width, width) for name in REDUCED[:3]}
    reduced.update(zip(WEIGHTS[1:], full[1:]))
    if fused:
        for name, size in reduced.items():
            outputs[name + "_grad"] = (shape((size[0] // peers, size[1]), BF16), vmem)
    else:
        outputs["thirds_grad"] = (shape((3 * width, width), BF16), hbm)
        for name in WEIGHTS[1:]:
            outputs[name + "_grad"] = (shape(reduced[name], BF16), hbm)
    for name, size in zip(WEIGHTS, full):
        scratch[name] = pltpu.VMEM(size, BF16)
    if fused:
        groups, pieces = len(GATHERED), 2 * peers
        scratch.update(
            seq_tokens=pltpu.VMEM((length, width), BF16),
            seq_cotangent=pltpu.VMEM((length, width), BF16),
            meta_rows=pltpu.VMEM((8, length), F32),
            meta=pltpu.VMEM((8, length), BF16),
            vector_rows=pltpu.VMEM((16, 128), F32),
            packed_in=pltpu.VMEM((16, 128), BF16),
            packed=pltpu.VMEM((peers, 16, 128), BF16),
            small=pltpu.VMEM((8, width), F32),
            qkv_bias=pltpu.VMEM((1, 3 * width), F32),
            up_bias=pltpu.VMEM((1, hidden), F32),
            small_send=pltpu.SemaphoreType.DMA((peers,)),
            small_recv=pltpu.SemaphoreType.DMA((peers,)),
            rows_send=pltpu.SemaphoreType.DMA((2, 3)),
            rows_recv=pltpu.SemaphoreType.DMA((2, 3)),
            gather_send=pltpu.SemaphoreType.DMA((groups, 36)),
            gather_recv=pltpu.SemaphoreType.DMA((groups, pieces)),
            gather_core=pltpu.SemaphoreType.DMA((groups, pieces)),
            own_down=pltpu.VMEM((hidden, width // 2), BF16),
            given_recv=pltpu.SemaphoreType.DMA((hidden // UP_TILE,)),
            reduce_send=pltpu.SemaphoreType.DMA((groups, 40)),
            reduce_recv=pltpu.SemaphoreType.DMA((groups, 40)),
            home_send=pltpu.SemaphoreType.DMA((2, 2)),
            home_recv=pltpu.SemaphoreType.DMA((2, 2)),
            leaving=pltpu.VMEM((length // 4, width), BF16),
            owners=pltpu.VMEM((peers, 16, 128), F32),
            owned=pltpu.VMEM((peers, 16, 128), F32),
            owned_recv=pltpu.SemaphoreType.DMA((peers,)),
            shared=pltpu.VMEM((4, 16, 128), F32),
            shared_send=pltpu.SemaphoreType.DMA((4,)),
            shared_recv=pltpu.SemaphoreType.DMA((4,)),
        )
        for name, size in reduced.items():
            scratch["core_" + name] = pltpu.VMEM((size[0], size[1] // 2), BF16)
            scratch["box_" + name] = pltpu.VMEM((16, size[0] // (2 * peers), size[1] // 2), BF16)
    scratch.update(
        local_sems=pltpu.SemaphoreType.DMA((10,)),
        ones=pltpu.VMEM((8, bundle), BF16),
        start=pltpu.VMEM((8, 128), F32),
        place=pltpu.VMEM((bundle, length), BF16),
        marks_row=pltpu.VMEM((8, bundle), F32),
        mask_keys=pltpu.VMEM((16, bundle), BF16),
        mask_queries=pltpu.VMEM((16, bundle), BF16),
        shares=pltpu.VMEM((H, 1, bundle), F32),
        cosine=pltpu.VMEM((2, HD // 4, bundle), F32),
        sine=pltpu.VMEM((2, HD // 4, bundle), F32),
        head_gain=pltpu.VMEM((HD, 128), F32),
        head_gain_sums=pltpu.VMEM((HD, 128), F32),
        tokens=pltpu.VMEM((bundle, width), BF16),
        cotangent=pltpu.VMEM((bundle, width), BF16),
        hidden_pre_t=pltpu.VMEM((width, bundle), BF16),
        projected_t=pltpu.VMEM((3 * width, bundle), BF16),
        turned_t=pltpu.VMEM((2 * width, bundle), BF16),
        chances=pltpu.VMEM((2, bundle, bundle), BF16),
        chance_sems=pltpu.SemaphoreType.DMA((2,)),
        attended_t=pltpu.VMEM((width, bundle), BF16),
        middle=pltpu.VMEM((bundle, width), F32),
        hidden_mlp_t=pltpu.VMEM((width, bundle), BF16),
        active=pltpu.VMEM((bundle, hidden), BF16),
        stage=pltpu.VMEM((2, UP_TILE, width), BF16),
        stage_sems=pltpu.SemaphoreType.DMA((2,)),
        slope=pltpu.VMEM((bundle, hidden), BF16),
        grad_hidden=pltpu.VMEM((bundle, width), F32),
        rows=pltpu.VMEM((bundle, width), BF16),
        grad_attended_t=pltpu.VMEM((width, bundle), BF16),
    )
    names = tuple(inputs) + tuple(outputs) + tuple(scratch)
    params = dict(vmem_limit_bytes=63 << 20)
    if fused:
        params.update(collective_id=0, has_side_effects=True)
    return pl.pallas_call(
        functools.partial(fused_kernel if fused else whole_kernel, names),
        out_shape=tuple(o[0] for o in outputs.values()),
        in_specs=[i[1] for i in inputs.values()],
        out_specs=tuple(o[1] for o in outputs.values()),
        scratch_shapes=list(scratch.values()),
        compiler_params=pltpu.CompilerParams(**params),
        name="layer",
    )(*(i[0] for i in inputs.values()))


def finish_kernel(part, result, grad_result, small, third0, third1, third2, *refs):
    weights, outs = refs[:3], refs[3:]
    outs[0][...] = result[...]
    outs[1][...] = grad_result[...]
    for third, source in enumerate((third0, third1, third2)):
        lanes = source.shape[1] // 6
        for half in range(2):
            for block in range(3):
                first = block * 6 * lanes + (2 * third + half) * lanes
                given = (half * 3 + block) * lanes
                outs[2][:, first : first + lanes] = source[:, given : given + lanes].astype(F32)
    for source, target in zip(weights, outs[3:6]):
        target[...] = source[...].astype(F32)
    for target, first, count in zip(outs[6:], (0, 1, 2, 3, 4, 5, 6, 7, 8, 10, 11), (1,) * 8 + (2, 1, 4)):
        for i in range(count):
            target[i * part : (i + 1) * part] = small[first + i : first + i + 1, 0:part].reshape(part)


def finish(part, result, grad_result, small, *weights):
    shape = jax.ShapeDtypeStruct
    vmem = pl.BlockSpec(memory_space=pltpu.VMEM)
    rows, width = weights[0].shape
    outs = [shape(result.shape, BF16), shape(grad_result.shape, BF16), shape((rows, 3 * width), F32)]
    outs += [shape(w.shape, F32) for w in weights[3:]]
    outs += [shape((part * count,), F32) for count in (1,) * 8 + (2, 1, 4)]
    return pl.pallas_call(
        functools.partial(finish_kernel, part),
        out_shape=tuple(outs),
        in_specs=[vmem] * (3 + len(weights)),
        out_specs=tuple([vmem] * len(outs)),
        compiler_params=pltpu.CompilerParams(vmem_limit_bytes=63 << 20),
        name="finish",
    )(result, grad_result, small, *weights)


def shards(
    tokens,
    pre_gain,
    pre_bias,
    query_key_value_weight,
    query_key_value_bias,
    query_gain,
    key_gain,
    output_weight,
    output_bias,
    mlp_gain,
    mlp_bias,
    up_matrix_weight,
    up_offset_bias,
    down_matrix_weight,
    down_offset_bias,
    segments,
    positions,
    cotangent,
):
    rank = lax.axis_index("seq")
    x = rank // 2
    width = tokens.shape[2]
    length = segments.shape[1]
    fsdp = lax.axis_size("fsdp")
    part = width // fsdp
    weights_in = (query_key_value_weight, output_weight, up_matrix_weight, down_matrix_weight)
    vectors = (
        pre_gain, pre_bias, query_gain, key_gain, output_bias, mlp_gain, mlp_bias, down_offset_bias,
        query_key_value_bias, up_offset_bias,
    )
    if fsdp == 2 * LINE:
        result, grad_result, _, small_total, *weight_grads = layer(
            True, tokens, cotangent, segments, positions, vectors, None, None, *weights_in
        )
        result, grad_result, g0, g1, g2, g3, *v = finish(part, result, grad_result, small_total, *weight_grads)
        return (
            result, grad_result, v[PRE_GAIN], v[PRE_BIAS], g0, v[8], v[9], v[QUERY_GAIN], v[KEY_GAIN], g1, v[OUT_BIAS],
            v[MLP_GAIN], v[MLP_BIAS], g2, v[10], g3, v[DOWN_BIAS],
        )
    else:
        gather = functools.partial(lax.all_gather, axis_name="fsdp", axis=0, tiled=True)
        packed = gather(jnp.concatenate(vectors)[None]).astype(F32)
        small = jnp.stack([packed[:, i * part : (i + 1) * part].reshape(width) for i in range(8)])
        qkv_bias = packed[:, 8 * part : 11 * part].reshape(1, 3 * width)
        up_bias = packed[:, 11 * part :].reshape(1, -1)
        seq_tokens = lax.dynamic_index_in_dim(lax.all_gather(tokens, "seq", axis=1, tiled=True), x, 0, False)
        seq_cotangent = lax.dynamic_index_in_dim(lax.all_gather(cotangent, "seq", axis=1, tiled=True), x, 0, False)
        labels = lax.dynamic_index_in_dim(segments, x, 0, True)
        places = lax.dynamic_index_in_dim(positions, x, 1, False)
        meta = jnp.concatenate([labels, places, jnp.zeros((5, length), jnp.int32)], axis=0).astype(BF16)
        results = layer(False, seq_tokens, seq_cotangent, meta, None, small, qkv_bias, up_bias, *map(gather, weights_in))
    result, grad_result, _, grad_small, grad_qkv_bias, grad_up_bias, thirds, *weight_grads = results
    blocks = thirds.reshape(3, width, 2, 3, width // 6)
    weight_grads = [blocks.transpose(1, 3, 0, 2, 4).reshape(width, 3 * width), *weight_grads]
    counts = jnp.stack([jnp.sum(segments == v, axis=1) for v in range(4)])
    first = jnp.argmax(counts == length // 2, axis=0)
    starts = jnp.sum(segments < first[:, None], axis=1)

    def home(bundle):
        every = lax.all_gather(bundle, "seq").reshape(2, length, width)
        own = rank * (length // 4) + jnp.arange(length // 4)
        index = (own[None] - starts[:, None]) % length
        return jnp.take_along_axis(every, index[..., None], axis=1)

    scatter = functools.partial(lax.psum_scatter, axis_name="fsdp", scatter_dimension=0, tiled=True)

    def total_of(grad):
        return lax.psum(scatter(grad).astype(BF16), "seq").astype(F32)

    weights = [total_of(g) for g in weight_grads]
    pieces = [grad_small[i].reshape(fsdp, part) for i in range(8)]
    pieces += [grad_qkv_bias[0, : 2 * width].reshape(fsdp, -1), grad_qkv_bias[0, 2 * width :].reshape(fsdp, -1)]
    pieces += [grad_up_bias[0].reshape(fsdp, -1)]
    total = lax.psum(scatter(jnp.concatenate(pieces, axis=1)), "seq")[0]
    s = [total[i * part : (i + 1) * part] for i in range(8)]
    query_key_bias, value_bias, up_total = total[8 * part : 10 * part], total[10 * part : 11 * part], total[11 * part :]
    return (
        home(result), home(grad_result), s[PRE_GAIN], s[PRE_BIAS], weights[0], query_key_bias, value_bias,
        s[QUERY_GAIN], s[KEY_GAIN], weights[1], s[OUT_BIAS], s[MLP_GAIN], s[MLP_BIAS], weights[2], up_total,
        weights[3], s[DOWN_BIAS],
    )


def solution(mesh):
    rows, matrix, activations = P("fsdp"), P("fsdp", None), P("fsdp", "seq", None)
    placed = (
        activations, rows, rows, matrix, rows, rows, rows, matrix, rows, rows, rows, matrix, rows, matrix, rows,
        P("fsdp", None), P(None, "fsdp", None), activations,
    )
    given = (
        activations, activations, rows, rows, matrix, rows, rows, rows, rows, matrix, rows, rows, rows, matrix, rows,
        matrix, rows,
    )
    return jax.shard_map(shards, mesh=mesh, in_specs=placed, out_specs=given, check_vma=False)
```

```python
import functools

import jax
import jax.numpy as jnp
from jax import lax
from jax.experimental import pallas as pl
from jax.experimental.pallas import tpu as pltpu
from jax.sharding import PartitionSpec as P

H = 12
HD = 64
EPSILON = 1e-06
MASK = 128.0
ROPE_BASE = 100.0
F32 = jnp.float32
BF16 = jnp.bfloat16
TILE = 256
UP_TILE = 512


def dot_nn(a, b):
    return lax.dot_general(a, b, (((1,), (0,)), ((), ())), preferred_element_type=F32)


def dot_nt(a, b):
    return lax.dot_general(a, b, (((1,), (1,)), ((), ())), preferred_element_type=F32)


def dot_tn(a, b):
    return lax.dot_general(a, b, (((0,), (0,)), ((), ())), preferred_element_type=F32)


def tile_at(index, size=TILE):
    return pl.ds(pl.multiple_of(index * size, size), size)


def loop(count, body, first=0):
    def step(index, carry):
        body(index)
        return carry

    lax.fori_loop(first, first + count, step, 0)


def rows_sum(block):
    rows, width = block.shape
    return jnp.sum(block.reshape(rows // 8, 8, width), axis=0)


def column_sums_exact(ones, block):
    return dot_nn(ones, block)[0:1]


def place_tokens(r):
    bundle, length = r.place.shape
    labels = r.meta[0:1, :].astype(F32)
    start = jnp.zeros((1, 1), F32)
    found = jnp.zeros((1, 1), F32)
    for value in range(4):
        here = jnp.sum(jnp.where(labels == value, 1.0, 0.0), axis=1, keepdims=True)
        below = jnp.sum(jnp.where(labels < value, 1.0, 0.0), axis=1, keepdims=True)
        hit = jnp.where(here == bundle, 1.0, 0.0) * (1.0 - found)
        start = start + hit * below
        found = found + hit
    r.start[...] = jnp.broadcast_to(start, r.start.shape)
    core = lax.axis_index("seq") % 2

    def block(index):
        rows = tile_at(index, 128)
        shape = (128, length)
        mine = lax.broadcasted_iota(jnp.int32, shape, 0) + (index * 128 + core * bundle)
        target = mine.astype(F32) + start
        target = jnp.where(target >= length, target - length, target)
        source = lax.broadcasted_iota(jnp.int32, shape, 1).astype(F32)
        r.place[rows, :] = jnp.where(source == target, 1.0, 0.0).astype(BF16)

    loop(bundle // 128, block)
    r.marks_row[...] = dot_nt(r.meta[...], r.place[...])


def mask_channels(r):
    rows = lax.broadcasted_iota(jnp.int32, r.mask_keys.shape, 0).astype(F32)
    same = jnp.where(rows == r.marks_row[0:1, :], 1.0, 0.0)
    r.mask_keys[...] = jnp.where(rows == 4.0, 1.0, same).astype(BF16)
    r.mask_queries[...] = jnp.where(rows == 4.0, -MASK, same * MASK).astype(BF16)


def rope_tables(r):
    quarter = HD // 4
    bundle = r.cosine.shape[-1]
    step = lax.broadcasted_iota(jnp.int32, (quarter, bundle), 0).astype(F32)
    frequency = jnp.exp(step * (-jnp.log(jnp.float32(ROPE_BASE)) / quarter))
    for axis in range(2):
        angle = r.marks_row[1 + axis : 2 + axis, :] * frequency
        r.cosine[axis] = jnp.cos(angle)
        r.sine[axis] = jnp.sin(angle)


def normalized(block):
    mean = jnp.mean(block, axis=-1, keepdims=True)
    centred = block - mean
    scale = lax.rsqrt(jnp.mean(centred * centred, axis=-1, keepdims=True) + EPSILON)
    return centred * scale, scale


def norm_rows(source, gain, bias, target, rows=128):
    def block(index):
        where = tile_at(index, rows)
        unit, _ = normalized(source[where, :].astype(F32))
        target[where, :] = (unit * gain + bias).astype(target.dtype)

    loop(source.shape[0] // rows, block)


def norm_rows_back(source, grads, base, gain, store, rows=128):
    width = source.shape[1]

    def block(index, carry):
        gain_sum, bias_sum = carry
        where = tile_at(index, rows)
        unit, scale = normalized(source[where, :].astype(F32))
        outer = grads[where, :]
        inner = outer * gain
        first = jnp.mean(inner, axis=-1, keepdims=True)
        second = jnp.mean(inner * unit, axis=-1, keepdims=True)
        store(where, base[where, :].astype(F32) + scale * (inner - first - unit * second))
        return gain_sum + rows_sum(outer * unit), bias_sum + rows_sum(outer)

    zero = jnp.zeros((8, width), F32)
    gain_sum, bias_sum = lax.fori_loop(0, source.shape[0] // rows, block, (zero, zero))
    return jnp.sum(gain_sum, axis=0, keepdims=True), jnp.sum(bias_sum, axis=0, keepdims=True)


def transpose_into(target, source):
    def block(index):
        where = tile_at(index, 128)
        target[where, :] = jnp.transpose(source[:, where])

    loop(source.shape[1] // 128, block)


def head_norm(vectors):
    mean = jnp.mean(vectors, axis=0, keepdims=True)
    centred = vectors - mean
    scale = lax.rsqrt(jnp.mean(centred * centred, axis=0, keepdims=True) + EPSILON)
    return centred * scale, scale


def turn(vectors, r):
    q = HD // 4
    out = []
    for axis in range(2):
        one, two = vectors[2 * axis * q : (2 * axis + 1) * q], vectors[(2 * axis + 1) * q : (2 * axis + 2) * q]
        cosine, sine = r.cosine[axis], r.sine[axis]
        out.append(one * cosine - two * sine)
        out.append(two * cosine + one * sine)
    return jnp.concatenate(out, axis=0) * HD ** (-0.5)


def turn_back(vectors, r):
    q = HD // 4
    out = []
    for axis in range(2):
        one, two = vectors[2 * axis * q : (2 * axis + 1) * q], vectors[(2 * axis + 1) * q : (2 * axis + 2) * q]
        cosine, sine = r.cosine[axis], r.sine[axis]
        out.append(one * cosine + two * sine)
        out.append(two * cosine - one * sine)
    return jnp.concatenate(out, axis=0) * HD ** (-0.5)


PRE_GAIN, PRE_BIAS, QUERY_GAIN, KEY_GAIN, OUT_BIAS, MLP_GAIN, MLP_BIAS, DOWN_BIAS = range(8)


def gain_of(r, head):
    lanes = lax.broadcasted_iota(jnp.int32, (HD, 128), 1)
    return jnp.sum(jnp.where(lanes == head, r.head_gain[...], 0.0), axis=1, keepdims=True)


def spill(r, index):
    return pltpu.make_async_copy(r.chances.at[index % 2], r.chances_kept.at[index], r.chance_sems.at[index % 2])


def fetch(r, index):
    return pltpu.make_async_copy(r.chances_kept.at[index], r.chances.at[index % 2], r.chance_sems.at[index % 2])


def norm_tokens(r):
    norm_rows(r.tokens, r.small[PRE_GAIN : PRE_GAIN + 1, :], r.small[PRE_BIAS : PRE_BIAS + 1, :], r.rows)
    transpose_into(r.hidden_pre_t, r.rows)


def project(r, index):
    cols = tile_at(index, H // 2 * HD)
    part = dot_nn(r.rows[...], r.w_qkv[:, cols]) + r.qkv_bias[0:1, cols]
    r.projected_t[cols, :] = jnp.transpose(part.astype(BF16))

    def head(which):
        rows = tile_at(which, HD)
        unit, _ = head_norm(r.projected_t[rows, :].astype(F32))
        r.turned_t[rows, :] = turn(unit * gain_of(r, which), r).astype(BF16)

    @pl.when(index < 4)
    def _():
        loop(H // 2, head, index * (H // 2))


def attend(r, index):
    rows = tile_at(index, HD)
    key_rows = tile_at(index + H, HD)
    value_rows = tile_at(index + 2 * H, HD)
    slot = index % 2

    @pl.when(index >= 2)
    def _():
        spill(r, index - 2).wait()

    keys = jnp.concatenate([r.turned_t[key_rows, :], r.mask_keys[...]], axis=0)
    queries = jnp.concatenate([r.turned_t[rows, :], r.mask_queries[...]], axis=0)
    raised = jnp.exp(dot_tn(keys, queries))
    share = 1.0 / jnp.sum(raised, axis=0, keepdims=True)
    low = raised.astype(BF16)
    r.chances[slot] = low
    spill(r, index).start()
    r.shares[pl.ds(index, 1)] = share.reshape(1, 1, -1)
    r.attended_t[rows, :] = (dot_nn(r.projected_t[value_rows, :], low) * share).astype(BF16)


def attended_rows(r):
    for index in (H - 2, H - 1):
        spill(r, index).wait()
    transpose_into_rows(r.rows, r.attended_t)


def transpose_into_rows(target, source):
    def block(index):
        where = tile_at(index, 128)
        target[:, where] = jnp.transpose(source[where, :])

    loop(source.shape[0] // 128, block)


def branch(r, index):
    cols = tile_at(index)
    part = dot_nn(r.rows[...], r.w_out[:, cols]) + r.small[OUT_BIAS : OUT_BIAS + 1, cols]
    r.middle[:, cols] = r.tokens[:, cols].astype(F32) + part


def norm_middle(r):
    norm_rows(r.middle, r.small[MLP_GAIN : MLP_GAIN + 1, :], r.small[MLP_BIAS : MLP_BIAS + 1, :], r.rows)
    transpose_into(r.hidden_mlp_t, r.rows)


def up(r, index, give):
    cols = tile_at(index, UP_TILE)
    before = r.grad_hidden.at[:, pl.ds(0, UP_TILE)]
    before[...] = dot_nn(r.rows[...], r.w_up[:, cols]) + r.up_bias[0:1, cols]

    def activate(part):
        rows = tile_at(part, 64)
        v = before[rows, :]
        half = 0.5 + 0.5 * lax.erf(v * 0.7071067811865476)
        r.active[rows, cols] = (v * half).astype(BF16)
        r.slope[rows, cols] = (half + v * (jnp.exp(-0.5 * v * v) * 0.3989422804014327)).astype(BF16)

    loop(before.shape[0] // 64, activate)
    give(index, dot_nn(jnp.transpose(r.active[:, cols]), r.cotangent[...]).astype(BF16))


def down(r, index):
    cols = tile_at(index)
    part = dot_nn(r.active[...], r.w_down[:, cols]) + r.small[DOWN_BIAS : DOWN_BIAS + 1, cols]
    r.result_rows[:, cols] = (r.middle[:, cols] + part).astype(BF16)


def grad_before(r, index):
    rows = tile_at(index, 512)
    grads = dot_nt(r.cotangent[...], r.w_down[rows, :]) * r.slope[:, rows].astype(F32)
    r.slope[:, rows] = grads.astype(BF16)
    r.grad_up_bias[0:1, rows] = jnp.sum(rows_sum(grads), axis=0, keepdims=True)


def grad_hidden_up(r, index):
    cols = tile_at(index)
    r.grad_hidden[:, cols] = dot_nt(r.slope[...], r.w_up[cols, :])


def weight_up(r, index):
    cols = tile_at(index, 512)
    r.w_up[:, cols] = dot_nn(r.hidden_mlp_t[...], r.slope[:, cols]).astype(BF16)


def norm_middle_back(r):
    def store(where, value):
        r.middle[where, :] = value
        r.rows[where, :] = value.astype(BF16)

    gain, bias = norm_rows_back(r.middle, r.grad_hidden, r.cotangent, r.small[MLP_GAIN : MLP_GAIN + 1, :], store)
    r.grad_small[MLP_GAIN : MLP_GAIN + 1, :] = gain
    r.grad_small[MLP_BIAS : MLP_BIAS + 1, :] = bias
    r.grad_small[OUT_BIAS : OUT_BIAS + 1, :] = column_sums_exact(r.ones[...], r.rows[...])
    r.grad_small[DOWN_BIAS : DOWN_BIAS + 1, :] = column_sums_exact(r.ones[...], r.cotangent[...])


def out_back(r, index):
    rows = tile_at(index)
    r.grad_attended_t[rows, :] = dot_nt(r.w_out[rows, :], r.rows[...]).astype(BF16)
    r.w_out[rows, :] = dot_nn(r.attended_t[rows, :], r.rows[...]).astype(BF16)


def attend_back(r, index):
    rows = tile_at(index, HD)
    key_rows = tile_at(index + H, HD)
    value_rows = tile_at(index + 2 * H, HD)
    share = r.shares[pl.ds(index, 1)].reshape(1, -1)
    outer = (r.grad_attended_t[rows, :].astype(F32) * share).astype(BF16)
    grads = dot_tn(r.projected_t[value_rows, :], outer)
    fetch(r, index).wait()
    chances = r.chances[index % 2]
    wide = chances.astype(F32)
    inner = jnp.sum(wide * grads, axis=0, keepdims=True) * share
    scores = (wide * (grads - inner)).astype(BF16)
    r.projected_t[value_rows, :] = dot_nt(outer, chances).astype(BF16)

    @pl.when(index + 2 < H)
    def _():
        fetch(r, index + 2).start()

    for head, target, grad in (
        (index, rows, dot_nn(r.turned_t[key_rows, :], scores)),
        (index + H, key_rows, dot_nt(r.turned_t[rows, :], scores)),
    ):
        unit, scale = head_norm(r.projected_t[target, :].astype(F32))
        outer_turned = turn_back(grad, r)
        weighted = outer_turned * unit
        total = jnp.sum(weighted, axis=1, keepdims=True)
        lanes = lax.broadcasted_iota(jnp.int32, (HD, 128), 1)
        r.head_gain_sums[...] += jnp.where(lanes == head, total, 0.0)
        inner_turned = outer_turned * gain_of(r, head)
        first = jnp.mean(inner_turned, axis=0, keepdims=True)
        second = jnp.mean(inner_turned * unit, axis=0, keepdims=True)
        r.projected_t[target, :] = (scale * (inner_turned - first - unit * second)).astype(BF16)


def head_sums(r):
    width = r.tokens.shape[1]
    sums = jnp.transpose(r.head_gain_sums[...])
    for head in range(2 * H):
        row = QUERY_GAIN if head < H else KEY_GAIN
        first = head % H * HD
        r.grad_small[row : row + 1, first : first + HD] = sums[head : head + 1, :]
    r.grad_qkv_bias[0:1, :] = dot_nt(r.ones[...], r.projected_t[...])[0:1]


def grad_hidden_in(r, index):
    rows = tile_at(index)
    r.grad_hidden[:, rows] = jnp.transpose(dot_nn(r.w_qkv[rows, :], r.projected_t[...]))


def weight_in(r, third):
    width = r.tokens.shape[1]
    part = width // 6
    rows = [
        r.projected_t[block * width + (2 * third + half) * part : block * width + (2 * third + half + 1) * part, :]
        for half in range(2)
        for block in range(3)
    ]
    columns = jnp.concatenate(rows, axis=0)

    def block(index):
        part = dot_nt(r.hidden_pre_t[tile_at(index), :], columns)
        r.w_down[pl.ds(pl.multiple_of(third * width + index * TILE, TILE), TILE), :] = part.astype(BF16)

    loop(width // TILE, block)


def norm_tokens_back(r):
    def store(where, value):
        r.grad_rows[where, :] = value.astype(BF16)

    gain, bias = norm_rows_back(r.tokens, r.grad_hidden, r.middle, r.small[PRE_GAIN : PRE_GAIN + 1, :], store)
    r.grad_small[PRE_GAIN : PRE_GAIN + 1, :] = gain
    r.grad_small[PRE_BIAS : PRE_BIAS + 1, :] = bias


class Refs:
    pass

MESH = pl.DeviceIdType.MESH
GATHERED = (("w_qkv", 0, 1), ("w_qkv", 1, 1), ("w_qkv", 2, 1), ("w_out", 0, 1), ("w_up", 0, 4), ("w_down", 0, 1))
REDUCED = ("third0", "third1", "third2", "w_out", "w_up", "w_down")
LINE = 4


class Place:
    def __init__(self):
        seq, fsdp = lax.axis_index("seq"), lax.axis_index("fsdp")
        self.seq, self.fsdp = seq, fsdp
        self.x, self.c = seq // 2, seq % 2
        self.z, self.y = fsdp // 2, fsdp % 2
        self.other_x, self.other_y, self.other_c = 1 - self.x, 1 - self.y, 1 - self.c
        self.line_slot, self.other_slot = 32 + self.z, 24 + self.z
        x, c, z, y = self.x, self.c, self.z, self.y
        self.to = dict(
            core=(2 * x + 1 - c, fsdp),
            x=(2 * (1 - x) + c, fsdp),
            y=(seq, 2 * z + 1 - y),
        )
        high = z // 2
        low = z + high * (LINE - 1 - 2 * z)
        self.line = [z]
        for i in range(LINE - 1):
            other = (i + 1) - (low if i == 0 else 0)
            self.line.append(other + high * (LINE - 1 - 2 * other))
            self.to[i + 1] = (seq, self.line[i + 1] * 2 + y)


def push(source, target, to, send_sem, recv_sem):
    return pltpu.make_async_remote_copy(
        src_ref=source, dst_ref=target, send_sem=send_sem, recv_sem=recv_sem, device_id=to, device_id_type=MESH
    )


class Gather:
    def __init__(self, r, place, over_y, wide):
        self.r, self.p, self.over_y, self.wide = r, place, over_y, wide
        self.sends = {g: [] for g in range(len(GATHERED))}
    def kinds(self):
        return [("z", o) for o in (1, 2, 3)] + [(k, o) for k in ("y", "x", "d") for o in range(LINE) if (k, o) != ("x", 0)]

    def have(self, g):
        for kind, o in self.kinds():
            self.from_core(g, kind, o)

    def piece(self, g, z, y, h, c):
        name, column, count = GATHERED[g]
        ref, width = getattr(self.r, name), self.r.tokens.shape[1]
        shard, cols = ref.shape[0] // (2 * LINE), count * width // 2
        rows = shard // 2
        first = pl.multiple_of((z * 2 + y) * shard, 16) if h is None else pl.multiple_of((z * 2 + y) * shard + h * rows, 16)
        rows = shard if h is None else rows
        return ref.at[pl.ds(first, rows), pl.ds(pl.multiple_of(column * width + c * cols, 128), cols)]

    def ident(self, z, y, h):
        return (z * 2 + y) * 2 + (self.p.x if h is None else h)

    def start(self, *what):
        self.sends[what[0]].append(what)
        self.copy(*what).start()

    def copy(self, g, kind, o, to, z, y, h, recv):
        slot = dict(line=0, x1=4, y1=8, x2=12, y2=16, cz=20, cx=24, cy=28, cd=32)[kind] + o
        piece = self.piece(g, z, y, h, self.p.c)
        return push(piece, piece, self.p.to[to], self.r.gather_send.at[g, slot], recv.at[g, self.ident(z, y, h)])

    def wait(self, g, z, y, h, c, recv):
        piece = self.piece(g, z, y, h, c)
        push(piece, piece, self.p.to["core"], self.r.gather_send.at[g, 0], recv.at[g, self.ident(z, y, h)]).wait_recv()

    def own(self, g):
        p, recv = self.p, self.r.gather_recv
        self.load(g).wait()
        self.start(g, "y1", 0, "y", p.z, p.y, p.x, recv)
        for o in range(1, LINE):
            self.start(g, "line", o, o, p.z, p.y, None if g in self.wide else p.x, recv)
        if 0 in self.over_y[g]:
            self.start(g, "y2", 0, "y", p.z, p.y, p.other_x, recv)

    def load(self, g):
        name, column, count = GATHERED[g]
        ref, width = getattr(self.r, name), self.r.tokens.shape[1]
        rows = ref.shape[0] // (2 * LINE)
        cols = pl.ds(column * width, count * width)
        first = pl.multiple_of(self.p.fsdp * rows, 16)
        return pltpu.make_async_copy(getattr(self.r, name + "_in").at[:, cols], ref.at[pl.ds(first, rows), cols], self.r.local_sems.at[g])

    def from_line(self, g, o):
        p, recv = self.p, self.r.gather_recv
        z = p.line[o]
        half = None if g in self.wide else p.x
        self.wait(g, z, p.y, half, p.c, recv)
        if g not in self.wide:
            self.start(g, "x1", o, "x", z, p.y, p.x, recv)
        elif o in self.over_y[g]:
            self.start(g, "y2", o, "y", z, p.y, p.other_x, recv)
        self.start(g, "y1", o, "y", z, p.y, p.x, recv)
        self.start(g, "cz", o, "core", z, p.y, half, self.r.gather_core)

    def from_x(self, g, o):
        p, recv = self.p, self.r.gather_recv
        z = p.line[o]
        self.wait(g, z, p.y, p.other_x, p.c, recv)
        if o in self.over_y[g]:
            self.start(g, "y2", o, "y", z, p.y, p.other_x, recv)
        self.start(g, "cx", o, "core", z, p.y, p.other_x, self.r.gather_core)

    def from_y(self, g, o):
        p, recv = self.p, self.r.gather_recv
        z = p.line[o]
        self.wait(g, z, p.other_y, p.x, p.c, recv)
        if o not in self.over_y[g]:
            self.start(g, "x2", o, "x", z, p.other_y, p.x, recv)
        self.start(g, "cy", o, "core", z, p.other_y, p.x, self.r.gather_core)

    def from_corner(self, g, o):
        p = self.p
        z = p.line[o]
        self.wait(g, z, p.other_y, p.other_x, p.c, self.r.gather_recv)
        self.start(g, "cd", o, "core", z, p.other_y, p.other_x, self.r.gather_core)

    def from_core(self, g, kind, o):
        p = self.p
        if kind == "x" and g in self.wide:
            return
        y = p.y if kind in "zx" else p.other_y
        h = p.x if kind in "zy" else p.other_x
        if kind == "z" and g in self.wide:
            h = None
        self.wait(g, p.line[o], y, h, p.other_c, self.r.gather_core)

    def sent(self, g):
        for what in self.sends[g]:
            self.copy(*what).wait_send()


class Reduce:
    def __init__(self, r, place, over_y, wide):
        self.r, self.p, self.over_y, self.wide = r, place, over_y, wide
        self.sends = []

    def home(self, g):
        r, name = self.r, REDUCED[g]
        width = r.tokens.shape[1]
        if name == "w_down":
            return r.own_down, 0, r.own_down.shape[0] // (4 * LINE), width // 2
        if name.startswith("third"):
            return r.w_down, g * width, width // (4 * LINE), width // 2
        ref = getattr(r, name)
        return ref, 0, ref.shape[0] // (4 * LINE), ref.shape[1] // 2

    def rows_of(self, g):
        return self.home(g)[2]

    def piece(self, g, z, y, h):
        ref, base, rows, cols = self.home(g)
        first = pl.multiple_of(base + ((z * 2 + y) * 2 + h) * rows, 16)
        if REDUCED[g] == "w_down":
            return ref.at[pl.ds(first, rows), :]
        return ref.at[pl.ds(first, rows), pl.ds(pl.multiple_of(self.p.c * cols, 128), cols)]

    def spot(self, kind, o):
        p = self.p
        y = p.y if kind in "ox" else p.other_y
        h = p.x if kind in "oy" else p.other_x
        return p.line[o], y, h

    def from_core(self, g, kind, o):
        z, y, h = self.spot(kind, o)
        rows = self.rows_of(g)
        return getattr(self.r, "core_" + REDUCED[g]).at[pl.ds(pl.multiple_of(((z * 2 + y) * 2 + h) * rows, 16), rows), :]

    def box(self, g, kind, slot):
        return getattr(self.r, "box_" + REDUCED[g]).at[dict(corner=0, x=4, y=8, line=12)[kind] + slot]

    def send(self, g, what, to, slot, recv=None):
        self.sends.append((g, what, to, slot, recv))
        self.copy(g, what, to, slot, recv).start()

    def copy(self, g, what, to, slot, recv):
        source, target = what()
        return push(
            source, target, self.p.to[to], self.r.reduce_send.at[g, slot], self.r.reduce_recv.at[g, slot if recv is None else recv]
        )

    def arrive(self, g, target, slot):
        push(target, target, self.p.to["core"], self.r.reduce_send.at[g, 0], self.r.reduce_recv.at[g, slot]).wait_recv()

    def arrive_core(self, g, target, slot):
        if REDUCED[g] != "w_down":
            self.arrive(g, target, slot)

    def add(self, target, *others):
        total = target[...].astype(F32)
        for other in others:
            total = total + other[...].astype(F32)
        target[...] = total.astype(BF16)

    def give(self, index, tile):
        slot = index % 2

        @pl.when(index >= 2)
        def _():
            self.given(index - 2).wait_send()

        self.r.stage[slot] = tile
        self.given(index).start()
        cols = self.r.own_down.shape[1]
        first = pl.multiple_of(self.p.c * cols, 128)
        self.r.own_down[tile_at(index, UP_TILE), :] = self.r.stage[slot, :, pl.ds(first, cols)]

    def given(self, index):
        cols = self.r.own_down.shape[1]
        first = pl.multiple_of((self.p.other_c) * cols, 128)
        return push(
            self.r.stage.at[index % 2, :, pl.ds(first, cols)], self.r.core_w_down.at[tile_at(index, UP_TILE), :], self.p.to["core"],
            self.r.stage_sems.at[index % 2], self.r.given_recv.at[index],
        )

    def all_given(self):
        tiles = self.r.own_down.shape[0] // UP_TILE
        for index in (tiles - 2, tiles - 1):
            self.given(index).wait_send()
        for index in range(tiles):
            self.given(index).wait_recv()

    def begin(self, g):
        far = (3, 2, 1, 0)
        base = dict(d=0, y=4, x=8, o=12)
        if REDUCED[g] == "w_down":
            self.all_given()
            return
        for kind in "dyxo":
            for o in far:
                self.send(g, functools.partial(self.across, g, kind, o), "core", base[kind] + o)

    def across(self, g, kind, o):
        ref, base, rows, cols = self.home(g)
        z, y, h = self.spot(kind, o)
        first = pl.multiple_of(base + ((z * 2 + y) * 2 + h) * rows, 16)
        other = pl.multiple_of(self.p.other_c * cols, 128)
        return ref.at[pl.ds(first, rows), pl.ds(other, cols)], self.from_core(g, kind, o)

    def boxed(self, g, kind, box, o):
        return self.piece(g, *self.spot(kind, o)), self.box(g, box, o)

    def corner(self, g, o):
        source = self.from_core(g, "d", o)
        self.arrive_core(g, source, o)
        piece = self.piece(g, *self.spot("d", o))
        self.add(piece, source)
        self.send(g, functools.partial(self.boxed, g, "d", "corner", o), "y" if o in self.over_y[g] else "x", 16 + o)

    def side(self, g, kind, o):
        source = self.from_core(g, kind, o)
        self.arrive_core(g, source, dict(y=4, x=8)[kind] + o)
        piece = self.piece(g, *self.spot(kind, o))
        if (o in self.over_y[g]) == (kind == "x"):
            box = self.box(g, "corner", o)
            self.arrive(g, box, 16 + o)
            self.add(piece, source, box)
        else:
            self.add(piece, source)
        self.send(g, functools.partial(self.boxed, g, kind, kind, o), kind, dict(y=20, x=24)[kind] + o)

    def centre(self, g, o):
        source, along_y = self.from_core(g, "o", o), self.box(g, "y", o)
        self.arrive_core(g, source, 12 + o)
        self.arrive(g, along_y, 20 + o)
        if g in self.wide:
            self.add(self.piece(g, *self.spot("o", o)), source, along_y)
            other = [self.from_core(g, "x", o)]
            self.arrive_core(g, other[0], 8 + o)
            if o in self.over_y[g]:
                other.append(self.box(g, "corner", o))
                self.arrive(g, other[1], 16 + o)
            self.add(self.piece(g, *self.spot("x", o)), *other)
            if o:
                self.send(g, functools.partial(self.straight_other, g, o), o, 24 + o, self.p.other_slot)
        else:
            along_x = self.box(g, "x", o)
            self.arrive(g, along_x, 24 + o)
            self.add(self.piece(g, *self.spot("o", o)), source, along_x, along_y)
        if o:
            self.send(g, functools.partial(self.straight, g, o), o, 28 + o, self.p.line_slot)

    def straight_other(self, g, o):
        return self.piece(g, *self.spot("x", o)), self.box(g, "x", self.p.z)

    def cross(self, g):
        self.send(g, functools.partial(self.crossing, g), "x", 39)

    def crossing(self, g):
        p = self.p
        return self.piece(g, p.z, p.y, p.other_x), self.box(g, "x", p.z)

    def straight(self, g, o):
        return self.piece(g, *self.spot("o", o)), self.box(g, "line", self.p.z)

    def collect(self, g, o):
        p = self.p
        z = p.line[o]
        box = self.box(g, "line", z)
        self.arrive(g, box, 32 + z)
        self.add(self.piece(g, p.z, p.y, p.x), box)
        if g in self.wide:
            box = self.box(g, "x", z)
            self.arrive(g, box, 24 + z)
            self.add(self.piece(g, p.z, p.y, p.other_x), box)

    def quarter(self, g, x, c):
        ref = getattr(self.r, REDUCED[g] + "_grad")
        rows, cols = ref.shape[0] // 2, ref.shape[1] // 2
        return ref.at[pl.ds(pl.multiple_of(x * rows, 16), rows), pl.ds(pl.multiple_of(c * cols, 128), cols)]

    def share(self, g):
        p = self.p
        if g in self.wide:
            box = self.box(g, "x", p.z)
            self.arrive(g, box, 39)
            self.add(self.piece(g, p.z, p.y, p.x), box)
        mine = self.quarter(g, p.x, p.c)
        mine[...] = self.piece(g, p.z, p.y, p.x)[...]
        for to, slot in (("x", 36), ("core", 37)):
            self.send(g, lambda: (self.quarter(g, p.x, p.c),) * 2, to, slot)

    def done(self, g):
        p = self.p
        other = self.quarter(g, p.other_x, p.c)
        self.arrive(g, other, 36)
        self.send(g, lambda: (self.quarter(g, p.other_x, p.c),) * 2, "core", 38)

    def finish(self):
        p = self.p
        for g in range(len(REDUCED)):
            self.arrive(g, self.quarter(g, p.x, p.other_c), 37)
            self.arrive(g, self.quarter(g, p.other_x, p.other_c), 38)
        for what in self.sends:
            self.copy(*what).wait_send()


def pack_small(r):
    peers = 2 * LINE
    width = r.tokens.shape[1]
    part = width // peers
    r.owners[...] = jnp.zeros(r.owners.shape, F32)
    for shard in range(peers):
        r.owners[shard, 0:8, 0:part] = r.grad_small[:, shard * part : (shard + 1) * part]
        for i in range(2):
            first = (shard * 2 + i) * part
            r.owners[shard, 8 + i : 9 + i, 0:part] = r.grad_qkv_bias[0:1, first : first + part]
        first = 2 * width + shard * part
        r.owners[shard, 10:11, 0:part] = r.grad_qkv_bias[0:1, first : first + part]
        for i in range(4):
            first = (shard * 4 + i) * part
            r.owners[shard, 11 + i : 12 + i, 0:part] = r.grad_up_bias[0:1, first : first + part]


def owner_copy(r, place, k, receive=False):
    other = (place.fsdp + k) % (2 * LINE)
    slot = other if receive else place.fsdp
    return push(
        r.owners.at[other], r.owned.at[slot], (place.seq, other), r.small_send.at[k], r.owned_recv.at[slot]
    )


def small_reduce_start(r, place):
    pack_small(r)
    lax.fori_loop(1, 2 * LINE, lambda k, carry: (owner_copy(r, place, k).start(), carry)[1], 0)


def small_reduce_middle(r, place):
    def receive(k, total):
        owner_copy(r, place, k, True).wait_recv()
        owner_copy(r, place, k).wait_send()
        return total + r.owned[(place.fsdp + k) % (2 * LINE)]

    r.shared[place.seq] = lax.fori_loop(1, 2 * LINE, receive, r.owners[place.fsdp])
    for k in range(1, 4):
        shared_copy(r, place, k).start()


def shared_copy(r, place, k, receive=False):
    other = (place.seq + k) % 4
    slot = other if receive else place.seq
    return push(
        r.shared.at[place.seq], r.shared.at[slot], (other, place.fsdp), r.shared_send.at[k], r.shared_recv.at[slot]
    )


def small_reduce_finish(r, place):
    for k in range(1, 4):
        shared_copy(r, place, k, True).wait_recv()
        shared_copy(r, place, k).wait_send()
    r.small_total[...] = r.shared[0] + r.shared[1] + r.shared[2] + r.shared[3]


class Home:
    def __init__(self, r, place, both, target, index):
        self.r, self.p, self.both, self.target, self.index = r, place, both, target, index
        rows = both.shape[0] // 2
        self.rows = both.at[pl.ds(pl.multiple_of(place.c * rows, 16), rows), :]

    def across(self, c):
        rows = self.both.shape[0] // 2
        part = self.both.at[pl.ds(pl.multiple_of(c * rows, 16), rows), :]
        return push(part, part, self.p.to["core"], self.r.home_send.at[self.index, 0], self.r.home_recv.at[self.index, 0])

    def along_x(self, x):
        send, recv = self.r.home_send, self.r.home_recv
        return push(
            self.r.leaving, self.target.at[x], self.p.to["x"], send.at[self.index, 1], recv.at[self.index, 1]
        )

    def start(self):
        self.across(self.p.c).start()

    def turn(self):
        self.across(self.p.other_c).wait_recv()
        ordered = dot_nn(self.r.place[...], self.both[...]).astype(BF16)
        half = ordered.shape[0] // 2
        self.r.leaving[...] = ordered[half:]
        self.along_x(self.p.x).start()
        self.target[self.p.x] = ordered[:half]

    def left(self):
        self.along_x(self.p.x).wait_send()

    def finish(self):
        self.along_x(self.p.other_x).wait_recv()
        self.across(self.p.c).wait_send()


def place_back(r, place):
    bundle, length = r.place.shape
    start = r.start[0:1, 0:1]
    quarter = length // 4

    def block(index):
        rows = tile_at(index, 128)
        shape = (128, length)
        mine = lax.broadcasted_iota(jnp.int32, shape, 0) + index * 128
        away = mine >= quarter
        mine = jnp.where(away, mine - quarter + quarter * (2 * (1 - place.x) + place.c), mine + quarter * (2 * place.x + place.c))
        source = mine.astype(F32) - start
        source = jnp.where(source < 0, source + length, source)
        here = lax.broadcasted_iota(jnp.int32, shape, 1).astype(F32)
        r.place[rows, :] = jnp.where(here == source, 1.0, 0.0).astype(BF16)

    loop(bundle // 128, block)


def greet(place):
    barrier = pltpu.get_barrier_semaphore()
    seq, fsdp = place.seq, place.fsdp
    peers = 2 * LINE

    def others(k, carry):
        pl.semaphore_signal(barrier, inc=1, device_id=(seq, (fsdp + k) % peers), device_id_type=MESH)
        return carry

    lax.fori_loop(1, peers, others, 0)
    for k in range(1, 4):
        pl.semaphore_signal(barrier, inc=1, device_id=((seq + k) % 4, fsdp), device_id_type=MESH)


def greeted():
    pl.semaphore_wait(pltpu.get_barrier_semaphore(), 2 * LINE + 2)


VECTORS = ("v0", "v1", "v2", "v3", "v4", "v5", "v6", "v7", "v8", "v9")


def pack_vectors(r):
    part = r.v0.shape[0]
    r.vector_rows[...] = jnp.zeros(r.vector_rows.shape, F32)
    row = 0
    for name in VECTORS:
        values = getattr(r, name)[...].astype(F32)
        for i in range(values.shape[0] // part):
            r.vector_rows[row : row + 1, 0:part] = values[i * part : (i + 1) * part].reshape(1, part)
            row += 1
    r.packed_in[...] = r.vector_rows[...].astype(BF16)


def small_send(r, place, k):
    peers = 2 * LINE
    other = (place.fsdp + k) % peers
    return push(
        r.packed_in, r.packed.at[place.fsdp], (place.seq, other), r.small_send.at[k], r.small_recv.at[place.fsdp]
    )


def small_start(r, place):
    lax.fori_loop(1, 2 * LINE, lambda k, carry: (small_send(r, place, k).start(), carry)[1], 0)
    r.packed[place.fsdp] = r.packed_in[...]


def small_finish(r, place):
    def receive(k, carry):
        other = (place.fsdp + k) % (2 * LINE)
        push(
            r.packed_in, r.packed.at[other], (place.seq, other), r.small_send.at[k], r.small_recv.at[other]
        ).wait_recv()
        small_send(r, place, k).wait_send()
        return carry

    lax.fori_loop(1, 2 * LINE, receive, 0)
    part = r.tokens.shape[1] // (2 * LINE)
    for shard in range(2 * LINE):
        rows = r.packed[shard].astype(F32)
        for i in range(8):
            r.small[i : i + 1, shard * part : (shard + 1) * part] = rows[i : i + 1, 0:part]
        for i in range(3):
            first = (shard * 3 + i) * part
            r.qkv_bias[0:1, first : first + part] = rows[8 + i : 9 + i, 0:part]
        for i in range(4):
            first = (shard * 4 + i) * part
            r.up_bias[0:1, first : first + part] = rows[11 + i : 12 + i, 0:part]


class Exchange:
    def __init__(self, r, place, source, target, index):
        self.p, self.target = place, target
        rows = target.shape[0] // 4
        p = place

        def quarter(x, c):
            return target.at[pl.ds(pl.multiple_of((2 * x + c) * rows, 16), rows), :]

        self.keep = pltpu.make_async_copy(source.at[p.x], quarter(p.x, p.c), r.local_sems.at[len(GATHERED) + index])
        send, recv = r.rows_send, r.rows_recv
        self.along_x = push(source.at[1 - p.x], quarter(p.x, p.c), p.to["x"], send.at[index, 0], recv.at[index, 0])
        self.own = push(source.at[p.x], quarter(p.x, p.c), p.to["core"], send.at[index, 1], recv.at[index, 1])
        passed = quarter(1 - p.x, p.c)
        self.passed = push(passed, passed, p.to["core"], send.at[index, 2], recv.at[index, 2])
        there = quarter(1 - p.x, p.c)
        self.arrive_x = push(there, there, p.to["x"], send.at[index, 0], recv.at[index, 0])
        one, two = quarter(p.x, 1 - p.c), quarter(1 - p.x, 1 - p.c)
        self.arrive = [
            push(one, one, p.to["core"], send.at[index, 1], recv.at[index, 1]),
            push(two, two, p.to["core"], send.at[index, 2], recv.at[index, 2]),
        ]

    def start(self):
        self.keep.start()
        self.along_x.start()
        self.own.start()

    def forward(self):
        self.arrive_x.wait_recv()
        self.passed.start()

    def finish(self):
        self.keep.wait()
        for copy in self.arrive:
            copy.wait_recv()
        for copy in (self.along_x, self.own, self.passed):
            copy.wait_send()


def collect_meta(r, place):
    r.meta_rows[...] = jnp.zeros(r.meta_rows.shape, F32)
    r.meta_rows[0:1, :] = r.segments[pl.ds(place.x, 1), :].astype(F32)
    for axis in range(2):
        r.meta_rows[1 + axis : 2 + axis, :] = r.positions[axis, pl.ds(place.x, 1), :].astype(F32)
    r.meta[...] = r.meta_rows[...].astype(BF16)


WEIGHTS = ("w_qkv", "w_out", "w_up", "w_down")


def spread_head_gains(r):
    columns = jnp.transpose(r.small[...])
    r.head_gain[...] = jnp.zeros(r.head_gain.shape, F32)
    r.head_gain_sums[...] = jnp.zeros(r.head_gain_sums.shape, F32)
    for head in range(2 * H):
        row = head % H * HD
        column = QUERY_GAIN if head < H else KEY_GAIN
        r.head_gain[:, head : head + 1] = columns[row : row + HD, column : column + 1]


TILES = dict(project=6, attend=12, branch=3, up=6, grad_before=6, down=3, grad_hidden_up=3, weight_up=6, out_back=3,
             attend_back=12, grad_hidden_in=3)
ORDER = ("place", "vectors", "rows", "norm", "project", "attend", "attended_rows", "branch", "norm_middle", "cotangent", "up",
         "grad_before", "down", "grad_hidden_up", "weight_up", "norm_middle_back", "out_back", "attend_back", "head_sums",
         "grad_hidden_in", "norm_tokens_back")


def place_rows(r, source, target):
    target[...] = dot_nn(r.place[...], source[...]).astype(BF16)


def computes(r, give):
    part = functools.partial

    def norm():
        rope_tables(r)
        mask_channels(r)
        norm_tokens(r)

    def attend_back_first(index):
        attend_back(r, index)

    table = dict(
        place=part(place_tokens, r), vectors=part(spread_head_gains, r), rows=lambda: place_rows(r, r.seq_tokens, r.tokens),
        norm=norm, attended_rows=part(attended_rows, r), norm_middle=part(norm_middle, r),
        cotangent=lambda: place_rows(r, r.seq_cotangent, r.cotangent), norm_middle_back=part(norm_middle_back, r),
        head_sums=part(head_sums, r), norm_tokens_back=part(norm_tokens_back, r), up=part(up, r, give=give),
    )
    for function in (
        project, attend, branch, grad_before, down, grad_hidden_up, weight_up, out_back, attend_back, grad_hidden_in
    ):
        table[function.__name__] = part(function, r)
    return table


def whole_kernel(names, *refs):
    r = Refs()
    for name, ref in zip(names, refs, strict=True):
        setattr(r, name, ref)
    r.result_rows, r.grad_rows = r.result, r.grad_result
    copies = [
        pltpu.make_async_copy(getattr(r, name + "_in"), getattr(r, name), r.local_sems.at[i]) for i, name in enumerate(WEIGHTS)
    ]
    for copy in copies:
        copy.start()
    r.ones[...] = jnp.ones(r.ones.shape, BF16)

    def out(index):
        return pltpu.make_async_copy(r.stage.at[index % 2], r.w_down_grad.at[tile_at(index, UP_TILE), :], r.stage_sems.at[index % 2])

    def give(index, tile):
        @pl.when(index >= 2)
        def _():
            out(index - 2).wait()

        r.stage[index % 2] = tile
        out(index).start()

    for copy in copies:
        copy.wait()
    table = computes(r, give)
    for name in ORDER:
        if name == "attend_back":
            for index in (0, 1):
                fetch(r, index).start()
        if name in TILES:
            loop(TILES[name], table[name])
        else:
            table[name]()
    for third in range(3):
        weight_in(r, third)
    for index in range(2):
        out(index).wait()
    kept = {"w_out": r.w_out, "w_up": r.w_up}
    kept["thirds"] = r.w_down.at[pl.ds(0, r.thirds_grad.shape[0]), :]
    back = [pltpu.make_async_copy(ref, getattr(r, name + "_grad"), r.local_sems.at[i]) for i, (name, ref) in enumerate(kept.items())]
    for copy in back:
        copy.start()
    for copy in back:
        copy.wait()


SCHEDULE = (
    ("tokens_start",), ("own", 0), ("place",), ("own", 2), ("small_have",), ("y", 0, 0), ("own", 1), ("z", 2, 1), ("z", 0, 2),
    ("vectors",), ("z", 0, 3), ("z", 0, 1), ("d", 1, 0), ("d", 0, 0), ("z", 1, 1), ("tokens_pass",), ("x", 0, 2), ("y", 0, 3),
    ("tokens_have",), ("x", 0, 1), ("z", 1, 3), ("z", 1, 2), ("y", 2, 1), ("x", 0, 3), ("rows",), ("y", 0, 2), ("z", 2, 3),
    ("norm",), ("y", 0, 1), ("d", 0, 2), ("x", 2, 1), ("z", 2, 2), ("d", 0, 3), ("d", 0, 1), ("have", 0), ("project",),
    ("own", 3), ("y", 2, 3), ("project",), ("y", 1, 3), ("own", 4), ("y", 2, 2), ("y", 1, 0), ("d", 1, 2), ("z", 3, 1),
    ("d", 2, 0), ("x", 2, 2), ("y", 1, 2), ("cotangent_start",), ("y", 1, 1), ("d", 1, 1), ("d", 2, 3), ("z", 3, 2),
    ("d", 1, 3), ("x", 2, 3), ("z", 3, 3), ("d", 2, 2), ("d", 2, 1), ("have", 1), ("y", 2, 0), ("project",), ("project",),
    ("have", 2), ("project",), ("project",), ("z", 4, 1), ("attend",), ("attend",), ("attend",), ("x", 3, 1), ("y", 3, 3),
    ("attend",), ("d", 3, 0), ("z", 4, 3), ("attend",), ("attend",), ("y", 4, 0), ("attend",), ("d", 3, 1), ("z", 4, 2),
    ("attend",), ("d", 3, 3), ("attend",), ("attend",), ("x", 4, 1), ("y", 4, 1), ("y", 3, 1), ("y", 3, 2), ("y", 3, 0),
    ("attend",), ("own", 5), ("y", 4, 3), ("x", 3, 3), ("x", 3, 2), ("d", 4, 0), ("attend",), ("y", 4, 2), ("attended_rows",),
    ("d", 3, 2), ("have", 3), ("branch",), ("branch",), ("branch",), ("cotangent_pass",), ("norm_middle",), ("cotangent_have",),
    ("x", 4, 2), ("cotangent",), ("d", 4, 3), ("x", 4, 3), ("z", 5, 1), ("d", 4, 1), ("d", 4, 2), ("have", 4), ("up",),
    ("y", 5, 0), ("z", 5, 2), ("up",), ("z", 5, 3), ("up",), ("d", 5, 0), ("x", 5, 1), ("up",), ("y", 5, 2), ("up",),
    ("y", 5, 3), ("x", 5, 2), ("y", 5, 1), ("up",), ("begin", 5), ("corner", 5, 3), ("d", 5, 1), ("x", 5, 3), ("d", 5, 2),
    ("corner", 5, 0), ("d", 5, 3), ("corner", 5, 1), ("have", 5), ("grad_before",), ("corner", 5, 2), ("grad_before",),
    ("grad_before",), ("grad_before",), ("grad_before",), ("side", 5, "x", 3), ("grad_before",), ("side", 5, "y", 3),
    ("place_back",), ("grad_hidden_up",), ("side", 5, "x", 2), ("grad_hidden_up",), ("side", 5, "y", 2), ("grad_hidden_up",),
    ("sent", 4), ("side", 5, "x", 1), ("weight_up",), ("weight_up",), ("side", 5, "y", 1), ("weight_up",), ("centre", 5, 3),
    ("weight_up",), ("weight_up",), ("side", 5, "x", 0), ("weight_up",), ("begin", 4), ("side", 5, "y", 0), ("centre", 5, 2),
    ("down",), ("centre", 5, 1), ("down",), ("down",), ("norm_middle_back",), ("result_start",), ("side", 4, "x", 2),
    ("sent", 3), ("corner", 4, 0), ("out_back",), ("out_back",), ("fetch",), ("corner", 4, 1), ("corner", 4, 2), ("out_back",),
    ("centre", 5, 0), ("begin", 3), ("sent", 5), ("corner", 4, 3), ("side", 4, "y", 1), ("collect", 5, 1), ("result_turn",),
    ("attend_back",), ("attend_back",), ("attend_back",), ("attend_back",), ("corner", 3, 3), ("weight_in", 0),
    ("collect", 5, 3), ("side", 4, "x", 0), ("collect", 5, 2), ("begin", 0), ("side", 3, "y", 3), ("attend_back",),
    ("corner", 3, 1), ("corner", 3, 2), ("corner", 0, 2), ("attend_back",), ("attend_back",), ("side", 4, "y", 2),
    ("attend_back",), ("corner", 0, 1), ("weight_in", 1), ("corner", 3, 0), ("side", 4, "x", 3), ("side", 4, "y", 3),
    ("side", 0, "y", 2), ("begin", 1), ("attend_back",), ("attend_back",), ("corner", 1, 0), ("share", 5), ("side", 0, "x", 1),
    ("centre", 3, 3), ("side", 1, "y", 0), ("corner", 1, 2), ("side", 4, "x", 1), ("attend_back",), ("side", 3, "y", 0),
    ("attend_back",), ("weight_in", 2), ("begin", 2), ("centre", 4, 2), ("head_sums",), ("side", 0, "x", 3), ("corner", 1, 3),
    ("corner", 0, 0), ("side", 3, "y", 2), ("side", 1, "x", 3), ("grad_hidden_in",), ("grad_hidden_in",), ("grad_hidden_in",),
    ("norm_tokens_back",), ("grads_start",), ("side", 0, "y", 0), ("corner", 0, 3), ("corner", 2, 2), ("side", 0, "x", 2),
    ("centre", 4, 3), ("side", 0, "x", 0), ("side", 1, "x", 1), ("side", 4, "y", 0), ("small_start",), ("side", 0, "y", 1),
    ("side", 1, "x", 2), ("grads_turn",), ("centre", 4, 1), ("side", 2, "y", 1), ("side", 0, "y", 3), ("centre", 3, 2),
    ("centre", 3, 0), ("centre", 0, 1), ("small_middle",), ("side", 3, "y", 1), ("side", 1, "y", 3), ("side", 2, "y", 3),
    ("corner", 2, 3), ("collect", 4, 3), ("side", 1, "y", 2), ("corner", 2, 1), ("centre", 0, 2), ("centre", 0, 0),
    ("small_finish",), ("centre", 0, 3), ("corner", 1, 1), ("result_have",), ("collect", 3, 3), ("side", 2, "y", 0),
    ("done", 5), ("side", 2, "y", 2), ("side", 2, "x", 2), ("centre", 3, 1), ("corner", 2, 0), ("side", 2, "x", 3),
    ("grads_have",), ("grads_left",), ("collect", 0, 1), ("sent", 0), ("sent", 1), ("centre", 1, 3), ("sent", 2),
    ("centre", 1, 2), ("collect", 0, 2), ("side", 1, "y", 1), ("collect", 4, 1), ("collect", 0, 3), ("side", 1, "x", 0),
    ("side", 2, "x", 1), ("centre", 2, 3), ("collect", 4, 2), ("share", 0), ("centre", 4, 0), ("side", 2, "x", 0),
    ("centre", 2, 2), ("centre", 1, 1), ("collect", 3, 2), ("collect", 3, 1), ("collect", 1, 2), ("centre", 1, 0),
    ("centre", 2, 1), ("cross", 3), ("share", 4), ("collect", 1, 3), ("centre", 2, 0), ("collect", 1, 1), ("share", 1),
    ("collect", 2, 3), ("collect", 2, 1), ("collect", 2, 2), ("done", 0), ("share", 2), ("share", 3), ("done", 1), ("done", 2),
    ("done", 4), ("done", 3), ("finish",),
)
GATHER_OVER_Y = ((0, 1, 2), (0, 1, 2), (0,), (0, 1), (0, 1), (0, 1))
REDUCE_OVER_Y = ((0, 2), (0, 2), (0, 1, 2, 3), (0, 1, 2, 3), (0, 1, 3), (0, 1))
GATHER_WIDE = (1,)
REDUCE_WIDE = (3,)


def fused_kernel(names, *refs):
    r = Refs()
    for name, ref in zip(names, refs, strict=True):
        setattr(r, name, ref)
    place = Place()
    gather = Gather(r, place, dict(enumerate(GATHER_OVER_Y)), GATHER_WIDE)
    reduce = Reduce(r, place, dict(enumerate(REDUCE_OVER_Y)), REDUCE_WIDE)
    for g in range(len(GATHERED)):
        gather.load(g).start()
    tokens = Exchange(r, place, r.tokens_in, r.seq_tokens, 0)
    cotangent = Exchange(r, place, r.cotangent_in, r.seq_cotangent, 1)
    result = Home(r, place, r.seq_tokens, r.result, 0)
    grads = Home(r, place, r.seq_cotangent, r.grad_result, 1)
    r.result_rows, r.grad_rows = result.rows, grads.rows
    greet(place)
    pack_vectors(r)
    r.ones[...] = jnp.ones(r.ones.shape, BF16)
    collect_meta(r, place)
    greeted()
    small_start(r, place)

    def fetch_first():
        for index in (0, 1):
            fetch(r, index).start()

    def grads_turn():
        result.left()
        grads.turn()

    plain = dict(
        own=gather.own, z=gather.from_line, x=gather.from_x, y=gather.from_y, d=gather.from_corner, have=gather.have, sent=gather.sent,
        tokens_start=tokens.start, tokens_pass=tokens.forward, tokens_have=tokens.finish,
        cotangent_start=cotangent.start, cotangent_pass=cotangent.forward, cotangent_have=cotangent.finish,
        small_have=functools.partial(small_finish, r, place), fetch=fetch_first, weight_in=functools.partial(weight_in, r),
        begin=reduce.begin, corner=reduce.corner, side=reduce.side, centre=reduce.centre, collect=reduce.collect, share=reduce.share, cross=reduce.cross,
        done=reduce.done, finish=reduce.finish,
        place_back=functools.partial(place_back, r, place), result_start=result.start, result_turn=result.turn,
        result_have=result.finish, grads_start=grads.start, grads_turn=grads_turn, grads_have=grads.finish, grads_left=grads.left,
        small_start=functools.partial(small_reduce_start, r, place), small_middle=functools.partial(small_reduce_middle, r, place),
        small_finish=functools.partial(small_reduce_finish, r, place),
    )
    table = computes(r, reduce.give)
    items = list(SCHEDULE)
    while items:
        name, *args = items.pop(0)
        if name in plain:
            plain[name](*args)
        elif name not in TILES:
            table[name]()
        else:
            between = {}
            tile = 0
            while tile < TILES[name] - 1:
                item = items.pop(0)
                if item[0] == name:
                    tile += 1
                else:
                    between.setdefault(tile, []).append(item)
            tiled_loop(TILES[name], table[name], between, plain)


def tiled_loop(count, body, between, plain):
    def step(index):
        body(index)
        for tile, todo in between.items():

            @pl.when(index == tile)
            def _():
                for name, *args in todo:
                    plain[name](*args)

    loop(count, step)


def layer(fused, tokens, cotangent, segments, positions, small, qkv_bias, up_bias, *weights):
    peers = 2 * LINE
    scale = peers if fused else 1
    width = tokens.shape[-1]
    length = segments.shape[1]
    bundle = length // 2
    hidden = weights[2].shape[1]
    shape = jax.ShapeDtypeStruct
    vmem = pl.BlockSpec(memory_space=pltpu.VMEM)
    hbm = pl.BlockSpec(memory_space=pl.ANY)
    inputs = {}
    if fused:
        inputs.update(
            tokens_in=(tokens, hbm),
            cotangent_in=(cotangent, hbm),
            segments=(segments, vmem),
            positions=(positions, vmem),
            **{name: (v, vmem) for name, v in zip(VECTORS, small)},
        )
    else:
        inputs.update(
            seq_tokens=(tokens, vmem),
            seq_cotangent=(cotangent, vmem),
            meta=(segments, vmem),
            small=(small, vmem),
            qkv_bias=(qkv_bias, vmem),
            up_bias=(up_bias, vmem),
        )
    full = [(w.shape[0] * scale, w.shape[1]) for w in weights]
    for name, w in zip(WEIGHTS, weights):
        inputs[name + "_in"] = (w, hbm)
    outputs = dict(
        result=(shape(tokens.shape if fused else (bundle, width), BF16), vmem),
        grad_result=(shape(tokens.shape if fused else (bundle, width), BF16), vmem),
        chances_kept=(shape((H, bundle, bundle), BF16), hbm),
    )
    scratch = {}
    vectors = dict(grad_small=(8, width), grad_qkv_bias=(8, 3 * width), grad_up_bias=(8, hidden))
    if fused:
        outputs["small_total"] = (shape((16, 128), F32), vmem)
        scratch.update({name: pltpu.VMEM(size, F32) for name, size in vectors.items()})
    else:
        outputs.update({name: (shape(size, F32), vmem) for name, size in vectors.items()})
    reduced = {name: (width, width) for name in REDUCED[:3]}
    reduced.update(zip(WEIGHTS[1:], full[1:]))
    if fused:
        for name, size in reduced.items():
            outputs[name + "_grad"] = (shape((size[0] // peers, size[1]), BF16), vmem)
    else:
        outputs["thirds_grad"] = (shape((3 * width, width), BF16), hbm)
        for name in WEIGHTS[1:]:
            outputs[name + "_grad"] = (shape(reduced[name], BF16), hbm)
    for name, size in zip(WEIGHTS, full):
        scratch[name] = pltpu.VMEM(size, BF16)
    if fused:
        groups, pieces = len(GATHERED), 2 * peers
        scratch.update(
            seq_tokens=pltpu.VMEM((length, width), BF16),
            seq_cotangent=pltpu.VMEM((length, width), BF16),
            meta_rows=pltpu.VMEM((8, length), F32),
            meta=pltpu.VMEM((8, length), BF16),
            vector_rows=pltpu.VMEM((16, 128), F32),
            packed_in=pltpu.VMEM((16, 128), BF16),
            packed=pltpu.VMEM((peers, 16, 128), BF16),
            small=pltpu.VMEM((8, width), F32),
            qkv_bias=pltpu.VMEM((1, 3 * width), F32),
            up_bias=pltpu.VMEM((1, hidden), F32),
            small_send=pltpu.SemaphoreType.DMA((peers,)),
            small_recv=pltpu.SemaphoreType.DMA((peers,)),
            rows_send=pltpu.SemaphoreType.DMA((2, 3)),
            rows_recv=pltpu.SemaphoreType.DMA((2, 3)),
            gather_send=pltpu.SemaphoreType.DMA((groups, 36)),
            gather_recv=pltpu.SemaphoreType.DMA((groups, pieces)),
            gather_core=pltpu.SemaphoreType.DMA((groups, pieces)),
            own_down=pltpu.VMEM((hidden, width // 2), BF16),
            given_recv=pltpu.SemaphoreType.DMA((hidden // UP_TILE,)),
            reduce_send=pltpu.SemaphoreType.DMA((groups, 40)),
            reduce_recv=pltpu.SemaphoreType.DMA((groups, 40)),
            home_send=pltpu.SemaphoreType.DMA((2, 2)),
            home_recv=pltpu.SemaphoreType.DMA((2, 2)),
            leaving=pltpu.VMEM((length // 4, width), BF16),
            owners=pltpu.VMEM((peers, 16, 128), F32),
            owned=pltpu.VMEM((peers, 16, 128), F32),
            owned_recv=pltpu.SemaphoreType.DMA((peers,)),
            shared=pltpu.VMEM((4, 16, 128), F32),
            shared_send=pltpu.SemaphoreType.DMA((4,)),
            shared_recv=pltpu.SemaphoreType.DMA((4,)),
        )
        for name, size in reduced.items():
            scratch["core_" + name] = pltpu.VMEM((size[0], size[1] // 2), BF16)
            scratch["box_" + name] = pltpu.VMEM((16, size[0] // (2 * peers), size[1] // 2), BF16)
    scratch.update(
        local_sems=pltpu.SemaphoreType.DMA((10,)),
        ones=pltpu.VMEM((8, bundle), BF16),
        start=pltpu.VMEM((8, 128), F32),
        place=pltpu.VMEM((bundle, length), BF16),
        marks_row=pltpu.VMEM((8, bundle), F32),
        mask_keys=pltpu.VMEM((16, bundle), BF16),
        mask_queries=pltpu.VMEM((16, bundle), BF16),
        shares=pltpu.VMEM((H, 1, bundle), F32),
        cosine=pltpu.VMEM((2, HD // 4, bundle), F32),
        sine=pltpu.VMEM((2, HD // 4, bundle), F32),
        head_gain=pltpu.VMEM((HD, 128), F32),
        head_gain_sums=pltpu.VMEM((HD, 128), F32),
        tokens=pltpu.VMEM((bundle, width), BF16),
        cotangent=pltpu.VMEM((bundle, width), BF16),
        hidden_pre_t=pltpu.VMEM((width, bundle), BF16),
        projected_t=pltpu.VMEM((3 * width, bundle), BF16),
        turned_t=pltpu.VMEM((2 * width, bundle), BF16),
        chances=pltpu.VMEM((2, bundle, bundle), BF16),
        chance_sems=pltpu.SemaphoreType.DMA((2,)),
        attended_t=pltpu.VMEM((width, bundle), BF16),
        middle=pltpu.VMEM((bundle, width), F32),
        hidden_mlp_t=pltpu.VMEM((width, bundle), BF16),
        active=pltpu.VMEM((bundle, hidden), BF16),
        stage=pltpu.VMEM((2, UP_TILE, width), BF16),
        stage_sems=pltpu.SemaphoreType.DMA((2,)),
        slope=pltpu.VMEM((bundle, hidden), BF16),
        grad_hidden=pltpu.VMEM((bundle, width), F32),
        rows=pltpu.VMEM((bundle, width), BF16),
        grad_attended_t=pltpu.VMEM((width, bundle), BF16),
    )
    names = tuple(inputs) + tuple(outputs) + tuple(scratch)
    params = dict(vmem_limit_bytes=63 << 20)
    if fused:
        params.update(collective_id=0, has_side_effects=True)
    return pl.pallas_call(
        functools.partial(fused_kernel if fused else whole_kernel, names),
        out_shape=tuple(o[0] for o in outputs.values()),
        in_specs=[i[1] for i in inputs.values()],
        out_specs=tuple(o[1] for o in outputs.values()),
        scratch_shapes=list(scratch.values()),
        compiler_params=pltpu.CompilerParams(**params),
        name="layer",
    )(*(i[0] for i in inputs.values()))


def finish_kernel(part, result, grad_result, small, third0, third1, third2, *refs):
    weights, outs = refs[:3], refs[3:]
    outs[0][...] = result[...]
    outs[1][...] = grad_result[...]
    for third, source in enumerate((third0, third1, third2)):
        lanes = source.shape[1] // 6
        for half in range(2):
            for block in range(3):
                first = block * 6 * lanes + (2 * third + half) * lanes
                given = (half * 3 + block) * lanes
                outs[2][:, first : first + lanes] = source[:, given : given + lanes].astype(F32)
    for source, target in zip(weights, outs[3:6]):
        target[...] = source[...].astype(F32)
    for target, first, count in zip(outs[6:], (0, 1, 2, 3, 4, 5, 6, 7, 8, 10, 11), (1,) * 8 + (2, 1, 4)):
        for i in range(count):
            target[i * part : (i + 1) * part] = small[first + i : first + i + 1, 0:part].reshape(part)


def finish(part, result, grad_result, small, *weights):
    shape = jax.ShapeDtypeStruct
    vmem = pl.BlockSpec(memory_space=pltpu.VMEM)
    rows, width = weights[0].shape
    outs = [shape(result.shape, BF16), shape(grad_result.shape, BF16), shape((rows, 3 * width), F32)]
    outs += [shape(w.shape, F32) for w in weights[3:]]
    outs += [shape((part * count,), F32) for count in (1,) * 8 + (2, 1, 4)]
    return pl.pallas_call(
        functools.partial(finish_kernel, part),
        out_shape=tuple(outs),
        in_specs=[vmem] * (3 + len(weights)),
        out_specs=tuple([vmem] * len(outs)),
        compiler_params=pltpu.CompilerParams(vmem_limit_bytes=63 << 20),
        name="finish",
    )(result, grad_result, small, *weights)


def shards(
    tokens,
    pre_gain,
    pre_bias,
    query_key_value_weight,
    query_key_value_bias,
    query_gain,
    key_gain,
    output_weight,
    output_bias,
    mlp_gain,
    mlp_bias,
    up_matrix_weight,
    up_offset_bias,
    down_matrix_weight,
    down_offset_bias,
    segments,
    positions,
    cotangent,
):
    rank = lax.axis_index("seq")
    x = rank // 2
    width = tokens.shape[2]
    length = segments.shape[1]
    fsdp = lax.axis_size("fsdp")
    part = width // fsdp
    weights_in = (query_key_value_weight, output_weight, up_matrix_weight, down_matrix_weight)
    vectors = (
        pre_gain, pre_bias, query_gain, key_gain, output_bias, mlp_gain, mlp_bias, down_offset_bias,
        query_key_value_bias, up_offset_bias,
    )
    if fsdp == 2 * LINE:
        result, grad_result, _, small_total, *weight_grads = layer(
            True, tokens, cotangent, segments, positions, vectors, None, None, *weights_in
        )
        result, grad_result, g0, g1, g2, g3, *v = finish(part, result, grad_result, small_total, *weight_grads)
        return (
            result, grad_result, v[PRE_GAIN], v[PRE_BIAS], g0, v[8], v[9], v[QUERY_GAIN], v[KEY_GAIN], g1, v[OUT_BIAS],
            v[MLP_GAIN], v[MLP_BIAS], g2, v[10], g3, v[DOWN_BIAS],
        )
    else:
        gather = functools.partial(lax.all_gather, axis_name="fsdp", axis=0, tiled=True)
        packed = gather(jnp.concatenate(vectors)[None]).astype(F32)
        small = jnp.stack([packed[:, i * part : (i + 1) * part].reshape(width) for i in range(8)])
        qkv_bias = packed[:, 8 * part : 11 * part].reshape(1, 3 * width)
        up_bias = packed[:, 11 * part :].reshape(1, -1)
        seq_tokens = lax.dynamic_index_in_dim(lax.all_gather(tokens, "seq", axis=1, tiled=True), x, 0, False)
        seq_cotangent = lax.dynamic_index_in_dim(lax.all_gather(cotangent, "seq", axis=1, tiled=True), x, 0, False)
        labels = lax.dynamic_index_in_dim(segments, x, 0, True)
        places = lax.dynamic_index_in_dim(positions, x, 1, False)
        meta = jnp.concatenate([labels, places, jnp.zeros((5, length), jnp.int32)], axis=0).astype(BF16)
        results = layer(False, seq_tokens, seq_cotangent, meta, None, small, qkv_bias, up_bias, *map(gather, weights_in))
    result, grad_result, _, grad_small, grad_qkv_bias, grad_up_bias, thirds, *weight_grads = results
    blocks = thirds.reshape(3, width, 2, 3, width // 6)
    weight_grads = [blocks.transpose(1, 3, 0, 2, 4).reshape(width, 3 * width), *weight_grads]
    counts = jnp.stack([jnp.sum(segments == v, axis=1) for v in range(4)])
    first = jnp.argmax(counts == length // 2, axis=0)
    starts = jnp.sum(segments < first[:, None], axis=1)

    def home(bundle):
        every = lax.all_gather(bundle, "seq").reshape(2, length, width)
        own = rank * (length // 4) + jnp.arange(length // 4)
        index = (own[None] - starts[:, None]) % length
        return jnp.take_along_axis(every, index[..., None], axis=1)

    scatter = functools.partial(lax.psum_scatter, axis_name="fsdp", scatter_dimension=0, tiled=True)

    def total_of(grad):
        return lax.psum(scatter(grad).astype(BF16), "seq").astype(F32)

    weights = [total_of(g) for g in weight_grads]
    pieces = [grad_small[i].reshape(fsdp, part) for i in range(8)]
    pieces += [grad_qkv_bias[0, : 2 * width].reshape(fsdp, -1), grad_qkv_bias[0, 2 * width :].reshape(fsdp, -1)]
    pieces += [grad_up_bias[0].reshape(fsdp, -1)]
    total = lax.psum(scatter(jnp.concatenate(pieces, axis=1)), "seq")[0]
    s = [total[i * part : (i + 1) * part] for i in range(8)]
    query_key_bias, value_bias, up_total = total[8 * part : 10 * part], total[10 * part : 11 * part], total[11 * part :]
    return (
        home(result), home(grad_result), s[PRE_GAIN], s[PRE_BIAS], weights[0], query_key_bias, value_bias,
        s[QUERY_GAIN], s[KEY_GAIN], weights[1], s[OUT_BIAS], s[MLP_GAIN], s[MLP_BIAS], weights[2], up_total,
        weights[3], s[DOWN_BIAS],
    )


def solution(mesh):
    rows, matrix, activations = P("fsdp"), P("fsdp", None), P("fsdp", "seq", None)
    placed = (
        activations, rows, rows, matrix, rows, rows, rows, matrix, rows, rows, rows, matrix, rows, matrix, rows,
        P("fsdp", None), P(None, "fsdp", None), activations,
    )
    given = (
        activations, activations, rows, rows, matrix, rows, rows, rows, rows, matrix, rows, rows, rows, matrix, rows,
        matrix, rows,
    )
    return jax.shard_map(shards, mesh=mesh, in_specs=placed, out_specs=given, check_vma=False)
```
